128 devices in a mesh: dp: 64 (over z, y, x), tensor: 2 (over core).
Axes of the slice: x: 4, y: 4, z: 4, core: 2. Of those that a mesh axis runs over, the one named last changes fastest.
Arguments:
- square_grad: float32 [32, 2359296], P(None, ('dp', 'tensor')), may hold values from -80 to 80
- square_state: float32 [32, 2359296], P(None, ('dp', 'tensor')), may hold values from -6 to 6
- swiglu_grad: float32 [24, 6291456], P(None, ('dp', 'tensor')), may hold values from -80 to 80
- swiglu_state: float32 [24, 6291456], P(None, ('dp', 'tensor')), may hold values from -6 to 6
- square_order: int32 [32], replicated, may hold values from 0 to 31, each once
- swiglu_order: int32 [24], replicated, may hold values from 0 to 23, each once
- owners: int32 [56], replicated, may hold values from 0 to 63, as said below
- vector_values: float32 [172032], P(('dp', 'tensor')), may hold values from -6 to 6
- vector_grad: float32 [172032], P(('dp', 'tensor')), may hold values from -6 to 6
- vector_first: float32 [172032], P(('dp', 'tensor')), may hold values from -4 to 4
- vector_second: float32 [172032], P(('dp', 'tensor')), may hold values from 0.01 to 1
- embed_values: float32 [8192, 1536], P('dp', 'tensor'), may hold values from -6 to 6
- embed_grad: float32 [8192, 1536], P('dp', 'tensor'), may hold values from -6 to 6
- embed_first: float32 [8192, 1536], P('dp', 'tensor'), may hold values from -4 to 4
- embed_second: float32 [8192, 1536], P('dp', 'tensor'), may hold values from 0.01 to 1
- embed_ranges: int32 [16, 2], replicated, may hold values from 0 to 8192, as said below
Outputs:
- square_next: float32 [32, 2359296], P(None, ('dp', 'tensor'))
- swiglu_next: float32 [24, 6291456], P(None, ('dp', 'tensor'))
- square_update: bfloat16 [32, 1536, 1536], P(None, 'dp', 'tensor')
- swiglu_update: bfloat16 [24, 1536, 4096], P(None, 'dp', 'tensor')
- owner_norms: float32 [64], P('dp')
- vector_step: float32 [172032], P(('dp', 'tensor'))
- first_vector: float32 [172032], P(('dp', 'tensor'))
- second_vector: float32 [172032], P(('dp', 'tensor'))
- embed_step: float32 [8192, 1536], P('dp', 'tensor')
- first_embed: float32 [8192, 1536], P('dp', 'tensor')
- second_embed: float32 [8192, 1536], P('dp', 'tensor')
The draws below stay inside these ranges and needn't reach their ends.
Inputs may be any that keep to these rules, and one draw needn't show every extreme that they name: Different matrices have different owners. `square_order`: each matrix once. `swiglu_order`: each matrix once. `embed_ranges`: start < end in every row.
All inputs are finite; a program needn't handle non-finite values.
Results may differ from the reference program's by a relative error of at most 0.0065.
Values may be sent and summed in bfloat16 or wider, within the bound.
A program may use at most 128 MiB of HBM per device.

```python
import math
import jax
import jax.numpy as jnp
from jax import lax

D = 1536
FF = 4096
NS_STEPS = 2
NRANGE = 16
SQ = 32
ML = 24
MATS = 56
OWNERS = 64
EMB_ROWS = 8192
VEC = 172032


def matrix_grads(key, count, rows, width):
    keys = jax.random.split(key, 3)
    row_scale = jnp.exp(jax.random.uniform(keys[0], (count, rows, 1), jnp.float32, 0.0, math.log(10.0)))
    row_scale = row_scale * jnp.exp(math.log(3.0) * jnp.arange(rows, dtype=jnp.float32) / rows)[None, :, None]
    col_scale = jnp.exp(jax.random.uniform(keys[1], (count, 1, width), jnp.float32, 0.0, math.log(10.0)))
    base = jnp.clip(jax.random.normal(keys[2], (count, rows, width), jnp.float32), -5.0, 5.0)
    values = base * row_scale * col_scale / 30.0
    return values.reshape(count, rows * width)


def draw_square_grad(key, part):
    return matrix_grads(jax.random.fold_in(key, 11), SQ, D, D)


def draw_swiglu_grad(key, part):
    return matrix_grads(jax.random.fold_in(key, 23), ML, D, FF)


def draw_owners(key, part):
    keys = jax.random.split(jax.random.fold_in(key, 37), 2)
    middle = jax.random.permutation(keys[0], jnp.arange(1, OWNERS - 1, dtype=jnp.int32))
    listed = jnp.concatenate([jnp.array([0, OWNERS - 1], jnp.int32), middle])[:MATS]
    return jax.random.permutation(keys[1], listed).astype(jnp.int32)


def draw_embed_ranges(key, part):
    keys = jax.random.split(jax.random.fold_in(key, 53), 2)
    lengths = jax.random.randint(keys[0], (NRANGE,), 1, EMB_ROWS // 8 + 1)
    starts = jax.random.randint(keys[1], (NRANGE,), 0, EMB_ROWS - lengths + 1)
    starts = starts.at[0].set(0)
    starts = starts.at[1].set(EMB_ROWS - lengths[1])
    return jnp.stack([starts, starts + lengths], axis=1).astype(jnp.int32)


def level_of(own_key, dims, cuts, smallest, top_value):
    loudness = 1.0
    for axis_at, parts in cuts:
        steps = jax.random.uniform(jax.random.fold_in(jax.random.fold_in(own_key, 6), axis_at), (parts,), jnp.float32, smallest / len(cuts), top_value / len(cuts))
        loudness = loudness * jnp.repeat(jnp.exp(steps), dims[axis_at] // parts).reshape((-1,) + (1,) * (len(dims) - 1 - axis_at))
    return loudness


def noise(stream_key, extent, deviation, reach, cuts=(), kind=jnp.bfloat16):
    result = jax.random.normal(stream_key, extent, jnp.float32) * deviation
    if len(cuts) > 0:
        result = level_of(stream_key, extent, cuts, -0.22, 0.18) * result
    return jnp.clip(result, min=-reach, max=reach).astype(kind)


def setup_inputs(seed: int = 0) -> dict:
    seeds = jax.random.split(jax.random.key(seed), 17)
    square_grad = draw_square_grad(jax.random.fold_in(seeds[16], 71), 0)
    square_state = noise(seeds[1], (SQ, D * D), 1.0, 6.0, ((1, 128),), jnp.float32)
    swiglu_grad = draw_swiglu_grad(jax.random.fold_in(seeds[16], 71), 0)
    swiglu_state = noise(seeds[3], (ML, D * FF), 1.0, 6.0, ((1, 128),), jnp.float32)
    square_order = jax.random.permutation(seeds[4], SQ).astype(jnp.int32)
    swiglu_order = jax.random.permutation(seeds[5], ML).astype(jnp.int32)
    owners = draw_owners(jax.random.fold_in(seeds[16], 71), 0)
    vector_values = noise(seeds[7], (VEC,), 1.0, 6.0, ((0, 128),), jnp.float32)
    vector_grad = noise(seeds[8], (VEC,), 1.0, 6.0, ((0, 128),), jnp.float32)
    vector_first = noise(seeds[9], (VEC,), 0.3, 4.0, ((0, 128),), jnp.float32)
    vector_second = jnp.clip(jnp.exp(math.log(1.0) - 4.6051702 * jax.random.uniform(seeds[10], (VEC,), jnp.float32) ** level_of(seeds[10], (VEC,), ((0, 128),), -0.2, 0.2)), 0.01, 1.0)
    embed_values = noise(seeds[11], (EMB_ROWS, D), 1.0, 6.0, ((0, 64), (1, 2)), jnp.float32)
    embed_grad = noise(seeds[12], (EMB_ROWS, D), 1.0, 6.0, ((0, 64), (1, 2)), jnp.float32)
    embed_first = noise(seeds[13], (EMB_ROWS, D), 0.3, 4.0, ((0, 64), (1, 2)), jnp.float32)
    embed_second = jnp.clip(jnp.exp(math.log(1.0) - 4.6051702 * jax.random.uniform(seeds[14], (EMB_ROWS, D), jnp.float32) ** level_of(seeds[14], (EMB_ROWS, D), ((0, 64), (1, 2)), -0.2, 0.2)), 0.01, 1.0)
    embed_ranges = draw_embed_ranges(jax.random.fold_in(seeds[16], 71), 0)
    return {"square_grad": square_grad, "square_state": square_state, "swiglu_grad": swiglu_grad, "swiglu_state": swiglu_state, "square_order": square_order, "swiglu_order": swiglu_order, "owners": owners, "vector_values": vector_values, "vector_grad": vector_grad, "vector_first": vector_first, "vector_second": vector_second, "embed_values": embed_values, "embed_grad": embed_grad, "embed_first": embed_first, "embed_second": embed_second, "embed_ranges": embed_ranges}


QUINTIC_LINEAR = 3.4445
QUINTIC_CUBIC = -4.775
QUINTIC_FIFTH = 2.0315
MOMENTUM = 0.95
BIAS_FIRST = 1.0 - 0.9 ** 10
BIAS_SECOND = 1.0 - 0.95 ** 10

def orthogonalize(slot_matrix, factor):
    iterate = slot_matrix
    first_scale = jnp.float32(1.0)
    for round_index in range(NS_STEPS):
        gram = jnp.dot(iterate, iterate.T, preferred_element_type=jnp.float32)
        if round_index == 0:
            gram_scale = jnp.sqrt(jnp.sum(gram * gram)) + 1e-06
            first_scale = gram_scale
        else:
            gram_scale = jnp.float32(1.0)
        normed = (gram / gram_scale).astype(jnp.bfloat16)
        squared = jnp.dot(normed, normed, preferred_element_type=jnp.float32)
        polynomial = (QUINTIC_CUBIC * normed.astype(jnp.float32) + QUINTIC_FIFTH * squared).astype(jnp.bfloat16)
        product = jnp.dot(polynomial, iterate, preferred_element_type=jnp.float32)
        mixed = (QUINTIC_LINEAR * iterate.astype(jnp.float32) + product) / jnp.sqrt(gram_scale)
        if round_index == NS_STEPS - 1:
            iterate = (factor * mixed).astype(jnp.bfloat16)
        else:
            iterate = mixed.astype(jnp.bfloat16)
    return (iterate, first_scale)

def square_run(matrix):
    return orthogonalize(matrix, math.sqrt(D))

def swiglu_run(matrix):
    return orthogonalize(matrix, math.sqrt(FF))

def momentum_terms(gradient, state):
    state_next = MOMENTUM * state + gradient
    return (state_next, (gradient + MOMENTUM * state_next).astype(jnp.bfloat16))

def canonical(slots, order, count):
    inverse = jnp.zeros((count,), jnp.int32).at[order].set(jnp.arange(count, dtype=jnp.int32))
    return slots[inverse]

def adamw_terms(values, gradient, first, second):
    first_next = 0.9 * first + 0.1 * gradient
    second_next = 0.95 * second + 0.05 * gradient * gradient
    direction = first_next / BIAS_FIRST / (jnp.sqrt(second_next / BIAS_SECOND) + 1e-08) + 0.1 * values
    return (direction, first_next, second_next)

def reference(square_grad, square_state, swiglu_grad, swiglu_state, square_order, swiglu_order, owners, vector_values, vector_grad, vector_first, vector_second, embed_values, embed_grad, embed_first, embed_second, embed_ranges):
    square_next, square_send = momentum_terms(square_grad, square_state)
    swiglu_next, swiglu_send = momentum_terms(swiglu_grad, swiglu_state)
    square_mats = canonical(square_send, square_order, SQ).reshape(SQ, D, D)
    swiglu_mats = canonical(swiglu_send, swiglu_order, ML).reshape(ML, D, FF)
    square_update, square_scale = lax.map(square_run, square_mats)
    swiglu_update, swiglu_scale = lax.map(swiglu_run, swiglu_mats)
    all_scales = jnp.concatenate([square_scale, swiglu_scale])
    owner_norms = jnp.zeros((OWNERS,), jnp.float32).at[owners].set(0.5 * jnp.log(all_scales))
    vector_step, first_vector, second_vector = adamw_terms(vector_values, vector_grad, vector_first, vector_second)
    row_numbers = jnp.arange(EMB_ROWS, dtype=jnp.int32)[:, None]
    inside = (row_numbers >= embed_ranges[None, :, 0]) & (row_numbers < embed_ranges[None, :, 1])
    row_live = lax.optimization_barrier(jnp.sum(inside.astype(jnp.int32), axis=1)) > 0
    direction, first_next, second_next = adamw_terms(embed_values, embed_grad, embed_first, embed_second)
    embed_step = jnp.where(row_live[:, None], direction, 0.0)
    first_embed = jnp.where(row_live[:, None], first_next, embed_first)
    second_embed = jnp.where(row_live[:, None], second_next, embed_second)
    return (square_next, swiglu_next, square_update, swiglu_update, owner_norms, vector_step, first_vector, second_vector, embed_step, first_embed, second_embed)
```

```python
import math

import jax
import jax.numpy as jnp
from jax import lax
from jax.experimental import pallas as pl
from jax.experimental.pallas import tpu as pltpu
from jax.sharding import PartitionSpec as P

D = 1536
FF = 4096
NS_STEPS = 2
MESH = pl.DeviceIdType.MESH

QUINTIC_LINEAR = 3.4445
QUINTIC_CUBIC = -4.775
QUINTIC_FIFTH = 2.0315
MOMENTUM = 0.95
BIAS_FIRST = 1.0 - 0.9**10
BIAS_SECOND = 1.0 - 0.95**10


def momentum_terms(gradient, state):
    state_next = MOMENTUM * state + gradient
    return (state_next, (gradient + MOMENTUM * state_next).astype(jnp.bfloat16))


def adamw_terms(values, gradient, first, second):
    first_next = 0.9 * first + 0.1 * gradient
    second_next = 0.95 * second + 0.05 * gradient * gradient
    direction = (
        first_next / BIAS_FIRST / (jnp.sqrt(second_next / BIAS_SECOND) + 1e-08) + 0.1 * values
    )
    return (direction, first_next, second_next)


def inverse_of(order):
    count = order.shape[0]
    return jnp.zeros((count,), jnp.int32).at[order].set(jnp.arange(count, dtype=jnp.int32))


def device_barrier(n_dev, me):
    barrier = pltpu.get_barrier_semaphore()

    def signal(k, carry):
        target = lax.rem(me + k, n_dev)
        pl.semaphore_signal(
            barrier, inc=1, device_id=(target // 2, lax.rem(target, 2)), device_id_type=MESH
        )
        return carry

    lax.fori_loop(1, n_dev, signal, 0)
    pl.semaphore_wait(barrier, n_dev - 1)


def scatter_kernel(n_sq, n_sw, sq_ref, sw_ref, out_ref, send_sem, recv_sem):
    d = lax.axis_index("dp")
    t = lax.axis_index("tensor")
    n_dev = lax.axis_size("dp") * 2
    me = d * 2 + t
    device_barrier(n_dev, me)

    def sq_copy(j):
        return pltpu.make_async_remote_copy(
            src_ref=sq_ref.at[j],
            dst_ref=out_ref.at[me, :, pl.ds(0, D)],
            send_sem=send_sem.at[j],
            recv_sem=recv_sem.at[0],
            device_id=(j, 0),
            device_id_type=MESH,
        )

    def sw_copy(j):
        return pltpu.make_async_remote_copy(
            src_ref=sw_ref.at[j],
            dst_ref=out_ref.at[me],
            send_sem=send_sem.at[n_sq + j],
            recv_sem=recv_sem.at[0],
            device_id=(n_sq + j, 0),
            device_id_type=MESH,
        )

    def start_sq(j, carry):
        @pl.when(me == 2 * j)
        def _():
            pltpu.make_async_copy(sq_ref.at[j], out_ref.at[me, :, pl.ds(0, D)], recv_sem.at[0]).start()

        @pl.when(me != 2 * j)
        def _():
            sq_copy(j).start()

        return carry

    def start_sw(j, carry):
        @pl.when(me == 2 * (n_sq + j))
        def _():
            pltpu.make_async_copy(sw_ref.at[j], out_ref.at[me], recv_sem.at[0]).start()

        @pl.when(me != 2 * (n_sq + j))
        def _():
            sw_copy(j).start()

        return carry

    lax.fori_loop(0, n_sq, start_sq, 0)
    lax.fori_loop(0, n_sw, start_sw, 0)

    @pl.when((t == 0) & (d < n_sq))
    def _():
        region = out_ref.at[:, :, pl.ds(0, D)]
        pltpu.make_async_copy(region, region, recv_sem.at[0]).wait()

    @pl.when((t == 0) & (d >= n_sq) & (d < n_sq + n_sw))
    def _():
        pltpu.make_async_copy(out_ref, out_ref, recv_sem.at[0]).wait()

    def wait_sq(j, carry):
        @pl.when(me != 2 * j)
        def _():
            sq_copy(j).wait_send()

        return carry

    def wait_sw(j, carry):
        @pl.when(me != 2 * (n_sq + j))
        def _():
            sw_copy(j).wait_send()

        return carry

    lax.fori_loop(0, n_sq, wait_sq, 0)
    lax.fori_loop(0, n_sw, wait_sw, 0)


def gather_kernel(n_sq, n_sw, it_ref, osq_ref, osw_ref, send_sem, recv_sem):
    d = lax.axis_index("dp")
    t = lax.axis_index("tensor")
    n_dev = lax.axis_size("dp") * 2
    me = d * 2 + t
    device_barrier(n_dev, me)
    is_sq = (t == 0) & (d < n_sq)
    is_sw = (t == 0) & (d >= n_sq) & (d < n_sq + n_sw)
    sq_w = osq_ref.shape[2]
    sw_w = osw_ref.shape[2]
    j_sq = jnp.minimum(d, n_sq - 1)
    j_sw = jnp.clip(d - n_sq, 0, n_sw - 1)

    def sq_copy(g):
        return pltpu.make_async_remote_copy(
            src_ref=it_ref.at[g // 2, :, pl.ds(pl.multiple_of(lax.rem(g, 2) * sq_w, 128), sq_w)],
            dst_ref=osq_ref.at[j_sq],
            send_sem=send_sem.at[g],
            recv_sem=recv_sem.at[0],
            device_id=(g // 2, lax.rem(g, 2)),
            device_id_type=MESH,
        )

    def sw_copy(g):
        return pltpu.make_async_remote_copy(
            src_ref=it_ref.at[g // 2, :, pl.ds(pl.multiple_of(lax.rem(g, 2) * sw_w, 128), sw_w)],
            dst_ref=osw_ref.at[j_sw],
            send_sem=send_sem.at[g],
            recv_sem=recv_sem.at[1],
            device_id=(g // 2, lax.rem(g, 2)),
            device_id_type=MESH,
        )

    @pl.when(is_sq)
    def _():
        def start(g, carry):
            @pl.when(g == me)
            def _():
                pltpu.make_async_copy(
                    it_ref.at[d, :, pl.ds(0, sq_w)], osq_ref.at[j_sq], recv_sem.at[0]
                ).start()

            @pl.when(g != me)
            def _():
                sq_copy(g).start()

            return carry

        lax.fori_loop(0, n_dev, start, 0)

    @pl.when(is_sw)
    def _():
        def start(g, carry):
            @pl.when(g == me)
            def _():
                pltpu.make_async_copy(
                    it_ref.at[d, :, pl.ds(0, sw_w)], osw_ref.at[j_sw], recv_sem.at[1]
                ).start()

            @pl.when(g != me)
            def _():
                sw_copy(g).start()

            return carry

        lax.fori_loop(0, n_dev, start, 0)

    pltpu.make_async_copy(osq_ref, osq_ref, recv_sem.at[0]).wait()
    pltpu.make_async_copy(osw_ref, osw_ref, recv_sem.at[1]).wait()

    @pl.when(is_sq)
    def _():
        def wait(g, carry):
            @pl.when(g != me)
            def _():
                sq_copy(g).wait_send()

            return carry

        lax.fori_loop(0, n_dev, wait, 0)

    @pl.when(is_sw)
    def _():
        def wait(g, carry):
            @pl.when(g != me)
            def _():
                sw_copy(g).wait_send()

            return carry

        lax.fori_loop(0, n_dev, wait, 0)


def orthogonalize(matrix, factor):
    iterate = matrix
    first_scale = jnp.float32(1.0)
    for round_index in range(NS_STEPS):
        gram = jnp.dot(iterate, iterate.T, preferred_element_type=jnp.float32)
        if round_index == 0:
            gram_scale = jnp.sqrt(jnp.sum(gram * gram)) + 1e-06
            first_scale = gram_scale
        else:
            gram_scale = jnp.float32(1.0)
        normed = (gram / gram_scale).astype(jnp.bfloat16)
        squared = jnp.dot(normed, normed, preferred_element_type=jnp.float32)
        polynomial = (QUINTIC_CUBIC * normed.astype(jnp.float32) + QUINTIC_FIFTH * squared).astype(
            jnp.bfloat16
        )
        product = jnp.dot(polynomial, iterate, preferred_element_type=jnp.float32)
        mixed = (QUINTIC_LINEAR * iterate.astype(jnp.float32) + product) / jnp.sqrt(gram_scale)
        if round_index == NS_STEPS - 1:
            iterate = (factor * mixed).astype(jnp.bfloat16)
        else:
            iterate = mixed.astype(jnp.bfloat16)
    return (iterate, first_scale)


def local(
    square_grad,
    square_state,
    swiglu_grad,
    swiglu_state,
    square_order,
    swiglu_order,
    owners,
    vector_values,
    vector_grad,
    vector_first,
    vector_second,
    embed_values,
    embed_grad,
    embed_first,
    embed_second,
    embed_ranges,
):
    wide_count = lax.axis_size("dp")
    n_dev = wide_count * 2
    d = lax.axis_index("dp")
    t = lax.axis_index("tensor")
    n_sq = square_grad.shape[0]
    n_sw = swiglu_grad.shape[0]
    flat_rows = D // n_dev
    out_rows = D // wide_count
    square_next, square_send = momentum_terms(square_grad, square_state)
    swiglu_next, swiglu_send = momentum_terms(swiglu_grad, swiglu_state)
    sq_pieces = square_send.reshape(n_sq, flat_rows, D)
    sw_pieces = swiglu_send.reshape(n_sw, flat_rows, FF)

    arrived = pl.pallas_call(
        lambda *refs: scatter_kernel(n_sq, n_sw, *refs),
        out_shape=jax.ShapeDtypeStruct((n_dev, flat_rows, FF), jnp.bfloat16),
        in_specs=[pl.BlockSpec(memory_space=pl.ANY)] * 2,
        out_specs=pl.BlockSpec(memory_space=pl.ANY),
        scratch_shapes=[
            pltpu.SemaphoreType.DMA((n_sq + n_sw,)),
            pltpu.SemaphoreType.DMA((1,)),
        ],
        compiler_params=pltpu.CompilerParams(collective_id=0, has_side_effects=True),
    )(sq_pieces, sw_pieces)

    is_sq = (t == 0) & (d < n_sq)
    is_sw = (t == 0) & (d >= n_sq) & (d < n_sq + n_sw)
    width = jnp.where(is_sq, D, jnp.where(is_sw, FF, 0))
    columns = lax.broadcasted_iota(jnp.int32, (D, FF), 1)
    matrix = jnp.where(columns < width, arrived.reshape(D, FF), jnp.zeros((), jnp.bfloat16))
    factor = jnp.where(is_sq, jnp.float32(math.sqrt(D)), jnp.float32(math.sqrt(FF)))
    iterate, first_scale = orthogonalize(matrix, factor)

    returned_sq, returned_sw = pl.pallas_call(
        lambda *refs: gather_kernel(n_sq, n_sw, *refs),
        out_shape=(
            jax.ShapeDtypeStruct((n_sq, out_rows, D // 2), jnp.bfloat16),
            jax.ShapeDtypeStruct((n_sw, out_rows, FF // 2), jnp.bfloat16),
        ),
        in_specs=[pl.BlockSpec(memory_space=pl.ANY)],
        out_specs=(pl.BlockSpec(memory_space=pl.ANY), pl.BlockSpec(memory_space=pl.ANY)),
        scratch_shapes=[
            pltpu.SemaphoreType.DMA((n_dev,)),
            pltpu.SemaphoreType.DMA((2,)),
        ],
        compiler_params=pltpu.CompilerParams(collective_id=1, has_side_effects=True),
    )(iterate.reshape(wide_count, out_rows, FF))

    inv_sq = inverse_of(square_order)
    inv_sw = inverse_of(swiglu_order)
    square_update = returned_sq[inv_sq]
    swiglu_update = returned_sw[inv_sw]

    slots = jnp.arange(n_sq + n_sw, dtype=jnp.int32)
    mine = (is_sq | is_sw) & (slots == d)
    slot_norms = lax.psum(jnp.where(mine, 0.5 * jnp.log(first_scale), 0.0), ("dp", "tensor"))
    matrix_slot = jnp.concatenate([inv_sq, n_sq + inv_sw])
    matrix_norms = slot_norms[matrix_slot]
    owner_norms = jnp.sum(jnp.where(owners == d, matrix_norms, 0.0)).reshape(1)

    vector_step, first_vector, second_vector = adamw_terms(
        vector_values, vector_grad, vector_first, vector_second
    )
    embed_rows = embed_values.shape[0]
    row_numbers = d * embed_rows + jnp.arange(embed_rows, dtype=jnp.int32)
    inside = (row_numbers[:, None] >= embed_ranges[None, :, 0]) & (
        row_numbers[:, None] < embed_ranges[None, :, 1]
    )
    row_live = jnp.sum(inside.astype(jnp.int32), axis=1) > 0
    direction, first_next, second_next = adamw_terms(
        embed_values, embed_grad, embed_first, embed_second
    )
    embed_step = jnp.where(row_live[:, None], direction, 0.0)
    first_embed = jnp.where(row_live[:, None], first_next, embed_first)
    second_embed = jnp.where(row_live[:, None], second_next, embed_second)
    return (
        square_next,
        swiglu_next,
        square_update,
        swiglu_update,
        owner_norms,
        vector_step,
        first_vector,
        second_vector,
        embed_step,
        first_embed,
        second_embed,
    )


def solution(mesh):
    placed = (
        P(None, ("dp", "tensor")),
        P(None, ("dp", "tensor")),
        P(None, ("dp", "tensor")),
        P(None, ("dp", "tensor")),
        P(),
        P(),
        P(),
        P(("dp", "tensor")),
        P(("dp", "tensor")),
        P(("dp", "tensor")),
        P(("dp", "tensor")),
        P("dp", "tensor"),
        P("dp", "tensor"),
        P("dp", "tensor"),
        P("dp", "tensor"),
        P(),
    )
    return jax.shard_map(
        local,
        mesh=mesh,
        in_specs=placed,
        out_specs=(
            P(None, ("dp", "tensor")),
            P(None, ("dp", "tensor")),
            P(None, "dp", "tensor"),
            P(None, "dp", "tensor"),
            P("dp"),
            P(("dp", "tensor")),
            P(("dp", "tensor")),
            P(("dp", "tensor")),
            P("dp", "tensor"),
            P("dp", "tensor"),
            P("dp", "tensor"),
        ),
        check_vma=False,
    )
```

```python
import math

import jax
import jax.numpy as jnp
from jax import lax
from jax.experimental import pallas as pl
from jax.experimental.pallas import tpu as pltpu
from jax.sharding import PartitionSpec as P

D = 1536
FF = 4096
NS_STEPS = 2
MESH = pl.DeviceIdType.MESH

QUINTIC_LINEAR = 3.4445
QUINTIC_CUBIC = -4.775
QUINTIC_FIFTH = 2.0315
MOMENTUM = 0.95
BIAS_FIRST = 1.0 - 0.9**10
BIAS_SECOND = 1.0 - 0.95**10


def momentum_terms(gradient, state):
    state_next = MOMENTUM * state + gradient
    return (state_next, (gradient + MOMENTUM * state_next).astype(jnp.bfloat16))


def adamw_terms(values, gradient, first, second):
    first_next = 0.9 * first + 0.1 * gradient
    second_next = 0.95 * second + 0.05 * gradient * gradient
    direction = (
        first_next / BIAS_FIRST / (jnp.sqrt(second_next / BIAS_SECOND) + 1e-08) + 0.1 * values
    )
    return (direction, first_next, second_next)


def inverse_of(order):
    count = order.shape[0]
    return jnp.zeros((count,), jnp.int32).at[order].set(jnp.arange(count, dtype=jnp.int32))


def device_barrier(n_dev, me, pairs):
    barrier = pltpu.get_barrier_semaphore()
    t = lax.axis_index("tensor")

    def signal(k, carry):
        target = lax.rem(me + k, n_dev)
        if pairs:
            device = (target // 2, lax.rem(target, 2))
        else:
            device = (target, t)
        pl.semaphore_signal(barrier, inc=1, device_id=device, device_id_type=MESH)
        return carry

    lax.fori_loop(1, n_dev, signal, 0)
    pl.semaphore_wait(barrier, n_dev - 1)


def scatter_kernel(n_sq, n_sw, sq_ref, sw_ref, zero_ref, out_ref, send_sem, recv_sem):
    del zero_ref
    d = lax.axis_index("dp")
    t = lax.axis_index("tensor")
    n_dev = lax.axis_size("dp") * 2
    me = d * 2 + t
    n_pairs = 2 * (n_sq + n_sw)
    sq_w = sq_ref.shape[2] // 2
    sw_w = sw_ref.shape[2] // 2
    device_barrier(n_dev, me, True)

    def sq_copy(g, h):
        return pltpu.make_async_remote_copy(
            src_ref=sq_ref.at[g, :, pl.ds(pl.multiple_of(h * sq_w, 128), sq_w)],
            dst_ref=out_ref.at[me, :, pl.ds(0, sq_w)],
            send_sem=send_sem.at[2 * g + h],
            recv_sem=recv_sem.at[0],
            device_id=(g, h),
            device_id_type=MESH,
        )

    def sw_copy(g, h):
        j = g - n_sq
        return pltpu.make_async_remote_copy(
            src_ref=sw_ref.at[j, :, pl.ds(pl.multiple_of(h * sw_w, 128), sw_w)],
            dst_ref=out_ref.at[me, :, pl.ds(0, sw_w)],
            send_sem=send_sem.at[2 * g + h],
            recv_sem=recv_sem.at[0],
            device_id=(g, h),
            device_id_type=MESH,
        )

    def start(k, carry):
        q = lax.rem(k + me, n_pairs)
        g = q // 2
        h = lax.rem(q, 2)
        local = (g == d) & (h == t)

        @pl.when(local & (g < n_sq))
        def _():
            pltpu.make_async_copy(
                sq_ref.at[g, :, pl.ds(pl.multiple_of(h * sq_w, 128), sq_w)],
                out_ref.at[me, :, pl.ds(0, sq_w)],
                recv_sem.at[0],
            ).start()

        @pl.when(local & (g >= n_sq))
        def _():
            pltpu.make_async_copy(
                sw_ref.at[g - n_sq, :, pl.ds(pl.multiple_of(h * sw_w, 128), sw_w)],
                out_ref.at[me, :, pl.ds(0, sw_w)],
                recv_sem.at[0],
            ).start()

        @pl.when(jnp.logical_not(local) & (g < n_sq))
        def _():
            sq_copy(g, h).start()

        @pl.when(jnp.logical_not(local) & (g >= n_sq))
        def _():
            sw_copy(g, h).start()

        return carry

    lax.fori_loop(0, n_pairs, start, 0)

    @pl.when(d < n_sq)
    def _():
        region = out_ref.at[:, :, pl.ds(0, sq_w)]
        pltpu.make_async_copy(region, region, recv_sem.at[0]).wait()

    @pl.when((d >= n_sq) & (d < n_sq + n_sw))
    def _():
        region = out_ref.at[:, :, pl.ds(0, sw_w)]
        pltpu.make_async_copy(region, region, recv_sem.at[0]).wait()

    def wait(q, carry):
        g = q // 2
        h = lax.rem(q, 2)
        local = (g == d) & (h == t)

        @pl.when(jnp.logical_not(local) & (g < n_sq))
        def _():
            sq_copy(g, h).wait_send()

        @pl.when(jnp.logical_not(local) & (g >= n_sq))
        def _():
            sw_copy(g, h).wait_send()

        return carry

    lax.fori_loop(0, n_pairs, wait, 0)


def gather_kernel(n_sq, n_sw, it_ref, osq_ref, osw_ref, send_sem, recv_sem):
    d = lax.axis_index("dp")
    t = lax.axis_index("tensor")
    n_dp = lax.axis_size("dp")
    device_barrier(n_dp, d, False)
    is_sq = d < n_sq
    is_sw = (d >= n_sq) & (d < n_sq + n_sw)
    sq_w = osq_ref.shape[2]
    sw_w = osw_ref.shape[2]
    j_sq = jnp.minimum(d, n_sq - 1)
    j_sw = jnp.clip(d - n_sq, 0, n_sw - 1)

    def sq_copy(r):
        return pltpu.make_async_remote_copy(
            src_ref=it_ref.at[r, :, pl.ds(0, sq_w)],
            dst_ref=osq_ref.at[j_sq],
            send_sem=send_sem.at[r],
            recv_sem=recv_sem.at[0],
            device_id=(r, t),
            device_id_type=MESH,
        )

    def sw_copy(r):
        return pltpu.make_async_remote_copy(
            src_ref=it_ref.at[r, :, pl.ds(0, sw_w)],
            dst_ref=osw_ref.at[j_sw],
            send_sem=send_sem.at[r],
            recv_sem=recv_sem.at[1],
            device_id=(r, t),
            device_id_type=MESH,
        )

    @pl.when(is_sq)
    def _():
        def start(k, carry):
            r = lax.rem(d + k, n_dp)

            @pl.when(r == d)
            def _():
                pltpu.make_async_copy(
                    it_ref.at[d, :, pl.ds(0, sq_w)], osq_ref.at[j_sq], recv_sem.at[0]
                ).start()

            @pl.when(r != d)
            def _():
                sq_copy(r).start()

            return carry

        lax.fori_loop(0, n_dp, start, 0)

    @pl.when(is_sw)
    def _():
        def start(k, carry):
            r = lax.rem(d + k, n_dp)

            @pl.when(r == d)
            def _():
                pltpu.make_async_copy(
                    it_ref.at[d, :, pl.ds(0, sw_w)], osw_ref.at[j_sw], recv_sem.at[1]
                ).start()

            @pl.when(r != d)
            def _():
                sw_copy(r).start()

            return carry

        lax.fori_loop(0, n_dp, start, 0)

    pltpu.make_async_copy(osq_ref, osq_ref, recv_sem.at[0]).wait()
    pltpu.make_async_copy(osw_ref, osw_ref, recv_sem.at[1]).wait()

    @pl.when(is_sq)
    def _():
        def wait(r, carry):
            @pl.when(r != d)
            def _():
                sq_copy(r).wait_send()

            return carry

        lax.fori_loop(0, n_dp, wait, 0)

    @pl.when(is_sw)
    def _():
        def wait(r, carry):
            @pl.when(r != d)
            def _():
                sw_copy(r).wait_send()

            return carry

        lax.fori_loop(0, n_dp, wait, 0)


def orthogonalize(arrived, factor):
    iterate = arrived
    first_scale = jnp.float32(1.0)
    for round_index in range(NS_STEPS):
        current = iterate
        gram_part = lax.psum_scatter(
            jnp.einsum("rc,sc->rs", current, current, preferred_element_type=jnp.float32),
            "tensor",
            scatter_dimension=0,
            tiled=True,
        )
        if round_index == 0:
            squares_total = lax.psum(jnp.sum(gram_part * gram_part), "tensor")
            gram_scale = jnp.sqrt(squares_total) + 1e-06
            first_scale = gram_scale
        else:
            gram_scale = jnp.float32(1.0)
        normed_part = (gram_part / gram_scale).astype(jnp.bfloat16)
        squared = jnp.dot(
            normed_part,
            lax.all_gather(normed_part, "tensor", axis=0, tiled=True),
            preferred_element_type=jnp.float32,
        )
        polynomial = (
            QUINTIC_CUBIC * normed_part.astype(jnp.float32) + QUINTIC_FIFTH * squared
        ).astype(jnp.bfloat16)
        product = jnp.dot(
            lax.all_gather(polynomial, "tensor", axis=0, tiled=True),
            current,
            preferred_element_type=jnp.float32,
        )
        mixed = (QUINTIC_LINEAR * current.astype(jnp.float32) + product) / jnp.sqrt(gram_scale)
        if round_index == NS_STEPS - 1:
            iterate = (factor * mixed).astype(jnp.bfloat16)
        else:
            iterate = mixed.astype(jnp.bfloat16)
    return (iterate, first_scale)


def local(
    square_grad,
    square_state,
    swiglu_grad,
    swiglu_state,
    square_order,
    swiglu_order,
    owners,
    vector_values,
    vector_grad,
    vector_first,
    vector_second,
    embed_values,
    embed_grad,
    embed_first,
    embed_second,
    embed_ranges,
):
    wide_count = lax.axis_size("dp")
    n_dev = wide_count * 2
    d = lax.axis_index("dp")
    t = lax.axis_index("tensor")
    n_sq = square_grad.shape[0]
    n_sw = swiglu_grad.shape[0]
    flat_rows = D // n_dev
    out_rows = D // wide_count
    square_next, square_send = momentum_terms(square_grad, square_state)
    swiglu_next, swiglu_send = momentum_terms(swiglu_grad, swiglu_state)
    sq_pieces = square_send.reshape(n_sq, flat_rows, D)
    sw_pieces = swiglu_send.reshape(n_sw, flat_rows, FF)

    half = FF // 2
    arrived = pl.pallas_call(
        lambda *refs: scatter_kernel(n_sq, n_sw, *refs),
        out_shape=jax.ShapeDtypeStruct((n_dev, flat_rows, half), jnp.bfloat16),
        in_specs=[pl.BlockSpec(memory_space=pl.ANY)] * 3,
        out_specs=pl.BlockSpec(memory_space=pl.ANY),
        scratch_shapes=[
            pltpu.SemaphoreType.DMA((2 * (n_sq + n_sw),)),
            pltpu.SemaphoreType.DMA((1,)),
        ],
        input_output_aliases={2: 0},
        compiler_params=pltpu.CompilerParams(collective_id=0, has_side_effects=True),
    )(sq_pieces, sw_pieces, jnp.zeros((n_dev, flat_rows, half), jnp.bfloat16))

    is_sq = d < n_sq
    is_sw = (d >= n_sq) & (d < n_sq + n_sw)
    factor = jnp.where(is_sq, jnp.float32(math.sqrt(D)), jnp.float32(math.sqrt(FF)))
    iterate, first_scale = orthogonalize(arrived.reshape(D, half), factor)

    returned_sq, returned_sw = pl.pallas_call(
        lambda *refs: gather_kernel(n_sq, n_sw, *refs),
        out_shape=(
            jax.ShapeDtypeStruct((n_sq, out_rows, D // 2), jnp.bfloat16),
            jax.ShapeDtypeStruct((n_sw, out_rows, FF // 2), jnp.bfloat16),
        ),
        in_specs=[pl.BlockSpec(memory_space=pl.ANY)],
        out_specs=(pl.BlockSpec(memory_space=pl.ANY), pl.BlockSpec(memory_space=pl.ANY)),
        scratch_shapes=[
            pltpu.SemaphoreType.DMA((wide_count,)),
            pltpu.SemaphoreType.DMA((2,)),
        ],
        compiler_params=pltpu.CompilerParams(collective_id=1, has_side_effects=True),
    )(iterate.reshape(wide_count, out_rows, half))

    inv_sq = inverse_of(square_order)
    inv_sw = inverse_of(swiglu_order)
    square_update = returned_sq[inv_sq]
    swiglu_update = returned_sw[inv_sw]

    slots = jnp.arange(n_sq + n_sw, dtype=jnp.int32)
    mine = (t == 0) & (slots == d)
    slot_norms = lax.psum(jnp.where(mine, 0.5 * jnp.log(first_scale), 0.0), ("dp", "tensor"))
    matrix_slot = jnp.concatenate([inv_sq, n_sq + inv_sw])
    matrix_norms = slot_norms[matrix_slot]
    owner_norms = jnp.sum(jnp.where(owners == d, matrix_norms, 0.0)).reshape(1)

    vector_step, first_vector, second_vector = adamw_terms(
        vector_values, vector_grad, vector_first, vector_second
    )
    embed_rows = embed_values.shape[0]
    row_numbers = d * embed_rows + jnp.arange(embed_rows, dtype=jnp.int32)
    inside = (row_numbers[:, None] >= embed_ranges[None, :, 0]) & (
        row_numbers[:, None] < embed_ranges[None, :, 1]
    )
    row_live = jnp.sum(inside.astype(jnp.int32), axis=1) > 0
    direction, first_next, second_next = adamw_terms(
        embed_values, embed_grad, embed_first, embed_second
    )
    embed_step = jnp.where(row_live[:, None], direction, 0.0)
    first_embed = jnp.where(row_live[:, None], first_next, embed_first)
    second_embed = jnp.where(row_live[:, None], second_next, embed_second)
    return (
        square_next,
        swiglu_next,
        square_update,
        swiglu_update,
        owner_norms,
        vector_step,
        first_vector,
        second_vector,
        embed_step,
        first_embed,
        second_embed,
    )


def solution(mesh):
    placed = (
        P(None, ("dp", "tensor")),
        P(None, ("dp", "tensor")),
        P(None, ("dp", "tensor")),
        P(None, ("dp", "tensor")),
        P(),
        P(),
        P(),
        P(("dp", "tensor")),
        P(("dp", "tensor")),
        P(("dp", "tensor")),
        P(("dp", "tensor")),
        P("dp", "tensor"),
        P("dp", "tensor"),
        P("dp", "tensor"),
        P("dp", "tensor"),
        P(),
    )
    return jax.shard_map(
        local,
        mesh=mesh,
        in_specs=placed,
        out_specs=(
            P(None, ("dp", "tensor")),
            P(None, ("dp", "tensor")),
            P(None, "dp", "tensor"),
            P(None, "dp", "tensor"),
            P("dp"),
            P(("dp", "tensor")),
            P(("dp", "tensor")),
            P(("dp", "tensor")),
            P("dp", "tensor"),
            P("dp", "tensor"),
            P("dp", "tensor"),
        ),
        check_vma=False,
    )
```

```python
import math

import jax
import jax.numpy as jnp
from jax import lax
from jax.experimental import pallas as pl
from jax.experimental.pallas import tpu as pltpu
from jax.sharding import PartitionSpec as P

D = 1536
FF = 4096
NS_STEPS = 2
MESH = pl.DeviceIdType.MESH

QUINTIC_LINEAR = 3.4445
QUINTIC_CUBIC = -4.775
QUINTIC_FIFTH = 2.0315
MOMENTUM = 0.95
BIAS_FIRST = 1.0 - 0.9**10
BIAS_SECOND = 1.0 - 0.95**10


def momentum_terms(gradient, state):
    state_next = MOMENTUM * state + gradient
    return (state_next, (gradient + MOMENTUM * state_next).astype(jnp.bfloat16))


def adamw_terms(values, gradient, first, second):
    first_next = 0.9 * first + 0.1 * gradient
    second_next = 0.95 * second + 0.05 * gradient * gradient
    direction = (
        first_next / BIAS_FIRST / (jnp.sqrt(second_next / BIAS_SECOND) + 1e-08) + 0.1 * values
    )
    return (direction, first_next, second_next)


def inverse_of(order):
    count = order.shape[0]
    return jnp.zeros((count,), jnp.int32).at[order].set(jnp.arange(count, dtype=jnp.int32))


def device_barrier(n_dev, me, pairs):
    barrier = pltpu.get_barrier_semaphore()
    t = lax.axis_index("tensor")

    def signal(k, carry):
        target = lax.rem(me + k, n_dev)
        if pairs:
            device = (target // 2, lax.rem(target, 2))
        else:
            device = (target, t)
        pl.semaphore_signal(barrier, inc=1, device_id=device, device_id_type=MESH)
        return carry

    lax.fori_loop(1, n_dev, signal, 0)
    pl.semaphore_wait(barrier, n_dev - 1)


def scatter_kernel(n_sq, n_sw, sq_ref, sw_ref, zero_ref, out_ref, send_sem, recv_sem):
    del zero_ref
    d = lax.axis_index("dp")
    t = lax.axis_index("tensor")
    n_dev = lax.axis_size("dp") * 2
    me = d * 2 + t
    n_pairs = 2 * (n_sq + n_sw)
    sq_w = sq_ref.shape[2] // 2
    sw_w = sw_ref.shape[2] // 2
    device_barrier(n_dev, me, True)

    def sq_copy(g, h):
        return pltpu.make_async_remote_copy(
            src_ref=sq_ref.at[g, :, pl.ds(pl.multiple_of(h * sq_w, 128), sq_w)],
            dst_ref=out_ref.at[me, :, pl.ds(0, sq_w)],
            send_sem=send_sem.at[2 * g + h],
            recv_sem=recv_sem.at[0],
            device_id=(g, h),
            device_id_type=MESH,
        )

    def sw_copy(g, h):
        j = g - n_sq
        return pltpu.make_async_remote_copy(
            src_ref=sw_ref.at[j, :, pl.ds(pl.multiple_of(h * sw_w, 128), sw_w)],
            dst_ref=out_ref.at[me, :, pl.ds(0, sw_w)],
            send_sem=send_sem.at[2 * g + h],
            recv_sem=recv_sem.at[0],
            device_id=(g, h),
            device_id_type=MESH,
        )

    def start(k, carry):
        q = lax.rem(k + me, n_pairs)
        g = q // 2
        h = lax.rem(q, 2)
        local = (g == d) & (h == t)

        @pl.when(local & (g < n_sq))
        def _():
            pltpu.make_async_copy(
                sq_ref.at[g, :, pl.ds(pl.multiple_of(h * sq_w, 128), sq_w)],
                out_ref.at[me, :, pl.ds(0, sq_w)],
                recv_sem.at[0],
            ).start()

        @pl.when(local & (g >= n_sq))
        def _():
            pltpu.make_async_copy(
                sw_ref.at[g - n_sq, :, pl.ds(pl.multiple_of(h * sw_w, 128), sw_w)],
                out_ref.at[me, :, pl.ds(0, sw_w)],
                recv_sem.at[0],
            ).start()

        @pl.when(jnp.logical_not(local) & (g < n_sq))
        def _():
            sq_copy(g, h).start()

        @pl.when(jnp.logical_not(local) & (g >= n_sq))
        def _():
            sw_copy(g, h).start()

        return carry

    lax.fori_loop(0, n_pairs, start, 0)

    @pl.when(d < n_sq)
    def _():
        region = out_ref.at[:, :, pl.ds(0, sq_w)]
        pltpu.make_async_copy(region, region, recv_sem.at[0]).wait()

    @pl.when((d >= n_sq) & (d < n_sq + n_sw))
    def _():
        region = out_ref.at[:, :, pl.ds(0, sw_w)]
        pltpu.make_async_copy(region, region, recv_sem.at[0]).wait()

    def wait(q, carry):
        g = q // 2
        h = lax.rem(q, 2)
        local = (g == d) & (h == t)

        @pl.when(jnp.logical_not(local) & (g < n_sq))
        def _():
            sq_copy(g, h).wait_send()

        @pl.when(jnp.logical_not(local) & (g >= n_sq))
        def _():
            sw_copy(g, h).wait_send()

        return carry

    lax.fori_loop(0, n_pairs, wait, 0)


def gather_kernel(n_sq, n_sw, it_ref, osq_ref, osw_ref, send_sem, recv_sem):
    d = lax.axis_index("dp")
    t = lax.axis_index("tensor")
    n_dp = lax.axis_size("dp")
    device_barrier(n_dp, d, False)
    is_sq = d < n_sq
    is_sw = (d >= n_sq) & (d < n_sq + n_sw)
    sq_w = osq_ref.shape[2]
    sw_w = osw_ref.shape[2]
    j_sq = jnp.minimum(d, n_sq - 1)
    j_sw = jnp.clip(d - n_sq, 0, n_sw - 1)

    def sq_copy(r):
        return pltpu.make_async_remote_copy(
            src_ref=it_ref.at[r, :, pl.ds(0, sq_w)],
            dst_ref=osq_ref.at[j_sq],
            send_sem=send_sem.at[r],
            recv_sem=recv_sem.at[0],
            device_id=(r, t),
            device_id_type=MESH,
        )

    def sw_copy(r):
        return pltpu.make_async_remote_copy(
            src_ref=it_ref.at[r, :, pl.ds(0, sw_w)],
            dst_ref=osw_ref.at[j_sw],
            send_sem=send_sem.at[r],
            recv_sem=recv_sem.at[1],
            device_id=(r, t),
            device_id_type=MESH,
        )

    @pl.when(is_sq)
    def _():
        def start(k, carry):
            r = lax.rem(d + k, n_dp)

            @pl.when(r == d)
            def _():
                pltpu.make_async_copy(
                    it_ref.at[d, :, pl.ds(0, sq_w)], osq_ref.at[j_sq], recv_sem.at[0]
                ).start()

            @pl.when(r != d)
            def _():
                sq_copy(r).start()

            return carry

        lax.fori_loop(0, n_dp, start, 0)

    @pl.when(is_sw)
    def _():
        def start(k, carry):
            r = lax.rem(d + k, n_dp)

            @pl.when(r == d)
            def _():
                pltpu.make_async_copy(
                    it_ref.at[d, :, pl.ds(0, sw_w)], osw_ref.at[j_sw], recv_sem.at[1]
                ).start()

            @pl.when(r != d)
            def _():
                sw_copy(r).start()

            return carry

        lax.fori_loop(0, n_dp, start, 0)

    pltpu.make_async_copy(osq_ref, osq_ref, recv_sem.at[0]).wait()
    pltpu.make_async_copy(osw_ref, osw_ref, recv_sem.at[1]).wait()

    @pl.when(is_sq)
    def _():
        def wait(r, carry):
            @pl.when(r != d)
            def _():
                sq_copy(r).wait_send()

            return carry

        lax.fori_loop(0, n_dp, wait, 0)

    @pl.when(is_sw)
    def _():
        def wait(r, carry):
            @pl.when(r != d)
            def _():
                sw_copy(r).wait_send()

            return carry

        lax.fori_loop(0, n_dp, wait, 0)


def orthogonalize(arrived, factor):
    iterate = arrived
    first_scale = jnp.float32(1.0)
    for round_index in range(NS_STEPS):
        current = iterate
        gram_part = lax.psum_scatter(
            jnp.einsum("rc,sc->rs", current, current, preferred_element_type=jnp.float32),
            "tensor",
            scatter_dimension=0,
            tiled=True,
        )
        if round_index == 0:
            squares_total = lax.psum(jnp.sum(gram_part * gram_part), "tensor")
            gram_scale = jnp.sqrt(squares_total) + 1e-06
            first_scale = gram_scale
        else:
            gram_scale = jnp.float32(1.0)
        normed_part = (gram_part / gram_scale).astype(jnp.bfloat16)
        squared = jnp.dot(
            normed_part,
            lax.all_gather(normed_part, "tensor", axis=0, tiled=True),
            preferred_element_type=jnp.float32,
        )
        polynomial = (
            QUINTIC_CUBIC * normed_part.astype(jnp.float32) + QUINTIC_FIFTH * squared
        ).astype(jnp.bfloat16)
        product = jnp.dot(
            lax.all_gather(polynomial, "tensor", axis=0, tiled=True),
            current,
            preferred_element_type=jnp.float32,
        )
        mixed = (QUINTIC_LINEAR * current.astype(jnp.float32) + product) / jnp.sqrt(gram_scale)
        if round_index == NS_STEPS - 1:
            iterate = (factor * mixed).astype(jnp.bfloat16)
        else:
            iterate = mixed.astype(jnp.bfloat16)
    return (iterate, first_scale)


def with_scale_row(blocks, scale):
    high = scale.astype(jnp.bfloat16)
    low = (scale - high.astype(jnp.float32)).astype(jnp.bfloat16)
    lanes = lax.broadcasted_iota(jnp.int32, (blocks.shape[0], 1, blocks.shape[2]), 2)
    row = jnp.where(lanes == 0, high, jnp.where(lanes == 1, low, jnp.zeros((), jnp.bfloat16)))
    return jnp.concatenate([blocks, row], axis=1)


def scale_of_row(returned):
    row = returned[:, -1, :2].astype(jnp.float32)
    return row[:, 0] + row[:, 1]


def local(
    square_grad,
    square_state,
    swiglu_grad,
    swiglu_state,
    square_order,
    swiglu_order,
    owners,
    vector_values,
    vector_grad,
    vector_first,
    vector_second,
    embed_values,
    embed_grad,
    embed_first,
    embed_second,
    embed_ranges,
):
    wide_count = lax.axis_size("dp")
    n_dev = wide_count * 2
    d = lax.axis_index("dp")
    t = lax.axis_index("tensor")
    n_sq = square_grad.shape[0]
    n_sw = swiglu_grad.shape[0]
    flat_rows = D // n_dev
    out_rows = D // wide_count
    square_next, square_send = momentum_terms(square_grad, square_state)
    swiglu_next, swiglu_send = momentum_terms(swiglu_grad, swiglu_state)
    sq_pieces = square_send.reshape(n_sq, flat_rows, D)
    sw_pieces = swiglu_send.reshape(n_sw, flat_rows, FF)

    half = FF // 2
    arrived = pl.pallas_call(
        lambda *refs: scatter_kernel(n_sq, n_sw, *refs),
        out_shape=jax.ShapeDtypeStruct((n_dev, flat_rows, half), jnp.bfloat16),
        in_specs=[pl.BlockSpec(memory_space=pl.ANY)] * 3,
        out_specs=pl.BlockSpec(memory_space=pl.ANY),
        scratch_shapes=[
            pltpu.SemaphoreType.DMA((2 * (n_sq + n_sw),)),
            pltpu.SemaphoreType.DMA((1,)),
        ],
        input_output_aliases={2: 0},
        compiler_params=pltpu.CompilerParams(collective_id=0, has_side_effects=True),
    )(sq_pieces, sw_pieces, jnp.zeros((n_dev, flat_rows, half), jnp.bfloat16))

    is_sq = d < n_sq
    is_sw = (d >= n_sq) & (d < n_sq + n_sw)
    factor = jnp.where(is_sq, jnp.float32(math.sqrt(D)), jnp.float32(math.sqrt(FF)))
    iterate, first_scale = orthogonalize(arrived.reshape(D, half), factor)

    returned_sq, returned_sw = pl.pallas_call(
        lambda *refs: gather_kernel(n_sq, n_sw, *refs),
        out_shape=(
            jax.ShapeDtypeStruct((n_sq, out_rows + 1, D // 2), jnp.bfloat16),
            jax.ShapeDtypeStruct((n_sw, out_rows + 1, FF // 2), jnp.bfloat16),
        ),
        in_specs=[pl.BlockSpec(memory_space=pl.ANY)],
        out_specs=(pl.BlockSpec(memory_space=pl.ANY), pl.BlockSpec(memory_space=pl.ANY)),
        scratch_shapes=[
            pltpu.SemaphoreType.DMA((wide_count,)),
            pltpu.SemaphoreType.DMA((2,)),
        ],
        compiler_params=pltpu.CompilerParams(collective_id=1, has_side_effects=True),
    )(with_scale_row(iterate.reshape(wide_count, out_rows, half), first_scale))

    inv_sq = inverse_of(square_order)
    inv_sw = inverse_of(swiglu_order)
    square_update = returned_sq[inv_sq][:, :out_rows]
    swiglu_update = returned_sw[inv_sw][:, :out_rows]

    slot_scales = jnp.concatenate([scale_of_row(returned_sq), scale_of_row(returned_sw)])
    slot_norms = 0.5 * jnp.log(slot_scales)
    matrix_slot = jnp.concatenate([inv_sq, n_sq + inv_sw])
    matrix_norms = slot_norms[matrix_slot]
    owner_norms = jnp.sum(jnp.where(owners == d, matrix_norms, 0.0)).reshape(1)

    vector_step, first_vector, second_vector = adamw_terms(
        vector_values, vector_grad, vector_first, vector_second
    )
    embed_rows = embed_values.shape[0]
    row_numbers = d * embed_rows + jnp.arange(embed_rows, dtype=jnp.int32)
    inside = (row_numbers[:, None] >= embed_ranges[None, :, 0]) & (
        row_numbers[:, None] < embed_ranges[None, :, 1]
    )
    row_live = jnp.sum(inside.astype(jnp.int32), axis=1) > 0
    direction, first_next, second_next = adamw_terms(
        embed_values, embed_grad, embed_first, embed_second
    )
    embed_step = jnp.where(row_live[:, None], direction, 0.0)
    first_embed = jnp.where(row_live[:, None], first_next, embed_first)
    second_embed = jnp.where(row_live[:, None], second_next, embed_second)
    return (
        square_next,
        swiglu_next,
        square_update,
        swiglu_update,
        owner_norms,
        vector_step,
        first_vector,
        second_vector,
        embed_step,
        first_embed,
        second_embed,
    )


def solution(mesh):
    placed = (
        P(None, ("dp", "tensor")),
        P(None, ("dp", "tensor")),
        P(None, ("dp", "tensor")),
        P(None, ("dp", "tensor")),
        P(),
        P(),
        P(),
        P(("dp", "tensor")),
        P(("dp", "tensor")),
        P(("dp", "tensor")),
        P(("dp", "tensor")),
        P("dp", "tensor"),
        P("dp", "tensor"),
        P("dp", "tensor"),
        P("dp", "tensor"),
        P(),
    )
    return jax.shard_map(
        local,
        mesh=mesh,
        in_specs=placed,
        out_specs=(
            P(None, ("dp", "tensor")),
            P(None, ("dp", "tensor")),
            P(None, "dp", "tensor"),
            P(None, "dp", "tensor"),
            P("dp"),
            P(("dp", "tensor")),
            P(("dp", "tensor")),
            P(("dp", "tensor")),
            P("dp", "tensor"),
            P("dp", "tensor"),
            P("dp", "tensor"),
        ),
        check_vma=False,
    )
```

```python
import math

import jax
import jax.numpy as jnp
from jax import lax
from jax.experimental import pallas as pl
from jax.experimental.pallas import tpu as pltpu
from jax.sharding import PartitionSpec as P

D = 1536
FF = 4096
NS_STEPS = 2
MESH = pl.DeviceIdType.MESH

QUINTIC_LINEAR = 3.4445
QUINTIC_CUBIC = -4.775
QUINTIC_FIFTH = 2.0315
MOMENTUM = 0.95
BIAS_FIRST = 1.0 - 0.9**10
BIAS_SECOND = 1.0 - 0.95**10


def momentum_terms(gradient, state):
    state_next = MOMENTUM * state + gradient
    return (state_next, (gradient + MOMENTUM * state_next).astype(jnp.bfloat16))


def adamw_terms(values, gradient, first, second):
    first_next = 0.9 * first + 0.1 * gradient
    second_next = 0.95 * second + 0.05 * gradient * gradient
    direction = (
        first_next / BIAS_FIRST / (jnp.sqrt(second_next / BIAS_SECOND) + 1e-08) + 0.1 * values
    )
    return (direction, first_next, second_next)


def inverse_of(order):
    count = order.shape[0]
    return jnp.zeros((count,), jnp.int32).at[order].set(jnp.arange(count, dtype=jnp.int32))


def device_barrier(n_dev, me, pairs):
    barrier = pltpu.get_barrier_semaphore()
    t = lax.axis_index("tensor")

    def signal(k, carry):
        target = lax.rem(me + k, n_dev)
        if pairs:
            device = (target // 2, lax.rem(target, 2))
        else:
            device = (target, t)
        pl.semaphore_signal(barrier, inc=1, device_id=device, device_id_type=MESH)
        return carry

    lax.fori_loop(1, n_dev, signal, 0)
    pl.semaphore_wait(barrier, n_dev - 1)


def scatter_kernel(n_sq, n_sw, sq_ref, sw_ref, zero_ref, out_ref, comb_sq, comb_sw, send_sem, recv_sem, pair_sem):
    del zero_ref
    d = lax.axis_index("dp")
    t = lax.axis_index("tensor")
    n_dev = lax.axis_size("dp") * 2
    n_slots = n_sq + n_sw
    me = d * 2 + t
    sq_w = comb_sq.shape[3]
    sw_w = comb_sw.shape[3]
    device_barrier(n_dev, me, True)

    other = 1 - t
    swap_sq = pltpu.make_async_remote_copy(
        src_ref=sq_ref.at[:, :, pl.ds(pl.multiple_of(other * sq_w, 128), sq_w)],
        dst_ref=comb_sq.at[:, t],
        send_sem=pair_sem.at[0],
        recv_sem=pair_sem.at[1],
        device_id=(d, other),
        device_id_type=MESH,
    )
    swap_sw = pltpu.make_async_remote_copy(
        src_ref=sw_ref.at[:, :, pl.ds(pl.multiple_of(other * sw_w, 128), sw_w)],
        dst_ref=comb_sw.at[:, t],
        send_sem=pair_sem.at[2],
        recv_sem=pair_sem.at[3],
        device_id=(d, other),
        device_id_type=MESH,
    )
    keep_sq = pltpu.make_async_copy(
        sq_ref.at[:, :, pl.ds(pl.multiple_of(t * sq_w, 128), sq_w)], comb_sq.at[:, t], pair_sem.at[4]
    )
    keep_sw = pltpu.make_async_copy(
        sw_ref.at[:, :, pl.ds(pl.multiple_of(t * sw_w, 128), sw_w)], comb_sw.at[:, t], pair_sem.at[5]
    )
    swap_sq.start()
    swap_sw.start()
    keep_sq.start()
    keep_sw.start()
    keep_sq.wait()
    keep_sw.wait()
    pltpu.make_async_copy(comb_sq.at[:, other], comb_sq.at[:, other], pair_sem.at[1]).wait()
    pltpu.make_async_copy(comb_sw.at[:, other], comb_sw.at[:, other], pair_sem.at[3]).wait()
    swap_sq.wait_send()
    swap_sw.wait_send()

    def sq_copy(g):
        return pltpu.make_async_remote_copy(
            src_ref=comb_sq.at[g],
            dst_ref=out_ref.at[d, :, :, pl.ds(0, sq_w)],
            send_sem=send_sem.at[g],
            recv_sem=recv_sem.at[0],
            device_id=(g, t),
            device_id_type=MESH,
        )

    def sw_copy(g):
        return pltpu.make_async_remote_copy(
            src_ref=comb_sw.at[g - n_sq],
            dst_ref=out_ref.at[d, :, :, pl.ds(0, sw_w)],
            send_sem=send_sem.at[g],
            recv_sem=recv_sem.at[0],
            device_id=(g, t),
            device_id_type=MESH,
        )

    def start(k, carry):
        g = lax.rem(k + d, n_slots)
        local = g == d

        @pl.when(local & (g < n_sq))
        def _():
            pltpu.make_async_copy(
                comb_sq.at[g], out_ref.at[d, :, :, pl.ds(0, sq_w)], recv_sem.at[0]
            ).start()

        @pl.when(local & (g >= n_sq))
        def _():
            pltpu.make_async_copy(
                comb_sw.at[g - n_sq], out_ref.at[d, :, :, pl.ds(0, sw_w)], recv_sem.at[0]
            ).start()

        @pl.when(jnp.logical_not(local) & (g < n_sq))
        def _():
            sq_copy(g).start()

        @pl.when(jnp.logical_not(local) & (g >= n_sq))
        def _():
            sw_copy(g).start()

        return carry

    lax.fori_loop(0, n_slots, start, 0)

    @pl.when(d < n_sq)
    def _():
        region = out_ref.at[:, :, :, pl.ds(0, sq_w)]
        pltpu.make_async_copy(region, region, recv_sem.at[0]).wait()

    @pl.when((d >= n_sq) & (d < n_slots))
    def _():
        region = out_ref.at[:, :, :, pl.ds(0, sw_w)]
        pltpu.make_async_copy(region, region, recv_sem.at[0]).wait()

    def wait(g, carry):
        @pl.when((g != d) & (g < n_sq))
        def _():
            sq_copy(g).wait_send()

        @pl.when((g != d) & (g >= n_sq))
        def _():
            sw_copy(g).wait_send()

        return carry

    lax.fori_loop(0, n_slots, wait, 0)


def gather_kernel(n_sq, n_sw, it_ref, osq_ref, osw_ref, send_sem, recv_sem):
    d = lax.axis_index("dp")
    t = lax.axis_index("tensor")
    n_dp = lax.axis_size("dp")
    device_barrier(n_dp, d, False)
    is_sq = d < n_sq
    is_sw = (d >= n_sq) & (d < n_sq + n_sw)
    sq_w = osq_ref.shape[2]
    sw_w = osw_ref.shape[2]
    j_sq = jnp.minimum(d, n_sq - 1)
    j_sw = jnp.clip(d - n_sq, 0, n_sw - 1)

    def sq_copy(r):
        return pltpu.make_async_remote_copy(
            src_ref=it_ref.at[r, :, pl.ds(0, sq_w)],
            dst_ref=osq_ref.at[j_sq],
            send_sem=send_sem.at[r],
            recv_sem=recv_sem.at[0],
            device_id=(r, t),
            device_id_type=MESH,
        )

    def sw_copy(r):
        return pltpu.make_async_remote_copy(
            src_ref=it_ref.at[r, :, pl.ds(0, sw_w)],
            dst_ref=osw_ref.at[j_sw],
            send_sem=send_sem.at[r],
            recv_sem=recv_sem.at[1],
            device_id=(r, t),
            device_id_type=MESH,
        )

    @pl.when(is_sq)
    def _():
        def start(k, carry):
            r = lax.rem(d + k, n_dp)

            @pl.when(r == d)
            def _():
                pltpu.make_async_copy(
                    it_ref.at[d, :, pl.ds(0, sq_w)], osq_ref.at[j_sq], recv_sem.at[0]
                ).start()

            @pl.when(r != d)
            def _():
                sq_copy(r).start()

            return carry

        lax.fori_loop(0, n_dp, start, 0)

    @pl.when(is_sw)
    def _():
        def start(k, carry):
            r = lax.rem(d + k, n_dp)

            @pl.when(r == d)
            def _():
                pltpu.make_async_copy(
                    it_ref.at[d, :, pl.ds(0, sw_w)], osw_ref.at[j_sw], recv_sem.at[1]
                ).start()

            @pl.when(r != d)
            def _():
                sw_copy(r).start()

            return carry

        lax.fori_loop(0, n_dp, start, 0)

    pltpu.make_async_copy(osq_ref, osq_ref, recv_sem.at[0]).wait()
    pltpu.make_async_copy(osw_ref, osw_ref, recv_sem.at[1]).wait()

    @pl.when(is_sq)
    def _():
        def wait(r, carry):
            @pl.when(r != d)
            def _():
                sq_copy(r).wait_send()

            return carry

        lax.fori_loop(0, n_dp, wait, 0)

    @pl.when(is_sw)
    def _():
        def wait(r, carry):
            @pl.when(r != d)
            def _():
                sw_copy(r).wait_send()

            return carry

        lax.fori_loop(0, n_dp, wait, 0)


def orthogonalize(arrived, factor):
    iterate = arrived
    first_scale = jnp.float32(1.0)
    for round_index in range(NS_STEPS):
        current = iterate
        gram_part = lax.psum_scatter(
            jnp.einsum("rc,sc->rs", current, current, preferred_element_type=jnp.float32),
            "tensor",
            scatter_dimension=0,
            tiled=True,
        )
        if round_index == 0:
            squares_total = lax.psum(jnp.sum(gram_part * gram_part), "tensor")
            gram_scale = jnp.sqrt(squares_total) + 1e-06
            first_scale = gram_scale
        else:
            gram_scale = jnp.float32(1.0)
        normed_part = (gram_part / gram_scale).astype(jnp.bfloat16)
        squared = jnp.dot(
            normed_part,
            lax.all_gather(normed_part, "tensor", axis=0, tiled=True),
            preferred_element_type=jnp.float32,
        )
        polynomial = (
            QUINTIC_CUBIC * normed_part.astype(jnp.float32) + QUINTIC_FIFTH * squared
        ).astype(jnp.bfloat16)
        product = jnp.dot(
            lax.all_gather(polynomial, "tensor", axis=0, tiled=True),
            current,
            preferred_element_type=jnp.float32,
        )
        mixed = (QUINTIC_LINEAR * current.astype(jnp.float32) + product) / jnp.sqrt(gram_scale)
        if round_index == NS_STEPS - 1:
            iterate = (factor * mixed).astype(jnp.bfloat16)
        else:
            iterate = mixed.astype(jnp.bfloat16)
    return (iterate, first_scale)


def with_scale_row(blocks, scale):
    high = scale.astype(jnp.bfloat16)
    low = (scale - high.astype(jnp.float32)).astype(jnp.bfloat16)
    lanes = lax.broadcasted_iota(jnp.int32, (blocks.shape[0], 1, blocks.shape[2]), 2)
    row = jnp.where(lanes == 0, high, jnp.where(lanes == 1, low, jnp.zeros((), jnp.bfloat16)))
    return jnp.concatenate([blocks, row], axis=1)


def scale_of_row(returned):
    row = returned[:, -1, :2].astype(jnp.float32)
    return row[:, 0] + row[:, 1]


def local(
    square_grad,
    square_state,
    swiglu_grad,
    swiglu_state,
    square_order,
    swiglu_order,
    owners,
    vector_values,
    vector_grad,
    vector_first,
    vector_second,
    embed_values,
    embed_grad,
    embed_first,
    embed_second,
    embed_ranges,
):
    wide_count = lax.axis_size("dp")
    n_dev = wide_count * 2
    d = lax.axis_index("dp")
    t = lax.axis_index("tensor")
    n_sq = square_grad.shape[0]
    n_sw = swiglu_grad.shape[0]
    flat_rows = D // n_dev
    out_rows = D // wide_count
    square_next, square_send = momentum_terms(square_grad, square_state)
    swiglu_next, swiglu_send = momentum_terms(swiglu_grad, swiglu_state)
    sq_pieces = square_send.reshape(n_sq, flat_rows, D)
    sw_pieces = swiglu_send.reshape(n_sw, flat_rows, FF)

    half = FF // 2
    arrived = pl.pallas_call(
        lambda *refs: scatter_kernel(n_sq, n_sw, *refs),
        out_shape=jax.ShapeDtypeStruct((wide_count, 2, flat_rows, half), jnp.bfloat16),
        in_specs=[pl.BlockSpec(memory_space=pl.ANY)] * 3,
        out_specs=pl.BlockSpec(memory_space=pl.ANY),
        scratch_shapes=[
            pltpu.VMEM((n_sq, 2, flat_rows, D // 2), jnp.bfloat16),
            pltpu.VMEM((n_sw, 2, flat_rows, half), jnp.bfloat16),
            pltpu.SemaphoreType.DMA((n_sq + n_sw,)),
            pltpu.SemaphoreType.DMA((1,)),
            pltpu.SemaphoreType.DMA((6,)),
        ],
        input_output_aliases={2: 0},
        compiler_params=pltpu.CompilerParams(collective_id=0, has_side_effects=True),
    )(sq_pieces, sw_pieces, jnp.zeros((wide_count, 2, flat_rows, half), jnp.bfloat16))

    is_sq = d < n_sq
    is_sw = (d >= n_sq) & (d < n_sq + n_sw)
    factor = jnp.where(is_sq, jnp.float32(math.sqrt(D)), jnp.float32(math.sqrt(FF)))
    iterate, first_scale = orthogonalize(arrived.reshape(D, half), factor)

    returned_sq, returned_sw = pl.pallas_call(
        lambda *refs: gather_kernel(n_sq, n_sw, *refs),
        out_shape=(
            jax.ShapeDtypeStruct((n_sq, out_rows + 1, D // 2), jnp.bfloat16),
            jax.ShapeDtypeStruct((n_sw, out_rows + 1, FF // 2), jnp.bfloat16),
        ),
        in_specs=[pl.BlockSpec(memory_space=pl.ANY)],
        out_specs=(pl.BlockSpec(memory_space=pl.ANY), pl.BlockSpec(memory_space=pl.ANY)),
        scratch_shapes=[
            pltpu.SemaphoreType.DMA((wide_count,)),
            pltpu.SemaphoreType.DMA((2,)),
        ],
        compiler_params=pltpu.CompilerParams(collective_id=1, has_side_effects=True),
    )(with_scale_row(iterate.reshape(wide_count, out_rows, half), first_scale))

    inv_sq = inverse_of(square_order)
    inv_sw = inverse_of(swiglu_order)
    square_update = returned_sq[inv_sq][:, :out_rows]
    swiglu_update = returned_sw[inv_sw][:, :out_rows]

    slot_scales = jnp.concatenate([scale_of_row(returned_sq), scale_of_row(returned_sw)])
    slot_norms = 0.5 * jnp.log(slot_scales)
    matrix_slot = jnp.concatenate([inv_sq, n_sq + inv_sw])
    matrix_norms = slot_norms[matrix_slot]
    owner_norms = jnp.sum(jnp.where(owners == d, matrix_norms, 0.0)).reshape(1)

    vector_step, first_vector, second_vector = adamw_terms(
        vector_values, vector_grad, vector_first, vector_second
    )
    embed_rows = embed_values.shape[0]
    row_numbers = d * embed_rows + jnp.arange(embed_rows, dtype=jnp.int32)
    inside = (row_numbers[:, None] >= embed_ranges[None, :, 0]) & (
        row_numbers[:, None] < embed_ranges[None, :, 1]
    )
    row_live = jnp.sum(inside.astype(jnp.int32), axis=1) > 0
    direction, first_next, second_next = adamw_terms(
        embed_values, embed_grad, embed_first, embed_second
    )
    embed_step = jnp.where(row_live[:, None], direction, 0.0)
    first_embed = jnp.where(row_live[:, None], first_next, embed_first)
    second_embed = jnp.where(row_live[:, None], second_next, embed_second)
    return (
        square_next,
        swiglu_next,
        square_update,
        swiglu_update,
        owner_norms,
        vector_step,
        first_vector,
        second_vector,
        embed_step,
        first_embed,
        second_embed,
    )


def solution(mesh):
    placed = (
        P(None, ("dp", "tensor")),
        P(None, ("dp", "tensor")),
        P(None, ("dp", "tensor")),
        P(None, ("dp", "tensor")),
        P(),
        P(),
        P(),
        P(("dp", "tensor")),
        P(("dp", "tensor")),
        P(("dp", "tensor")),
        P(("dp", "tensor")),
        P("dp", "tensor"),
        P("dp", "tensor"),
        P("dp", "tensor"),
        P("dp", "tensor"),
        P(),
    )
    return jax.shard_map(
        local,
        mesh=mesh,
        in_specs=placed,
        out_specs=(
            P(None, ("dp", "tensor")),
            P(None, ("dp", "tensor")),
            P(None, "dp", "tensor"),
            P(None, "dp", "tensor"),
            P("dp"),
            P(("dp", "tensor")),
            P(("dp", "tensor")),
            P(("dp", "tensor")),
            P("dp", "tensor"),
            P("dp", "tensor"),
            P("dp", "tensor"),
        ),
        check_vma=False,
    )
```

```python
import math

import jax
import jax.numpy as jnp
from jax import lax
from jax.experimental import pallas as pl
from jax.experimental.pallas import tpu as pltpu
from jax.sharding import PartitionSpec as P

D = 1536
FF = 4096
NS_STEPS = 2
MESH = pl.DeviceIdType.MESH

QUINTIC_LINEAR = 3.4445
QUINTIC_CUBIC = -4.775
QUINTIC_FIFTH = 2.0315
MOMENTUM = 0.95
BIAS_FIRST = 1.0 - 0.9**10
BIAS_SECOND = 1.0 - 0.95**10


def momentum_terms(gradient, state):
    state_next = MOMENTUM * state + gradient
    return (state_next, (gradient + MOMENTUM * state_next).astype(jnp.bfloat16))


def adamw_terms(values, gradient, first, second):
    first_next = 0.9 * first + 0.1 * gradient
    second_next = 0.95 * second + 0.05 * gradient * gradient
    direction = (
        first_next / BIAS_FIRST / (jnp.sqrt(second_next / BIAS_SECOND) + 1e-08) + 0.1 * values
    )
    return (direction, first_next, second_next)


def inverse_of(order):
    count = order.shape[0]
    return jnp.zeros((count,), jnp.int32).at[order].set(jnp.arange(count, dtype=jnp.int32))


def device_barrier(n_dev, me, pairs):
    barrier = pltpu.get_barrier_semaphore()
    t = lax.axis_index("tensor")

    def signal(k, carry):
        target = lax.rem(me + k, n_dev)
        if pairs:
            device = (target // 2, lax.rem(target, 2))
        else:
            device = (target, t)
        pl.semaphore_signal(barrier, inc=1, device_id=device, device_id_type=MESH)
        return carry

    lax.fori_loop(1, n_dev, signal, 0)
    pl.semaphore_wait(barrier, n_dev - 1)


def scatter_kernel(n_sq, n_sw, sq_ref, sw_ref, zero_ref, out_ref, comb_sq, comb_sw, send_sem, recv_sem, pair_sem):
    del zero_ref
    d = lax.axis_index("dp")
    t = lax.axis_index("tensor")
    n_dev = lax.axis_size("dp") * 2
    n_slots = n_sq + n_sw
    me = d * 2 + t
    sq_w = comb_sq.shape[3]
    sw_w = comb_sw.shape[3]
    device_barrier(n_dev, me, True)

    other = 1 - t
    swap_sq = pltpu.make_async_remote_copy(
        src_ref=sq_ref.at[:, :, pl.ds(pl.multiple_of(other * sq_w, 128), sq_w)],
        dst_ref=comb_sq.at[:, t],
        send_sem=pair_sem.at[0],
        recv_sem=pair_sem.at[1],
        device_id=(d, other),
        device_id_type=MESH,
    )
    swap_sw = pltpu.make_async_remote_copy(
        src_ref=sw_ref.at[:, :, pl.ds(pl.multiple_of(other * sw_w, 128), sw_w)],
        dst_ref=comb_sw.at[:, t],
        send_sem=pair_sem.at[2],
        recv_sem=pair_sem.at[3],
        device_id=(d, other),
        device_id_type=MESH,
    )
    keep_sq = pltpu.make_async_copy(
        sq_ref.at[:, :, pl.ds(pl.multiple_of(t * sq_w, 128), sq_w)], comb_sq.at[:, t], pair_sem.at[4]
    )
    keep_sw = pltpu.make_async_copy(
        sw_ref.at[:, :, pl.ds(pl.multiple_of(t * sw_w, 128), sw_w)], comb_sw.at[:, t], pair_sem.at[5]
    )
    swap_sq.start()
    swap_sw.start()
    keep_sq.start()
    keep_sw.start()
    keep_sq.wait()
    keep_sw.wait()
    pltpu.make_async_copy(comb_sq.at[:, other], comb_sq.at[:, other], pair_sem.at[1]).wait()
    pltpu.make_async_copy(comb_sw.at[:, other], comb_sw.at[:, other], pair_sem.at[3]).wait()
    swap_sq.wait_send()
    swap_sw.wait_send()

    def sq_copy(g):
        return pltpu.make_async_remote_copy(
            src_ref=comb_sq.at[g],
            dst_ref=out_ref.at[d, :, :, pl.ds(0, sq_w)],
            send_sem=send_sem.at[g],
            recv_sem=recv_sem.at[0],
            device_id=(g, t),
            device_id_type=MESH,
        )

    def sw_copy(g):
        return pltpu.make_async_remote_copy(
            src_ref=comb_sw.at[g - n_sq],
            dst_ref=out_ref.at[d, :, :, pl.ds(0, sw_w)],
            send_sem=send_sem.at[g],
            recv_sem=recv_sem.at[0],
            device_id=(g, t),
            device_id_type=MESH,
        )

    def start(k, carry):
        g = lax.rem(k + d, n_slots)
        local = g == d

        @pl.when(local & (g < n_sq))
        def _():
            pltpu.make_async_copy(
                comb_sq.at[g], out_ref.at[d, :, :, pl.ds(0, sq_w)], recv_sem.at[0]
            ).start()

        @pl.when(local & (g >= n_sq))
        def _():
            pltpu.make_async_copy(
                comb_sw.at[g - n_sq], out_ref.at[d, :, :, pl.ds(0, sw_w)], recv_sem.at[0]
            ).start()

        @pl.when(jnp.logical_not(local) & (g < n_sq))
        def _():
            sq_copy(g).start()

        @pl.when(jnp.logical_not(local) & (g >= n_sq))
        def _():
            sw_copy(g).start()

        return carry

    lax.fori_loop(0, n_slots, start, 0)

    @pl.when(d < n_sq)
    def _():
        region = out_ref.at[:, :, :, pl.ds(0, sq_w)]
        pltpu.make_async_copy(region, region, recv_sem.at[0]).wait()

    @pl.when((d >= n_sq) & (d < n_slots))
    def _():
        region = out_ref.at[:, :, :, pl.ds(0, sw_w)]
        pltpu.make_async_copy(region, region, recv_sem.at[0]).wait()

    def wait(g, carry):
        @pl.when((g != d) & (g < n_sq))
        def _():
            sq_copy(g).wait_send()

        @pl.when((g != d) & (g >= n_sq))
        def _():
            sw_copy(g).wait_send()

        return carry

    lax.fori_loop(0, n_slots, wait, 0)


def gather_kernel(n_sq, n_sw, it_ref, osq_ref, osw_ref, send_sem, recv_sem):
    d = lax.axis_index("dp")
    t = lax.axis_index("tensor")
    n_dp = lax.axis_size("dp")
    device_barrier(n_dp, d, False)
    is_sq = d < n_sq
    is_sw = (d >= n_sq) & (d < n_sq + n_sw)
    sq_w = osq_ref.shape[2]
    sw_w = osw_ref.shape[2]
    j_sq = jnp.minimum(d, n_sq - 1)
    j_sw = jnp.clip(d - n_sq, 0, n_sw - 1)

    def sq_copy(r):
        return pltpu.make_async_remote_copy(
            src_ref=it_ref.at[r, :, pl.ds(0, sq_w)],
            dst_ref=osq_ref.at[j_sq],
            send_sem=send_sem.at[r],
            recv_sem=recv_sem.at[0],
            device_id=(r, t),
            device_id_type=MESH,
        )

    def sw_copy(r):
        return pltpu.make_async_remote_copy(
            src_ref=it_ref.at[r, :, pl.ds(0, sw_w)],
            dst_ref=osw_ref.at[j_sw],
            send_sem=send_sem.at[r],
            recv_sem=recv_sem.at[1],
            device_id=(r, t),
            device_id_type=MESH,
        )

    @pl.when(is_sq)
    def _():
        def start(k, carry):
            r = lax.rem(d + k, n_dp)

            @pl.when(r == d)
            def _():
                pltpu.make_async_copy(
                    it_ref.at[d, :, pl.ds(0, sq_w)], osq_ref.at[j_sq], recv_sem.at[0]
                ).start()

            @pl.when(r != d)
            def _():
                sq_copy(r).start()

            return carry

        lax.fori_loop(0, n_dp, start, 0)

    @pl.when(is_sw)
    def _():
        def start(k, carry):
            r = lax.rem(d + k, n_dp)

            @pl.when(r == d)
            def _():
                pltpu.make_async_copy(
                    it_ref.at[d, :, pl.ds(0, sw_w)], osw_ref.at[j_sw], recv_sem.at[1]
                ).start()

            @pl.when(r != d)
            def _():
                sw_copy(r).start()

            return carry

        lax.fori_loop(0, n_dp, start, 0)

    pltpu.make_async_copy(osq_ref, osq_ref, recv_sem.at[0]).wait()
    pltpu.make_async_copy(osw_ref, osw_ref, recv_sem.at[1]).wait()

    @pl.when(is_sq)
    def _():
        def wait(r, carry):
            @pl.when(r != d)
            def _():
                sq_copy(r).wait_send()

            return carry

        lax.fori_loop(0, n_dp, wait, 0)

    @pl.when(is_sw)
    def _():
        def wait(r, carry):
            @pl.when(r != d)
            def _():
                sw_copy(r).wait_send()

            return carry

        lax.fori_loop(0, n_dp, wait, 0)


def swap_halves(x):
    return lax.ppermute(x, "tensor", perm=[(0, 1), (1, 0)])


def orthogonalize(arrived, factor):
    t = lax.axis_index("tensor")
    rows = arrived.shape[0] // 2
    mine = pl.multiple_of(t * rows, rows)
    theirs = pl.multiple_of((1 - t) * rows, rows)
    iterate = arrived
    first_scale = jnp.float32(1.0)
    for round_index in range(NS_STEPS):
        current = iterate
        their_rows = lax.dynamic_slice_in_dim(current, theirs, rows, 0)
        my_rows = lax.dynamic_slice_in_dim(current, mine, rows, 0)
        sent = swap_halves(
            jnp.einsum("rc,sc->rs", their_rows, current, preferred_element_type=jnp.float32)
        )
        kept = lax.optimization_barrier(
            jnp.einsum("rc,sc->rs", my_rows, current, preferred_element_type=jnp.float32)
        )
        gram_part = kept + sent
        if round_index == 0:
            squares_total = lax.psum(jnp.sum(gram_part * gram_part), "tensor")
            gram_scale = jnp.sqrt(squares_total) + 1e-06
            first_scale = gram_scale
        else:
            gram_scale = jnp.float32(1.0)
        normed_part = (gram_part / gram_scale).astype(jnp.bfloat16)
        normed_other = swap_halves(normed_part)
        squared = lax.optimization_barrier(
            jnp.dot(
                lax.dynamic_slice_in_dim(normed_part, mine, rows, 1),
                normed_part,
                preferred_element_type=jnp.float32,
            )
        ) + jnp.dot(
            lax.dynamic_slice_in_dim(normed_part, theirs, rows, 1),
            normed_other,
            preferred_element_type=jnp.float32,
        )
        polynomial = (
            QUINTIC_CUBIC * normed_part.astype(jnp.float32) + QUINTIC_FIFTH * squared
        ).astype(jnp.bfloat16)
        poly_other = swap_halves(polynomial)
        product_mine = lax.optimization_barrier(
            jnp.dot(polynomial, current, preferred_element_type=jnp.float32)
        )
        product_other = jnp.dot(poly_other, current, preferred_element_type=jnp.float32)
        first = t == 0
        product = jnp.concatenate(
            [
                jnp.where(first, product_mine, product_other),
                jnp.where(first, product_other, product_mine),
            ],
            axis=0,
        )
        mixed = (QUINTIC_LINEAR * current.astype(jnp.float32) + product) / jnp.sqrt(gram_scale)
        if round_index == NS_STEPS - 1:
            iterate = (factor * mixed).astype(jnp.bfloat16)
        else:
            iterate = mixed.astype(jnp.bfloat16)
    return (iterate, first_scale)


def with_scale_row(blocks, scale):
    high = scale.astype(jnp.bfloat16)
    low = (scale - high.astype(jnp.float32)).astype(jnp.bfloat16)
    lanes = lax.broadcasted_iota(jnp.int32, (blocks.shape[0], 1, blocks.shape[2]), 2)
    row = jnp.where(lanes == 0, high, jnp.where(lanes == 1, low, jnp.zeros((), jnp.bfloat16)))
    return jnp.concatenate([blocks, row], axis=1)


def scale_of_row(returned):
    row = returned[:, -1, :2].astype(jnp.float32)
    return row[:, 0] + row[:, 1]


def local(
    square_grad,
    square_state,
    swiglu_grad,
    swiglu_state,
    square_order,
    swiglu_order,
    owners,
    vector_values,
    vector_grad,
    vector_first,
    vector_second,
    embed_values,
    embed_grad,
    embed_first,
    embed_second,
    embed_ranges,
):
    wide_count = lax.axis_size("dp")
    n_dev = wide_count * 2
    d = lax.axis_index("dp")
    t = lax.axis_index("tensor")
    n_sq = square_grad.shape[0]
    n_sw = swiglu_grad.shape[0]
    flat_rows = D // n_dev
    out_rows = D // wide_count
    square_next, square_send = momentum_terms(square_grad, square_state)
    swiglu_next, swiglu_send = momentum_terms(swiglu_grad, swiglu_state)
    sq_pieces = square_send.reshape(n_sq, flat_rows, D)
    sw_pieces = swiglu_send.reshape(n_sw, flat_rows, FF)

    half = FF // 2
    arrived = pl.pallas_call(
        lambda *refs: scatter_kernel(n_sq, n_sw, *refs),
        out_shape=jax.ShapeDtypeStruct((wide_count, 2, flat_rows, half), jnp.bfloat16),
        in_specs=[pl.BlockSpec(memory_space=pl.ANY)] * 3,
        out_specs=pl.BlockSpec(memory_space=pl.ANY),
        scratch_shapes=[
            pltpu.VMEM((n_sq, 2, flat_rows, D // 2), jnp.bfloat16),
            pltpu.VMEM((n_sw, 2, flat_rows, half), jnp.bfloat16),
            pltpu.SemaphoreType.DMA((n_sq + n_sw,)),
            pltpu.SemaphoreType.DMA((1,)),
            pltpu.SemaphoreType.DMA((6,)),
        ],
        input_output_aliases={2: 0},
        compiler_params=pltpu.CompilerParams(collective_id=0, has_side_effects=True),
    )(sq_pieces, sw_pieces, jnp.zeros((wide_count, 2, flat_rows, half), jnp.bfloat16))

    is_sq = d < n_sq
    is_sw = (d >= n_sq) & (d < n_sq + n_sw)
    factor = jnp.where(is_sq, jnp.float32(math.sqrt(D)), jnp.float32(math.sqrt(FF)))
    iterate, first_scale = orthogonalize(arrived.reshape(D, half), factor)

    returned_sq, returned_sw = pl.pallas_call(
        lambda *refs: gather_kernel(n_sq, n_sw, *refs),
        out_shape=(
            jax.ShapeDtypeStruct((n_sq, out_rows + 1, D // 2), jnp.bfloat16),
            jax.ShapeDtypeStruct((n_sw, out_rows + 1, FF // 2), jnp.bfloat16),
        ),
        in_specs=[pl.BlockSpec(memory_space=pl.ANY)],
        out_specs=(pl.BlockSpec(memory_space=pl.ANY), pl.BlockSpec(memory_space=pl.ANY)),
        scratch_shapes=[
            pltpu.SemaphoreType.DMA((wide_count,)),
            pltpu.SemaphoreType.DMA((2,)),
        ],
        compiler_params=pltpu.CompilerParams(collective_id=1, has_side_effects=True),
    )(with_scale_row(iterate.reshape(wide_count, out_rows, half), first_scale))

    inv_sq = inverse_of(square_order)
    inv_sw = inverse_of(swiglu_order)
    square_update = returned_sq[inv_sq][:, :out_rows]
    swiglu_update = returned_sw[inv_sw][:, :out_rows]

    slot_scales = jnp.concatenate([scale_of_row(returned_sq), scale_of_row(returned_sw)])
    slot_norms = 0.5 * jnp.log(slot_scales)
    matrix_slot = jnp.concatenate([inv_sq, n_sq + inv_sw])
    matrix_norms = slot_norms[matrix_slot]
    owner_norms = jnp.sum(jnp.where(owners == d, matrix_norms, 0.0)).reshape(1)

    vector_step, first_vector, second_vector = adamw_terms(
        vector_values, vector_grad, vector_first, vector_second
    )
    embed_rows = embed_values.shape[0]
    row_numbers = d * embed_rows + jnp.arange(embed_rows, dtype=jnp.int32)
    inside = (row_numbers[:, None] >= embed_ranges[None, :, 0]) & (
        row_numbers[:, None] < embed_ranges[None, :, 1]
    )
    row_live = jnp.sum(inside.astype(jnp.int32), axis=1) > 0
    direction, first_next, second_next = adamw_terms(
        embed_values, embed_grad, embed_first, embed_second
    )
    embed_step = jnp.where(row_live[:, None], direction, 0.0)
    first_embed = jnp.where(row_live[:, None], first_next, embed_first)
    second_embed = jnp.where(row_live[:, None], second_next, embed_second)
    return (
        square_next,
        swiglu_next,
        square_update,
        swiglu_update,
        owner_norms,
        vector_step,
        first_vector,
        second_vector,
        embed_step,
        first_embed,
        second_embed,
    )


def solution(mesh):
    placed = (
        P(None, ("dp", "tensor")),
        P(None, ("dp", "tensor")),
        P(None, ("dp", "tensor")),
        P(None, ("dp", "tensor")),
        P(),
        P(),
        P(),
        P(("dp", "tensor")),
        P(("dp", "tensor")),
        P(("dp", "tensor")),
        P(("dp", "tensor")),
        P("dp", "tensor"),
        P("dp", "tensor"),
        P("dp", "tensor"),
        P("dp", "tensor"),
        P(),
    )
    return jax.shard_map(
        local,
        mesh=mesh,
        in_specs=placed,
        out_specs=(
            P(None, ("dp", "tensor")),
            P(None, ("dp", "tensor")),
            P(None, "dp", "tensor"),
            P(None, "dp", "tensor"),
            P("dp"),
            P(("dp", "tensor")),
            P(("dp", "tensor")),
            P(("dp", "tensor")),
            P("dp", "tensor"),
            P("dp", "tensor"),
            P("dp", "tensor"),
        ),
        check_vma=False,
    )
```

```python
import math

import jax
import jax.numpy as jnp
from jax import lax
from jax.experimental import pallas as pl
from jax.experimental.pallas import tpu as pltpu
from jax.sharding import PartitionSpec as P

D = 1536
FF = 4096
NS_STEPS = 2
MESH = pl.DeviceIdType.MESH

QUINTIC_LINEAR = 3.4445
QUINTIC_CUBIC = -4.775
QUINTIC_FIFTH = 2.0315
MOMENTUM = 0.95
BIAS_FIRST = 1.0 - 0.9**10
BIAS_SECOND = 1.0 - 0.95**10


def momentum_terms(gradient, state):
    state_next = MOMENTUM * state + gradient
    return (state_next, (gradient + MOMENTUM * state_next).astype(jnp.bfloat16))


def adamw_terms(values, gradient, first, second):
    first_next = 0.9 * first + 0.1 * gradient
    second_next = 0.95 * second + 0.05 * gradient * gradient
    direction = (
        first_next / BIAS_FIRST / (jnp.sqrt(second_next / BIAS_SECOND) + 1e-08) + 0.1 * values
    )
    return (direction, first_next, second_next)


def inverse_of(order):
    count = order.shape[0]
    return jnp.zeros((count,), jnp.int32).at[order].set(jnp.arange(count, dtype=jnp.int32))


def device_barrier(n_dev, me, pairs):
    barrier = pltpu.get_barrier_semaphore()
    t = lax.axis_index("tensor")

    def signal(k, carry):
        target = lax.rem(me + k, n_dev)
        if pairs:
            device = (target // 2, lax.rem(target, 2))
        else:
            device = (target, t)
        pl.semaphore_signal(barrier, inc=1, device_id=device, device_id_type=MESH)
        return carry

    lax.fori_loop(1, n_dev, signal, 0)
    pl.semaphore_wait(barrier, n_dev - 1)


def scatter_kernel(n_sq, n_sw, sq_ref, sw_ref, zero_ref, out_ref, comb_sq, comb_sw, send_sem, recv_sem, pair_sem):
    del zero_ref
    d = lax.axis_index("dp")
    t = lax.axis_index("tensor")
    n_dev = lax.axis_size("dp") * 2
    n_slots = n_sq + n_sw
    me = d * 2 + t
    sq_w = comb_sq.shape[3]
    sw_w = comb_sw.shape[3]
    device_barrier(n_dev, me, True)

    other = 1 - t
    swap_sq = pltpu.make_async_remote_copy(
        src_ref=sq_ref.at[:, :, pl.ds(pl.multiple_of(other * sq_w, 128), sq_w)],
        dst_ref=comb_sq.at[:, t],
        send_sem=pair_sem.at[0],
        recv_sem=pair_sem.at[1],
        device_id=(d, other),
        device_id_type=MESH,
    )
    swap_sw = pltpu.make_async_remote_copy(
        src_ref=sw_ref.at[:, :, pl.ds(pl.multiple_of(other * sw_w, 128), sw_w)],
        dst_ref=comb_sw.at[:, t],
        send_sem=pair_sem.at[2],
        recv_sem=pair_sem.at[3],
        device_id=(d, other),
        device_id_type=MESH,
    )
    keep_sq = pltpu.make_async_copy(
        sq_ref.at[:, :, pl.ds(pl.multiple_of(t * sq_w, 128), sq_w)], comb_sq.at[:, t], pair_sem.at[4]
    )
    keep_sw = pltpu.make_async_copy(
        sw_ref.at[:, :, pl.ds(pl.multiple_of(t * sw_w, 128), sw_w)], comb_sw.at[:, t], pair_sem.at[5]
    )
    swap_sq.start()
    swap_sw.start()
    keep_sq.start()
    keep_sw.start()
    keep_sq.wait()
    keep_sw.wait()
    pltpu.make_async_copy(comb_sq.at[:, other], comb_sq.at[:, other], pair_sem.at[1]).wait()
    pltpu.make_async_copy(comb_sw.at[:, other], comb_sw.at[:, other], pair_sem.at[3]).wait()
    swap_sq.wait_send()
    swap_sw.wait_send()

    def sq_copy(g):
        return pltpu.make_async_remote_copy(
            src_ref=comb_sq.at[g],
            dst_ref=out_ref.at[d, :, :, pl.ds(0, sq_w)],
            send_sem=send_sem.at[g],
            recv_sem=recv_sem.at[0],
            device_id=(g, t),
            device_id_type=MESH,
        )

    def sw_copy(g):
        return pltpu.make_async_remote_copy(
            src_ref=comb_sw.at[g - n_sq],
            dst_ref=out_ref.at[d, :, :, pl.ds(0, sw_w)],
            send_sem=send_sem.at[g],
            recv_sem=recv_sem.at[0],
            device_id=(g, t),
            device_id_type=MESH,
        )

    def start(k, carry):
        g = lax.rem(k + d, n_slots)
        local = g == d

        @pl.when(local & (g < n_sq))
        def _():
            pltpu.make_async_copy(
                comb_sq.at[g], out_ref.at[d, :, :, pl.ds(0, sq_w)], recv_sem.at[0]
            ).start()

        @pl.when(local & (g >= n_sq))
        def _():
            pltpu.make_async_copy(
                comb_sw.at[g - n_sq], out_ref.at[d, :, :, pl.ds(0, sw_w)], recv_sem.at[0]
            ).start()

        @pl.when(jnp.logical_not(local) & (g < n_sq))
        def _():
            sq_copy(g).start()

        @pl.when(jnp.logical_not(local) & (g >= n_sq))
        def _():
            sw_copy(g).start()

        return carry

    lax.fori_loop(0, n_slots, start, 0)

    @pl.when(d < n_sq)
    def _():
        region = out_ref.at[:, :, :, pl.ds(0, sq_w)]
        pltpu.make_async_copy(region, region, recv_sem.at[0]).wait()

    @pl.when((d >= n_sq) & (d < n_slots))
    def _():
        region = out_ref.at[:, :, :, pl.ds(0, sw_w)]
        pltpu.make_async_copy(region, region, recv_sem.at[0]).wait()

    def wait(g, carry):
        @pl.when((g != d) & (g < n_sq))
        def _():
            sq_copy(g).wait_send()

        @pl.when((g != d) & (g >= n_sq))
        def _():
            sw_copy(g).wait_send()

        return carry

    lax.fori_loop(0, n_slots, wait, 0)


def gather_kernel(n_sq, n_sw, it_ref, osq_ref, osw_ref, send_sem, recv_sem):
    d = lax.axis_index("dp")
    t = lax.axis_index("tensor")
    n_dp = lax.axis_size("dp")
    device_barrier(n_dp, d, False)
    is_sq = d < n_sq
    is_sw = (d >= n_sq) & (d < n_sq + n_sw)
    sq_w = osq_ref.shape[2]
    sw_w = osw_ref.shape[2]
    j_sq = jnp.minimum(d, n_sq - 1)
    j_sw = jnp.clip(d - n_sq, 0, n_sw - 1)

    def sq_copy(r):
        return pltpu.make_async_remote_copy(
            src_ref=it_ref.at[r, :, pl.ds(0, sq_w)],
            dst_ref=osq_ref.at[j_sq],
            send_sem=send_sem.at[r],
            recv_sem=recv_sem.at[0],
            device_id=(r, t),
            device_id_type=MESH,
        )

    def sw_copy(r):
        return pltpu.make_async_remote_copy(
            src_ref=it_ref.at[r, :, pl.ds(0, sw_w)],
            dst_ref=osw_ref.at[j_sw],
            send_sem=send_sem.at[r],
            recv_sem=recv_sem.at[1],
            device_id=(r, t),
            device_id_type=MESH,
        )

    @pl.when(is_sq)
    def _():
        def start(k, carry):
            r = lax.rem(d + k, n_dp)

            @pl.when(r == d)
            def _():
                pltpu.make_async_copy(
                    it_ref.at[d, :, pl.ds(0, sq_w)], osq_ref.at[j_sq], recv_sem.at[0]
                ).start()

            @pl.when(r != d)
            def _():
                sq_copy(r).start()

            return carry

        lax.fori_loop(0, n_dp, start, 0)

    @pl.when(is_sw)
    def _():
        def start(k, carry):
            r = lax.rem(d + k, n_dp)

            @pl.when(r == d)
            def _():
                pltpu.make_async_copy(
                    it_ref.at[d, :, pl.ds(0, sw_w)], osw_ref.at[j_sw], recv_sem.at[1]
                ).start()

            @pl.when(r != d)
            def _():
                sw_copy(r).start()

            return carry

        lax.fori_loop(0, n_dp, start, 0)

    pltpu.make_async_copy(osq_ref, osq_ref, recv_sem.at[0]).wait()
    pltpu.make_async_copy(osw_ref, osw_ref, recv_sem.at[1]).wait()

    @pl.when(is_sq)
    def _():
        def wait(r, carry):
            @pl.when(r != d)
            def _():
                sq_copy(r).wait_send()

            return carry

        lax.fori_loop(0, n_dp, wait, 0)

    @pl.when(is_sw)
    def _():
        def wait(r, carry):
            @pl.when(r != d)
            def _():
                sw_copy(r).wait_send()

            return carry

        lax.fori_loop(0, n_dp, wait, 0)


def swap_halves(x):
    return lax.ppermute(x, "tensor", perm=[(0, 1), (1, 0)])


def orthogonalize(arrived, factor):
    t = lax.axis_index("tensor")
    rows = arrived.shape[0] // 2
    mine = pl.multiple_of(t * rows, rows)
    theirs = pl.multiple_of((1 - t) * rows, rows)
    iterate = arrived
    first_scale = jnp.float32(1.0)
    for round_index in range(NS_STEPS):
        current = iterate
        their_rows = lax.dynamic_slice_in_dim(current, theirs, rows, 0)
        my_rows = lax.dynamic_slice_in_dim(current, mine, rows, 0)
        sent = swap_halves(
            jnp.einsum("rc,sc->rs", their_rows, current, preferred_element_type=jnp.float32)
        )
        kept = lax.optimization_barrier(
            jnp.einsum("rc,sc->rs", my_rows, current, preferred_element_type=jnp.float32)
        )
        gram_part = kept + sent
        if round_index == 0:
            squares_total = lax.psum(jnp.sum(gram_part * gram_part), "tensor")
            gram_scale = jnp.sqrt(squares_total) + 1e-06
            first_scale = gram_scale
        else:
            gram_scale = jnp.float32(1.0)
        normed_part = (gram_part / gram_scale).astype(jnp.bfloat16)
        normed_other = swap_halves(normed_part)
        squared = lax.optimization_barrier(
            jnp.dot(
                lax.dynamic_slice_in_dim(normed_part, mine, rows, 1),
                normed_part,
                preferred_element_type=jnp.float32,
            )
        ) + jnp.dot(
            lax.dynamic_slice_in_dim(normed_part, theirs, rows, 1),
            normed_other,
            preferred_element_type=jnp.float32,
        )
        polynomial = (
            QUINTIC_CUBIC * normed_part.astype(jnp.float32) + QUINTIC_FIFTH * squared
        ).astype(jnp.bfloat16)
        poly_other = swap_halves(polynomial)
        product_mine = lax.optimization_barrier(
            jnp.dot(polynomial, current, preferred_element_type=jnp.float32)
        )
        product_other = jnp.dot(poly_other, current, preferred_element_type=jnp.float32)
        scale_root = jnp.sqrt(gram_scale)
        halves = []
        for rows_here, product_here in ((my_rows, product_mine), (their_rows, product_other)):
            mixed = (QUINTIC_LINEAR * rows_here.astype(jnp.float32) + product_here) / scale_root
            if round_index == NS_STEPS - 1:
                mixed = factor * mixed
            halves.append(mixed.astype(jnp.bfloat16))
        iterate = lax.dynamic_update_slice_in_dim(
            lax.dynamic_update_slice_in_dim(jnp.zeros_like(current), halves[0], mine, 0),
            halves[1],
            theirs,
            0,
        )
    return (iterate, first_scale)


def with_scale_row(blocks, scale):
    high = scale.astype(jnp.bfloat16)
    low = (scale - high.astype(jnp.float32)).astype(jnp.bfloat16)
    lanes = lax.broadcasted_iota(jnp.int32, (blocks.shape[0], 1, blocks.shape[2]), 2)
    row = jnp.where(lanes == 0, high, jnp.where(lanes == 1, low, jnp.zeros((), jnp.bfloat16)))
    return jnp.concatenate([blocks, row], axis=1)


def scale_of_row(returned):
    row = returned[:, -1, :2].astype(jnp.float32)
    return row[:, 0] + row[:, 1]


def local(
    square_grad,
    square_state,
    swiglu_grad,
    swiglu_state,
    square_order,
    swiglu_order,
    owners,
    vector_values,
    vector_grad,
    vector_first,
    vector_second,
    embed_values,
    embed_grad,
    embed_first,
    embed_second,
    embed_ranges,
):
    wide_count = lax.axis_size("dp")
    n_dev = wide_count * 2
    d = lax.axis_index("dp")
    t = lax.axis_index("tensor")
    n_sq = square_grad.shape[0]
    n_sw = swiglu_grad.shape[0]
    flat_rows = D // n_dev
    out_rows = D // wide_count
    square_next, square_send = momentum_terms(square_grad, square_state)
    swiglu_next, swiglu_send = momentum_terms(swiglu_grad, swiglu_state)
    sq_pieces = square_send.reshape(n_sq, flat_rows, D)
    sw_pieces = swiglu_send.reshape(n_sw, flat_rows, FF)

    half = FF // 2
    arrived = pl.pallas_call(
        lambda *refs: scatter_kernel(n_sq, n_sw, *refs),
        out_shape=jax.ShapeDtypeStruct((wide_count, 2, flat_rows, half), jnp.bfloat16),
        in_specs=[pl.BlockSpec(memory_space=pl.ANY)] * 3,
        out_specs=pl.BlockSpec(memory_space=pl.ANY),
        scratch_shapes=[
            pltpu.VMEM((n_sq, 2, flat_rows, D // 2), jnp.bfloat16),
            pltpu.VMEM((n_sw, 2, flat_rows, half), jnp.bfloat16),
            pltpu.SemaphoreType.DMA((n_sq + n_sw,)),
            pltpu.SemaphoreType.DMA((1,)),
            pltpu.SemaphoreType.DMA((6,)),
        ],
        input_output_aliases={2: 0},
        compiler_params=pltpu.CompilerParams(collective_id=0, has_side_effects=True),
    )(sq_pieces, sw_pieces, jnp.zeros((wide_count, 2, flat_rows, half), jnp.bfloat16))

    is_sq = d < n_sq
    is_sw = (d >= n_sq) & (d < n_sq + n_sw)
    factor = jnp.where(is_sq, jnp.float32(math.sqrt(D)), jnp.float32(math.sqrt(FF)))
    iterate, first_scale = orthogonalize(arrived.reshape(D, half), factor)

    returned_sq, returned_sw = pl.pallas_call(
        lambda *refs: gather_kernel(n_sq, n_sw, *refs),
        out_shape=(
            jax.ShapeDtypeStruct((n_sq, out_rows + 1, D // 2), jnp.bfloat16),
            jax.ShapeDtypeStruct((n_sw, out_rows + 1, FF // 2), jnp.bfloat16),
        ),
        in_specs=[pl.BlockSpec(memory_space=pl.ANY)],
        out_specs=(pl.BlockSpec(memory_space=pl.ANY), pl.BlockSpec(memory_space=pl.ANY)),
        scratch_shapes=[
            pltpu.SemaphoreType.DMA((wide_count,)),
            pltpu.SemaphoreType.DMA((2,)),
        ],
        compiler_params=pltpu.CompilerParams(collective_id=1, has_side_effects=True),
    )(with_scale_row(iterate.reshape(wide_count, out_rows, half), first_scale))

    inv_sq = inverse_of(square_order)
    inv_sw = inverse_of(swiglu_order)
    square_update = returned_sq[inv_sq][:, :out_rows]
    swiglu_update = returned_sw[inv_sw][:, :out_rows]

    slot_scales = jnp.concatenate([scale_of_row(returned_sq), scale_of_row(returned_sw)])
    slot_norms = 0.5 * jnp.log(slot_scales)
    matrix_slot = jnp.concatenate([inv_sq, n_sq + inv_sw])
    matrix_norms = slot_norms[matrix_slot]
    owner_norms = jnp.sum(jnp.where(owners == d, matrix_norms, 0.0)).reshape(1)

    vector_step, first_vector, second_vector = adamw_terms(
        vector_values, vector_grad, vector_first, vector_second
    )
    embed_rows = embed_values.shape[0]
    row_numbers = d * embed_rows + jnp.arange(embed_rows, dtype=jnp.int32)
    inside = (row_numbers[:, None] >= embed_ranges[None, :, 0]) & (
        row_numbers[:, None] < embed_ranges[None, :, 1]
    )
    row_live = jnp.sum(inside.astype(jnp.int32), axis=1) > 0
    direction, first_next, second_next = adamw_terms(
        embed_values, embed_grad, embed_first, embed_second
    )
    embed_step = jnp.where(row_live[:, None], direction, 0.0)
    first_embed = jnp.where(row_live[:, None], first_next, embed_first)
    second_embed = jnp.where(row_live[:, None], second_next, embed_second)
    return (
        square_next,
        swiglu_next,
        square_update,
        swiglu_update,
        owner_norms,
        vector_step,
        first_vector,
        second_vector,
        embed_step,
        first_embed,
        second_embed,
    )


def solution(mesh):
    placed = (
        P(None, ("dp", "tensor")),
        P(None, ("dp", "tensor")),
        P(None, ("dp", "tensor")),
        P(None, ("dp", "tensor")),
        P(),
        P(),
        P(),
        P(("dp", "tensor")),
        P(("dp", "tensor")),
        P(("dp", "tensor")),
        P(("dp", "tensor")),
        P("dp", "tensor"),
        P("dp", "tensor"),
        P("dp", "tensor"),
        P("dp", "tensor"),
        P(),
    )
    return jax.shard_map(
        local,
        mesh=mesh,
        in_specs=placed,
        out_specs=(
            P(None, ("dp", "tensor")),
            P(None, ("dp", "tensor")),
            P(None, "dp", "tensor"),
            P(None, "dp", "tensor"),
            P("dp"),
            P(("dp", "tensor")),
            P(("dp", "tensor")),
            P(("dp", "tensor")),
            P("dp", "tensor"),
            P("dp", "tensor"),
            P("dp", "tensor"),
        ),
        check_vma=False,
    )
```

```python
import math

import jax
import jax.numpy as jnp
from jax import lax
from jax.experimental import pallas as pl
from jax.experimental.pallas import tpu as pltpu
from jax.sharding import PartitionSpec as P

D = 1536
FF = 4096
NS_STEPS = 2
MESH = pl.DeviceIdType.MESH

QUINTIC_LINEAR = 3.4445
QUINTIC_CUBIC = -4.775
QUINTIC_FIFTH = 2.0315
MOMENTUM = 0.95
BIAS_FIRST = 1.0 - 0.9**10
BIAS_SECOND = 1.0 - 0.95**10


def momentum_terms(gradient, state):
    state_next = MOMENTUM * state + gradient
    return (state_next, (gradient + MOMENTUM * state_next).astype(jnp.bfloat16))


def adamw_terms(values, gradient, first, second):
    first_next = 0.9 * first + 0.1 * gradient
    second_next = 0.95 * second + 0.05 * gradient * gradient
    direction = (
        first_next / BIAS_FIRST / (jnp.sqrt(second_next / BIAS_SECOND) + 1e-08) + 0.1 * values
    )
    return (direction, first_next, second_next)


def inverse_of(order):
    count = order.shape[0]
    return jnp.zeros((count,), jnp.int32).at[order].set(jnp.arange(count, dtype=jnp.int32))


def device_barrier(n_dev, me, pairs):
    barrier = pltpu.get_barrier_semaphore()
    t = lax.axis_index("tensor")

    def signal(k, carry):
        target = lax.rem(me + k, n_dev)
        if pairs:
            device = (target // 2, lax.rem(target, 2))
        else:
            device = (target, t)
        pl.semaphore_signal(barrier, inc=1, device_id=device, device_id_type=MESH)
        return carry

    lax.fori_loop(1, n_dev, signal, 0)
    pl.semaphore_wait(barrier, n_dev - 1)


def scatter_kernel(n_sq, n_sw, sq_ref, sw_ref, zero_ref, out_ref, comb_sq, comb_sw, send_sem, recv_sem, pair_sem):
    del zero_ref
    d = lax.axis_index("dp")
    t = lax.axis_index("tensor")
    n_dev = lax.axis_size("dp") * 2
    n_slots = n_sq + n_sw
    me = d * 2 + t
    sq_w = comb_sq.shape[3]
    sw_w = comb_sw.shape[3]
    device_barrier(n_dev, me, True)

    other = 1 - t
    swap_sq = pltpu.make_async_remote_copy(
        src_ref=sq_ref.at[:, :, pl.ds(pl.multiple_of(other * sq_w, 128), sq_w)],
        dst_ref=comb_sq.at[:, t],
        send_sem=pair_sem.at[0],
        recv_sem=pair_sem.at[1],
        device_id=(d, other),
        device_id_type=MESH,
    )
    swap_sw = pltpu.make_async_remote_copy(
        src_ref=sw_ref.at[:, :, pl.ds(pl.multiple_of(other * sw_w, 128), sw_w)],
        dst_ref=comb_sw.at[:, t],
        send_sem=pair_sem.at[2],
        recv_sem=pair_sem.at[3],
        device_id=(d, other),
        device_id_type=MESH,
    )
    keep_sq = pltpu.make_async_copy(
        sq_ref.at[:, :, pl.ds(pl.multiple_of(t * sq_w, 128), sq_w)], comb_sq.at[:, t], pair_sem.at[4]
    )
    keep_sw = pltpu.make_async_copy(
        sw_ref.at[:, :, pl.ds(pl.multiple_of(t * sw_w, 128), sw_w)], comb_sw.at[:, t], pair_sem.at[5]
    )
    swap_sq.start()
    swap_sw.start()
    keep_sq.start()
    keep_sw.start()
    keep_sq.wait()
    keep_sw.wait()
    pltpu.make_async_copy(comb_sq.at[:, other], comb_sq.at[:, other], pair_sem.at[1]).wait()
    pltpu.make_async_copy(comb_sw.at[:, other], comb_sw.at[:, other], pair_sem.at[3]).wait()
    swap_sq.wait_send()
    swap_sw.wait_send()

    def sq_copy(g):
        return pltpu.make_async_remote_copy(
            src_ref=comb_sq.at[g],
            dst_ref=out_ref.at[d, :, :, pl.ds(0, sq_w)],
            send_sem=send_sem.at[g],
            recv_sem=recv_sem.at[0],
            device_id=(g, t),
            device_id_type=MESH,
        )

    def sw_copy(g):
        return pltpu.make_async_remote_copy(
            src_ref=comb_sw.at[g - n_sq],
            dst_ref=out_ref.at[d, :, :, pl.ds(0, sw_w)],
            send_sem=send_sem.at[g],
            recv_sem=recv_sem.at[0],
            device_id=(g, t),
            device_id_type=MESH,
        )

    def start(k, carry):
        g = lax.rem(k + d, n_slots)
        local = g == d

        @pl.when(local & (g < n_sq))
        def _():
            pltpu.make_async_copy(
                comb_sq.at[g], out_ref.at[d, :, :, pl.ds(0, sq_w)], recv_sem.at[0]
            ).start()

        @pl.when(local & (g >= n_sq))
        def _():
            pltpu.make_async_copy(
                comb_sw.at[g - n_sq], out_ref.at[d, :, :, pl.ds(0, sw_w)], recv_sem.at[0]
            ).start()

        @pl.when(jnp.logical_not(local) & (g < n_sq))
        def _():
            sq_copy(g).start()

        @pl.when(jnp.logical_not(local) & (g >= n_sq))
        def _():
            sw_copy(g).start()

        return carry

    lax.fori_loop(0, n_slots, start, 0)

    @pl.when(d < n_sq)
    def _():
        region = out_ref.at[:, :, :, pl.ds(0, sq_w)]
        pltpu.make_async_copy(region, region, recv_sem.at[0]).wait()

    @pl.when((d >= n_sq) & (d < n_slots))
    def _():
        region = out_ref.at[:, :, :, pl.ds(0, sw_w)]
        pltpu.make_async_copy(region, region, recv_sem.at[0]).wait()

    def wait(g, carry):
        @pl.when((g != d) & (g < n_sq))
        def _():
            sq_copy(g).wait_send()

        @pl.when((g != d) & (g >= n_sq))
        def _():
            sw_copy(g).wait_send()

        return carry

    lax.fori_loop(0, n_slots, wait, 0)


def gather_kernel(n_sq, n_sw, it_ref, osq_ref, osw_ref, send_sem, recv_sem):
    d = lax.axis_index("dp")
    t = lax.axis_index("tensor")
    n_dp = lax.axis_size("dp")
    device_barrier(n_dp, d, False)
    is_sq = d < n_sq
    is_sw = (d >= n_sq) & (d < n_sq + n_sw)
    sq_w = osq_ref.shape[2]
    sw_w = osw_ref.shape[2]
    j_sq = jnp.minimum(d, n_sq - 1)
    j_sw = jnp.clip(d - n_sq, 0, n_sw - 1)

    def sq_copy(r):
        return pltpu.make_async_remote_copy(
            src_ref=it_ref.at[r, :, pl.ds(0, sq_w)],
            dst_ref=osq_ref.at[j_sq],
            send_sem=send_sem.at[r],
            recv_sem=recv_sem.at[0],
            device_id=(r, t),
            device_id_type=MESH,
        )

    def sw_copy(r):
        return pltpu.make_async_remote_copy(
            src_ref=it_ref.at[r, :, pl.ds(0, sw_w)],
            dst_ref=osw_ref.at[j_sw],
            send_sem=send_sem.at[r],
            recv_sem=recv_sem.at[1],
            device_id=(r, t),
            device_id_type=MESH,
        )

    @pl.when(is_sq)
    def _():
        def start(k, carry):
            r = lax.rem(d + k, n_dp)

            @pl.when(r == d)
            def _():
                pltpu.make_async_copy(
                    it_ref.at[d, :, pl.ds(0, sq_w)], osq_ref.at[j_sq], recv_sem.at[0]
                ).start()

            @pl.when(r != d)
            def _():
                sq_copy(r).start()

            return carry

        lax.fori_loop(0, n_dp, start, 0)

    @pl.when(is_sw)
    def _():
        def start(k, carry):
            r = lax.rem(d + k, n_dp)

            @pl.when(r == d)
            def _():
                pltpu.make_async_copy(
                    it_ref.at[d, :, pl.ds(0, sw_w)], osw_ref.at[j_sw], recv_sem.at[1]
                ).start()

            @pl.when(r != d)
            def _():
                sw_copy(r).start()

            return carry

        lax.fori_loop(0, n_dp, start, 0)

    pltpu.make_async_copy(osq_ref, osq_ref, recv_sem.at[0]).wait()
    pltpu.make_async_copy(osw_ref, osw_ref, recv_sem.at[1]).wait()

    @pl.when(is_sq)
    def _():
        def wait(r, carry):
            @pl.when(r != d)
            def _():
                sq_copy(r).wait_send()

            return carry

        lax.fori_loop(0, n_dp, wait, 0)

    @pl.when(is_sw)
    def _():
        def wait(r, carry):
            @pl.when(r != d)
            def _():
                sw_copy(r).wait_send()

            return carry

        lax.fori_loop(0, n_dp, wait, 0)


def swap_halves(x):
    return lax.ppermute(x, "tensor", perm=[(0, 1), (1, 0)])


def orthogonalize(arrived, factor):
    t = lax.axis_index("tensor")
    rows = arrived.shape[0] // 2
    mine = pl.multiple_of(t * rows, rows)
    theirs = pl.multiple_of((1 - t) * rows, rows)
    iterate = arrived
    first_scale = jnp.float32(1.0)
    for round_index in range(NS_STEPS):
        current = iterate
        their_rows = lax.dynamic_slice_in_dim(current, theirs, rows, 0)
        my_rows = lax.dynamic_slice_in_dim(current, mine, rows, 0)
        sent = swap_halves(
            jnp.einsum("rc,sc->rs", their_rows, current, preferred_element_type=jnp.float32)
        )
        kept = lax.optimization_barrier(
            jnp.einsum("rc,sc->rs", my_rows, current, preferred_element_type=jnp.float32)
        )
        gram_part = kept + sent
        if round_index == 0:
            squares_total = lax.psum(jnp.sum(gram_part * gram_part), "tensor")
            gram_scale = jnp.sqrt(squares_total) + 1e-06
            first_scale = gram_scale
        else:
            gram_scale = jnp.float32(1.0)
        normed_part = (gram_part / gram_scale).astype(jnp.bfloat16)
        normed_other = swap_halves(normed_part)
        squared = lax.optimization_barrier(
            jnp.dot(
                lax.dynamic_slice_in_dim(normed_part, mine, rows, 1),
                normed_part,
                preferred_element_type=jnp.float32,
            )
        ) + jnp.dot(
            lax.dynamic_slice_in_dim(normed_part, theirs, rows, 1),
            normed_other,
            preferred_element_type=jnp.float32,
        )
        polynomial = (
            QUINTIC_CUBIC * normed_part.astype(jnp.float32) + QUINTIC_FIFTH * squared
        ).astype(jnp.bfloat16)
        poly_other = swap_halves(polynomial)
        product_mine = lax.optimization_barrier(
            jnp.dot(polynomial, current, preferred_element_type=jnp.float32)
        )
        product_other = jnp.dot(poly_other, current, preferred_element_type=jnp.float32)
        scale_root = jnp.sqrt(gram_scale)
        halves = []
        for rows_here, product_here in ((my_rows, product_mine), (their_rows, product_other)):
            mixed = (QUINTIC_LINEAR * rows_here.astype(jnp.float32) + product_here) / scale_root
            if round_index == NS_STEPS - 1:
                mixed = factor * mixed
            halves.append(mixed.astype(jnp.bfloat16))
        iterate = lax.dynamic_update_slice_in_dim(
            lax.dynamic_update_slice_in_dim(jnp.zeros_like(current), halves[0], mine, 0),
            halves[1],
            theirs,
            0,
        )
    return (iterate, first_scale)


def with_scale_row(blocks, scale):
    high = scale.astype(jnp.bfloat16)
    low = (scale - high.astype(jnp.float32)).astype(jnp.bfloat16)
    lanes = lax.broadcasted_iota(jnp.int32, (blocks.shape[0], 1, blocks.shape[2]), 2)
    row = jnp.where(lanes == 0, high, jnp.where(lanes == 1, low, jnp.zeros((), jnp.bfloat16)))
    return jnp.concatenate([blocks, row], axis=1)


def scale_of_row(returned):
    row = returned[:, -1, :2].astype(jnp.float32)
    return row[:, 0] + row[:, 1]


def local(
    square_grad,
    square_state,
    swiglu_grad,
    swiglu_state,
    square_order,
    swiglu_order,
    owners,
    vector_values,
    vector_grad,
    vector_first,
    vector_second,
    embed_values,
    embed_grad,
    embed_first,
    embed_second,
    embed_ranges,
):
    wide_count = lax.axis_size("dp")
    n_dev = wide_count * 2
    d = lax.axis_index("dp")
    t = lax.axis_index("tensor")
    n_sq = square_grad.shape[0]
    n_sw = swiglu_grad.shape[0]
    flat_rows = D // n_dev
    out_rows = D // wide_count
    square_next, square_send = momentum_terms(square_grad, square_state)
    swiglu_next, swiglu_send = momentum_terms(swiglu_grad, swiglu_state)
    sq_pieces = square_send.reshape(n_sq, flat_rows, D)
    sw_pieces = swiglu_send.reshape(n_sw, flat_rows, FF)

    half = FF // 2
    sq_halves = jnp.pad(
        sq_pieces.reshape(n_sq, flat_rows, 2, D // 2).transpose(0, 2, 1, 3),
        ((0, 0), (0, 0), (0, 0), (0, half - D // 2)),
    )
    sw_halves = sw_pieces.reshape(n_sw, flat_rows, 2, half).transpose(0, 2, 1, 3)
    outgoing = jnp.pad(
        jnp.concatenate([sq_halves, sw_halves], axis=0),
        ((0, wide_count - n_sq - n_sw), (0, 0), (0, 0), (0, 0)),
    )
    arrived = lax.all_to_all(
        outgoing.reshape(D, half), ("dp", "tensor"), split_axis=0, concat_axis=0, tiled=True
    )

    is_sq = d < n_sq
    is_sw = (d >= n_sq) & (d < n_sq + n_sw)
    factor = jnp.where(is_sq, jnp.float32(math.sqrt(D)), jnp.float32(math.sqrt(FF)))
    iterate, first_scale = orthogonalize(arrived, factor)

    returned_sq, returned_sw = pl.pallas_call(
        lambda *refs: gather_kernel(n_sq, n_sw, *refs),
        out_shape=(
            jax.ShapeDtypeStruct((n_sq, out_rows + 1, D // 2), jnp.bfloat16),
            jax.ShapeDtypeStruct((n_sw, out_rows + 1, FF // 2), jnp.bfloat16),
        ),
        in_specs=[pl.BlockSpec(memory_space=pl.ANY)],
        out_specs=(pl.BlockSpec(memory_space=pl.ANY), pl.BlockSpec(memory_space=pl.ANY)),
        scratch_shapes=[
            pltpu.SemaphoreType.DMA((wide_count,)),
            pltpu.SemaphoreType.DMA((2,)),
        ],
        compiler_params=pltpu.CompilerParams(collective_id=1, has_side_effects=True),
    )(with_scale_row(iterate.reshape(wide_count, out_rows, half), first_scale))

    inv_sq = inverse_of(square_order)
    inv_sw = inverse_of(swiglu_order)
    square_update = returned_sq[inv_sq][:, :out_rows]
    swiglu_update = returned_sw[inv_sw][:, :out_rows]

    slot_scales = jnp.concatenate([scale_of_row(returned_sq), scale_of_row(returned_sw)])
    slot_norms = 0.5 * jnp.log(slot_scales)
    matrix_slot = jnp.concatenate([inv_sq, n_sq + inv_sw])
    matrix_norms = slot_norms[matrix_slot]
    owner_norms = jnp.sum(jnp.where(owners == d, matrix_norms, 0.0)).reshape(1)

    vector_step, first_vector, second_vector = adamw_terms(
        vector_values, vector_grad, vector_first, vector_second
    )
    embed_rows = embed_values.shape[0]
    row_numbers = d * embed_rows + jnp.arange(embed_rows, dtype=jnp.int32)
    inside = (row_numbers[:, None] >= embed_ranges[None, :, 0]) & (
        row_numbers[:, None] < embed_ranges[None, :, 1]
    )
    row_live = jnp.sum(inside.astype(jnp.int32), axis=1) > 0
    direction, first_next, second_next = adamw_terms(
        embed_values, embed_grad, embed_first, embed_second
    )
    embed_step = jnp.where(row_live[:, None], direction, 0.0)
    first_embed = jnp.where(row_live[:, None], first_next, embed_first)
    second_embed = jnp.where(row_live[:, None], second_next, embed_second)
    return (
        square_next,
        swiglu_next,
        square_update,
        swiglu_update,
        owner_norms,
        vector_step,
        first_vector,
        second_vector,
        embed_step,
        first_embed,
        second_embed,
    )


def solution(mesh):
    placed = (
        P(None, ("dp", "tensor")),
        P(None, ("dp", "tensor")),
        P(None, ("dp", "tensor")),
        P(None, ("dp", "tensor")),
        P(),
        P(),
        P(),
        P(("dp", "tensor")),
        P(("dp", "tensor")),
        P(("dp", "tensor")),
        P(("dp", "tensor")),
        P("dp", "tensor"),
        P("dp", "tensor"),
        P("dp", "tensor"),
        P("dp", "tensor"),
        P(),
    )
    return jax.shard_map(
        local,
        mesh=mesh,
        in_specs=placed,
        out_specs=(
            P(None, ("dp", "tensor")),
            P(None, ("dp", "tensor")),
            P(None, "dp", "tensor"),
            P(None, "dp", "tensor"),
            P("dp"),
            P(("dp", "tensor")),
            P(("dp", "tensor")),
            P(("dp", "tensor")),
            P("dp", "tensor"),
            P("dp", "tensor"),
            P("dp", "tensor"),
        ),
        check_vma=False,
    )
```

```python
import math

import jax
import jax.numpy as jnp
from jax import lax
from jax.experimental import pallas as pl
from jax.experimental.pallas import tpu as pltpu
from jax.sharding import PartitionSpec as P

D = 1536
FF = 4096
NS_STEPS = 2
MESH = pl.DeviceIdType.MESH

QUINTIC_LINEAR = 3.4445
QUINTIC_CUBIC = -4.775
QUINTIC_FIFTH = 2.0315
MOMENTUM = 0.95
BIAS_FIRST = 1.0 - 0.9**10
BIAS_SECOND = 1.0 - 0.95**10


def momentum_terms(gradient, state):
    state_next = MOMENTUM * state + gradient
    return (state_next, (gradient + MOMENTUM * state_next).astype(jnp.bfloat16))


def adamw_terms(values, gradient, first, second):
    first_next = 0.9 * first + 0.1 * gradient
    second_next = 0.95 * second + 0.05 * gradient * gradient
    direction = (
        first_next / BIAS_FIRST / (jnp.sqrt(second_next / BIAS_SECOND) + 1e-08) + 0.1 * values
    )
    return (direction, first_next, second_next)


def inverse_of(order):
    count = order.shape[0]
    return jnp.zeros((count,), jnp.int32).at[order].set(jnp.arange(count, dtype=jnp.int32))


def device_barrier(n_dev, me, pairs):
    barrier = pltpu.get_barrier_semaphore()
    t = lax.axis_index("tensor")

    def signal(k, carry):
        target = lax.rem(me + k, n_dev)
        if pairs:
            device = (target // 2, lax.rem(target, 2))
        else:
            device = (target, t)
        pl.semaphore_signal(barrier, inc=1, device_id=device, device_id_type=MESH)
        return carry

    lax.fori_loop(1, n_dev, signal, 0)
    pl.semaphore_wait(barrier, n_dev - 1)


def scatter_kernel(n_sq, n_sw, sq_ref, sw_ref, zero_ref, out_ref, comb_sq, comb_sw, send_sem, recv_sem, pair_sem):
    del zero_ref
    d = lax.axis_index("dp")
    t = lax.axis_index("tensor")
    n_dev = lax.axis_size("dp") * 2
    n_slots = n_sq + n_sw
    me = d * 2 + t
    sq_w = comb_sq.shape[3]
    sw_w = comb_sw.shape[3]
    device_barrier(n_dev, me, True)

    other = 1 - t
    swap_sq = pltpu.make_async_remote_copy(
        src_ref=sq_ref.at[:, :, pl.ds(pl.multiple_of(other * sq_w, 128), sq_w)],
        dst_ref=comb_sq.at[:, t],
        send_sem=pair_sem.at[0],
        recv_sem=pair_sem.at[1],
        device_id=(d, other),
        device_id_type=MESH,
    )
    swap_sw = pltpu.make_async_remote_copy(
        src_ref=sw_ref.at[:, :, pl.ds(pl.multiple_of(other * sw_w, 128), sw_w)],
        dst_ref=comb_sw.at[:, t],
        send_sem=pair_sem.at[2],
        recv_sem=pair_sem.at[3],
        device_id=(d, other),
        device_id_type=MESH,
    )
    keep_sq = pltpu.make_async_copy(
        sq_ref.at[:, :, pl.ds(pl.multiple_of(t * sq_w, 128), sq_w)], comb_sq.at[:, t], pair_sem.at[4]
    )
    keep_sw = pltpu.make_async_copy(
        sw_ref.at[:, :, pl.ds(pl.multiple_of(t * sw_w, 128), sw_w)], comb_sw.at[:, t], pair_sem.at[5]
    )
    swap_sq.start()
    swap_sw.start()
    keep_sq.start()
    keep_sw.start()
    keep_sq.wait()
    keep_sw.wait()
    pltpu.make_async_copy(comb_sq.at[:, other], comb_sq.at[:, other], pair_sem.at[1]).wait()
    pltpu.make_async_copy(comb_sw.at[:, other], comb_sw.at[:, other], pair_sem.at[3]).wait()
    swap_sq.wait_send()
    swap_sw.wait_send()

    def sq_copy(g):
        return pltpu.make_async_remote_copy(
            src_ref=comb_sq.at[g],
            dst_ref=out_ref.at[d, :, :, pl.ds(0, sq_w)],
            send_sem=send_sem.at[g],
            recv_sem=recv_sem.at[0],
            device_id=(g, t),
            device_id_type=MESH,
        )

    def sw_copy(g):
        return pltpu.make_async_remote_copy(
            src_ref=comb_sw.at[g - n_sq],
            dst_ref=out_ref.at[d, :, :, pl.ds(0, sw_w)],
            send_sem=send_sem.at[g],
            recv_sem=recv_sem.at[0],
            device_id=(g, t),
            device_id_type=MESH,
        )

    def start(k, carry):
        g = lax.rem(k + d, n_slots)
        local = g == d

        @pl.when(local & (g < n_sq))
        def _():
            pltpu.make_async_copy(
                comb_sq.at[g], out_ref.at[d, :, :, pl.ds(0, sq_w)], recv_sem.at[0]
            ).start()

        @pl.when(local & (g >= n_sq))
        def _():
            pltpu.make_async_copy(
                comb_sw.at[g - n_sq], out_ref.at[d, :, :, pl.ds(0, sw_w)], recv_sem.at[0]
            ).start()

        @pl.when(jnp.logical_not(local) & (g < n_sq))
        def _():
            sq_copy(g).start()

        @pl.when(jnp.logical_not(local) & (g >= n_sq))
        def _():
            sw_copy(g).start()

        return carry

    lax.fori_loop(0, n_slots, start, 0)

    @pl.when(d < n_sq)
    def _():
        region = out_ref.at[:, :, :, pl.ds(0, sq_w)]
        pltpu.make_async_copy(region, region, recv_sem.at[0]).wait()

    @pl.when((d >= n_sq) & (d < n_slots))
    def _():
        region = out_ref.at[:, :, :, pl.ds(0, sw_w)]
        pltpu.make_async_copy(region, region, recv_sem.at[0]).wait()

    def wait(g, carry):
        @pl.when((g != d) & (g < n_sq))
        def _():
            sq_copy(g).wait_send()

        @pl.when((g != d) & (g >= n_sq))
        def _():
            sw_copy(g).wait_send()

        return carry

    lax.fori_loop(0, n_slots, wait, 0)


def gather_kernel(n_sq, n_sw, it_ref, osq_ref, osw_ref, send_sem, recv_sem):
    d = lax.axis_index("dp")
    t = lax.axis_index("tensor")
    n_dp = lax.axis_size("dp")
    device_barrier(n_dp, d, False)
    is_sq = d < n_sq
    is_sw = (d >= n_sq) & (d < n_sq + n_sw)
    sq_w = osq_ref.shape[2]
    sw_w = osw_ref.shape[2]
    j_sq = jnp.minimum(d, n_sq - 1)
    j_sw = jnp.clip(d - n_sq, 0, n_sw - 1)

    def sq_copy(r):
        return pltpu.make_async_remote_copy(
            src_ref=it_ref.at[r, :, pl.ds(0, sq_w)],
            dst_ref=osq_ref.at[j_sq],
            send_sem=send_sem.at[r],
            recv_sem=recv_sem.at[0],
            device_id=(r, t),
            device_id_type=MESH,
        )

    def sw_copy(r):
        return pltpu.make_async_remote_copy(
            src_ref=it_ref.at[r, :, pl.ds(0, sw_w)],
            dst_ref=osw_ref.at[j_sw],
            send_sem=send_sem.at[r],
            recv_sem=recv_sem.at[1],
            device_id=(r, t),
            device_id_type=MESH,
        )

    @pl.when(is_sq)
    def _():
        def start(k, carry):
            r = lax.rem(d + k, n_dp)

            @pl.when(r == d)
            def _():
                pltpu.make_async_copy(
                    it_ref.at[d, :, pl.ds(0, sq_w)], osq_ref.at[j_sq], recv_sem.at[0]
                ).start()

            @pl.when(r != d)
            def _():
                sq_copy(r).start()

            return carry

        lax.fori_loop(0, n_dp, start, 0)

    @pl.when(is_sw)
    def _():
        def start(k, carry):
            r = lax.rem(d + k, n_dp)

            @pl.when(r == d)
            def _():
                pltpu.make_async_copy(
                    it_ref.at[d, :, pl.ds(0, sw_w)], osw_ref.at[j_sw], recv_sem.at[1]
                ).start()

            @pl.when(r != d)
            def _():
                sw_copy(r).start()

            return carry

        lax.fori_loop(0, n_dp, start, 0)

    pltpu.make_async_copy(osq_ref, osq_ref, recv_sem.at[0]).wait()
    pltpu.make_async_copy(osw_ref, osw_ref, recv_sem.at[1]).wait()

    @pl.when(is_sq)
    def _():
        def wait(r, carry):
            @pl.when(r != d)
            def _():
                sq_copy(r).wait_send()

            return carry

        lax.fori_loop(0, n_dp, wait, 0)

    @pl.when(is_sw)
    def _():
        def wait(r, carry):
            @pl.when(r != d)
            def _():
                sw_copy(r).wait_send()

            return carry

        lax.fori_loop(0, n_dp, wait, 0)


def swap_halves(x):
    return lax.ppermute(x, "tensor", perm=[(0, 1), (1, 0)])


def orthogonalize(arrived, factor):
    t = lax.axis_index("tensor")
    rows = arrived.shape[0] // 2
    mine = pl.multiple_of(t * rows, rows)
    theirs = pl.multiple_of((1 - t) * rows, rows)
    iterate = arrived
    first_scale = jnp.float32(1.0)
    for round_index in range(NS_STEPS):
        current = iterate
        their_rows = lax.dynamic_slice_in_dim(current, theirs, rows, 0)
        my_rows = lax.dynamic_slice_in_dim(current, mine, rows, 0)
        sent = swap_halves(
            jnp.einsum("rc,sc->rs", their_rows, current, preferred_element_type=jnp.float32)
        )
        kept = lax.optimization_barrier(
            jnp.einsum("rc,sc->rs", my_rows, current, preferred_element_type=jnp.float32)
        )
        gram_part = kept + sent
        if round_index == 0:
            squares_total = lax.psum(jnp.sum(gram_part * gram_part), "tensor")
            gram_scale = jnp.sqrt(squares_total) + 1e-06
            first_scale = gram_scale
        else:
            gram_scale = jnp.float32(1.0)
        normed_part = (gram_part / gram_scale).astype(jnp.bfloat16)
        normed_other = swap_halves(normed_part)
        squared = lax.optimization_barrier(
            jnp.dot(
                lax.dynamic_slice_in_dim(normed_part, mine, rows, 1),
                normed_part,
                preferred_element_type=jnp.float32,
            )
        ) + jnp.dot(
            lax.dynamic_slice_in_dim(normed_part, theirs, rows, 1),
            normed_other,
            preferred_element_type=jnp.float32,
        )
        polynomial = (
            QUINTIC_CUBIC * normed_part.astype(jnp.float32) + QUINTIC_FIFTH * squared
        ).astype(jnp.bfloat16)
        poly_other = swap_halves(polynomial)
        product_mine = lax.optimization_barrier(
            jnp.dot(polynomial, current, preferred_element_type=jnp.float32)
        )
        product_other = jnp.dot(poly_other, current, preferred_element_type=jnp.float32)
        scale_root = jnp.sqrt(gram_scale)
        halves = []
        for rows_here, product_here in ((my_rows, product_mine), (their_rows, product_other)):
            mixed = (QUINTIC_LINEAR * rows_here.astype(jnp.float32) + product_here) / scale_root
            if round_index == NS_STEPS - 1:
                mixed = factor * mixed
            halves.append(mixed.astype(jnp.bfloat16))
        iterate = lax.dynamic_update_slice_in_dim(
            lax.dynamic_update_slice_in_dim(jnp.zeros_like(current), halves[0], mine, 0),
            halves[1],
            theirs,
            0,
        )
    return (iterate, first_scale)


def with_scale_row(blocks, scale):
    high = scale.astype(jnp.bfloat16)
    low = (scale - high.astype(jnp.float32)).astype(jnp.bfloat16)
    lanes = lax.broadcasted_iota(jnp.int32, (blocks.shape[0], 1, blocks.shape[2]), 2)
    row = jnp.where(lanes == 0, high, jnp.where(lanes == 1, low, jnp.zeros((), jnp.bfloat16)))
    return jnp.concatenate([blocks, row], axis=1)


def scale_of_row(returned):
    row = returned[:, -1, :2].astype(jnp.float32)
    return row[:, 0] + row[:, 1]


def local(
    square_grad,
    square_state,
    swiglu_grad,
    swiglu_state,
    square_order,
    swiglu_order,
    owners,
    vector_values,
    vector_grad,
    vector_first,
    vector_second,
    embed_values,
    embed_grad,
    embed_first,
    embed_second,
    embed_ranges,
):
    wide_count = lax.axis_size("dp")
    n_dev = wide_count * 2
    d = lax.axis_index("dp")
    t = lax.axis_index("tensor")
    n_sq = square_grad.shape[0]
    n_sw = swiglu_grad.shape[0]
    flat_rows = D // n_dev
    out_rows = D // wide_count
    square_next, square_send = momentum_terms(square_grad, square_state)
    swiglu_next, swiglu_send = momentum_terms(swiglu_grad, swiglu_state)
    sq_pieces = square_send.reshape(n_sq, flat_rows, D)
    sw_pieces = swiglu_send.reshape(n_sw, flat_rows, FF)

    half = FF // 2
    sq_halves = jnp.pad(
        sq_pieces.reshape(n_sq, flat_rows, 2, D // 2).transpose(0, 2, 1, 3),
        ((0, 0), (0, 0), (0, 0), (0, half - D // 2)),
    )
    sw_halves = sw_pieces.reshape(n_sw, flat_rows, 2, half).transpose(0, 2, 1, 3)
    outgoing = jnp.pad(
        jnp.concatenate([sq_halves, sw_halves], axis=0),
        ((0, wide_count - n_sq - n_sw), (0, 0), (0, 0), (0, 0)),
    )
    arrived = lax.all_to_all(
        outgoing.reshape(D, half), ("dp", "tensor"), split_axis=0, concat_axis=0, tiled=True
    )

    is_sq = d < n_sq
    is_sw = (d >= n_sq) & (d < n_sq + n_sw)
    factor = jnp.where(is_sq, jnp.float32(math.sqrt(D)), jnp.float32(math.sqrt(FF)))
    iterate, first_scale = orthogonalize(arrived, factor)

    returned = lax.all_to_all(
        with_scale_row(iterate.reshape(wide_count, out_rows, half), first_scale),
        "dp",
        split_axis=0,
        concat_axis=0,
        tiled=True,
    )
    returned_sq = returned[:n_sq, :, : D // 2]
    returned_sw = returned[n_sq : n_sq + n_sw]

    inv_sq = inverse_of(square_order)
    inv_sw = inverse_of(swiglu_order)
    square_update = returned_sq[inv_sq][:, :out_rows]
    swiglu_update = returned_sw[inv_sw][:, :out_rows]

    slot_scales = jnp.concatenate([scale_of_row(returned_sq), scale_of_row(returned_sw)])
    slot_norms = 0.5 * jnp.log(slot_scales)
    matrix_slot = jnp.concatenate([inv_sq, n_sq + inv_sw])
    matrix_norms = slot_norms[matrix_slot]
    owner_norms = jnp.sum(jnp.where(owners == d, matrix_norms, 0.0)).reshape(1)

    vector_step, first_vector, second_vector = adamw_terms(
        vector_values, vector_grad, vector_first, vector_second
    )
    embed_rows = embed_values.shape[0]
    row_numbers = d * embed_rows + jnp.arange(embed_rows, dtype=jnp.int32)
    inside = (row_numbers[:, None] >= embed_ranges[None, :, 0]) & (
        row_numbers[:, None] < embed_ranges[None, :, 1]
    )
    row_live = jnp.sum(inside.astype(jnp.int32), axis=1) > 0
    direction, first_next, second_next = adamw_terms(
        embed_values, embed_grad, embed_first, embed_second
    )
    embed_step = jnp.where(row_live[:, None], direction, 0.0)
    first_embed = jnp.where(row_live[:, None], first_next, embed_first)
    second_embed = jnp.where(row_live[:, None], second_next, embed_second)
    return (
        square_next,
        swiglu_next,
        square_update,
        swiglu_update,
        owner_norms,
        vector_step,
        first_vector,
        second_vector,
        embed_step,
        first_embed,
        second_embed,
    )


def solution(mesh):
    placed = (
        P(None, ("dp", "tensor")),
        P(None, ("dp", "tensor")),
        P(None, ("dp", "tensor")),
        P(None, ("dp", "tensor")),
        P(),
        P(),
        P(),
        P(("dp", "tensor")),
        P(("dp", "tensor")),
        P(("dp", "tensor")),
        P(("dp", "tensor")),
        P("dp", "tensor"),
        P("dp", "tensor"),
        P("dp", "tensor"),
        P("dp", "tensor"),
        P(),
    )
    return jax.shard_map(
        local,
        mesh=mesh,
        in_specs=placed,
        out_specs=(
            P(None, ("dp", "tensor")),
            P(None, ("dp", "tensor")),
            P(None, "dp", "tensor"),
            P(None, "dp", "tensor"),
            P("dp"),
            P(("dp", "tensor")),
            P(("dp", "tensor")),
            P(("dp", "tensor")),
            P("dp", "tensor"),
            P("dp", "tensor"),
            P("dp", "tensor"),
        ),
        check_vma=False,
    )
```

```python
import math

import jax
import jax.numpy as jnp
from jax import lax
from jax.experimental import pallas as pl
from jax.experimental.pallas import tpu as pltpu
from jax.sharding import PartitionSpec as P

D = 1536
FF = 4096
NS_STEPS = 2
MESH = pl.DeviceIdType.MESH

QUINTIC_LINEAR = 3.4445
QUINTIC_CUBIC = -4.775
QUINTIC_FIFTH = 2.0315
MOMENTUM = 0.95
BIAS_FIRST = 1.0 - 0.9**10
BIAS_SECOND = 1.0 - 0.95**10


def momentum_terms(gradient, state):
    state_next = MOMENTUM * state + gradient
    return (state_next, (gradient + MOMENTUM * state_next).astype(jnp.bfloat16))


def adamw_terms(values, gradient, first, second):
    first_next = 0.9 * first + 0.1 * gradient
    second_next = 0.95 * second + 0.05 * gradient * gradient
    direction = (
        first_next / BIAS_FIRST / (jnp.sqrt(second_next / BIAS_SECOND) + 1e-08) + 0.1 * values
    )
    return (direction, first_next, second_next)


def inverse_of(order):
    count = order.shape[0]
    return jnp.zeros((count,), jnp.int32).at[order].set(jnp.arange(count, dtype=jnp.int32))


def device_barrier(n_dev, me, pairs):
    barrier = pltpu.get_barrier_semaphore()
    t = lax.axis_index("tensor")

    def signal(k, carry):
        target = lax.rem(me + k, n_dev)
        if pairs:
            device = (target // 2, lax.rem(target, 2))
        else:
            device = (target, t)
        pl.semaphore_signal(barrier, inc=1, device_id=device, device_id_type=MESH)
        return carry

    lax.fori_loop(1, n_dev, signal, 0)
    pl.semaphore_wait(barrier, n_dev - 1)


def scatter_kernel(n_sq, n_sw, sq_ref, sw_ref, zero_ref, out_ref, comb_sq, comb_sw, send_sem, recv_sem, pair_sem):
    del zero_ref
    d = lax.axis_index("dp")
    t = lax.axis_index("tensor")
    n_dev = lax.axis_size("dp") * 2
    n_slots = n_sq + n_sw
    me = d * 2 + t
    sq_w = comb_sq.shape[3]
    sw_w = comb_sw.shape[3]
    device_barrier(n_dev, me, True)

    other = 1 - t
    swap_sq = pltpu.make_async_remote_copy(
        src_ref=sq_ref.at[:, :, pl.ds(pl.multiple_of(other * sq_w, 128), sq_w)],
        dst_ref=comb_sq.at[:, t],
        send_sem=pair_sem.at[0],
        recv_sem=pair_sem.at[1],
        device_id=(d, other),
        device_id_type=MESH,
    )
    swap_sw = pltpu.make_async_remote_copy(
        src_ref=sw_ref.at[:, :, pl.ds(pl.multiple_of(other * sw_w, 128), sw_w)],
        dst_ref=comb_sw.at[:, t],
        send_sem=pair_sem.at[2],
        recv_sem=pair_sem.at[3],
        device_id=(d, other),
        device_id_type=MESH,
    )
    keep_sq = pltpu.make_async_copy(
        sq_ref.at[:, :, pl.ds(pl.multiple_of(t * sq_w, 128), sq_w)], comb_sq.at[:, t], pair_sem.at[4]
    )
    keep_sw = pltpu.make_async_copy(
        sw_ref.at[:, :, pl.ds(pl.multiple_of(t * sw_w, 128), sw_w)], comb_sw.at[:, t], pair_sem.at[5]
    )
    swap_sq.start()
    swap_sw.start()
    keep_sq.start()
    keep_sw.start()
    keep_sq.wait()
    keep_sw.wait()
    pltpu.make_async_copy(comb_sq.at[:, other], comb_sq.at[:, other], pair_sem.at[1]).wait()
    pltpu.make_async_copy(comb_sw.at[:, other], comb_sw.at[:, other], pair_sem.at[3]).wait()
    swap_sq.wait_send()
    swap_sw.wait_send()

    def sq_copy(g):
        return pltpu.make_async_remote_copy(
            src_ref=comb_sq.at[g],
            dst_ref=out_ref.at[d, :, :, pl.ds(0, sq_w)],
            send_sem=send_sem.at[g],
            recv_sem=recv_sem.at[0],
            device_id=(g, t),
            device_id_type=MESH,
        )

    def sw_copy(g):
        return pltpu.make_async_remote_copy(
            src_ref=comb_sw.at[g - n_sq],
            dst_ref=out_ref.at[d, :, :, pl.ds(0, sw_w)],
            send_sem=send_sem.at[g],
            recv_sem=recv_sem.at[0],
            device_id=(g, t),
            device_id_type=MESH,
        )

    def start(k, carry):
        g = lax.rem(k + d, n_slots)
        local = g == d

        @pl.when(local & (g < n_sq))
        def _():
            pltpu.make_async_copy(
                comb_sq.at[g], out_ref.at[d, :, :, pl.ds(0, sq_w)], recv_sem.at[0]
            ).start()

        @pl.when(local & (g >= n_sq))
        def _():
            pltpu.make_async_copy(
                comb_sw.at[g - n_sq], out_ref.at[d, :, :, pl.ds(0, sw_w)], recv_sem.at[0]
            ).start()

        @pl.when(jnp.logical_not(local) & (g < n_sq))
        def _():
            sq_copy(g).start()

        @pl.when(jnp.logical_not(local) & (g >= n_sq))
        def _():
            sw_copy(g).start()

        return carry

    lax.fori_loop(0, n_slots, start, 0)

    @pl.when(d < n_sq)
    def _():
        region = out_ref.at[:, :, :, pl.ds(0, sq_w)]
        pltpu.make_async_copy(region, region, recv_sem.at[0]).wait()

    @pl.when((d >= n_sq) & (d < n_slots))
    def _():
        region = out_ref.at[:, :, :, pl.ds(0, sw_w)]
        pltpu.make_async_copy(region, region, recv_sem.at[0]).wait()

    def wait(g, carry):
        @pl.when((g != d) & (g < n_sq))
        def _():
            sq_copy(g).wait_send()

        @pl.when((g != d) & (g >= n_sq))
        def _():
            sw_copy(g).wait_send()

        return carry

    lax.fori_loop(0, n_slots, wait, 0)


def gather_kernel(n_sq, n_sw, it_ref, osq_ref, osw_ref, send_sem, recv_sem):
    d = lax.axis_index("dp")
    t = lax.axis_index("tensor")
    n_dp = lax.axis_size("dp")
    device_barrier(n_dp, d, False)
    is_sq = d < n_sq
    is_sw = (d >= n_sq) & (d < n_sq + n_sw)
    sq_w = osq_ref.shape[2]
    sw_w = osw_ref.shape[2]
    j_sq = jnp.minimum(d, n_sq - 1)
    j_sw = jnp.clip(d - n_sq, 0, n_sw - 1)

    def sq_copy(r):
        return pltpu.make_async_remote_copy(
            src_ref=it_ref.at[r, :, pl.ds(0, sq_w)],
            dst_ref=osq_ref.at[j_sq],
            send_sem=send_sem.at[r],
            recv_sem=recv_sem.at[0],
            device_id=(r, t),
            device_id_type=MESH,
        )

    def sw_copy(r):
        return pltpu.make_async_remote_copy(
            src_ref=it_ref.at[r, :, pl.ds(0, sw_w)],
            dst_ref=osw_ref.at[j_sw],
            send_sem=send_sem.at[r],
            recv_sem=recv_sem.at[1],
            device_id=(r, t),
            device_id_type=MESH,
        )

    @pl.when(is_sq)
    def _():
        def start(k, carry):
            r = lax.rem(d + k, n_dp)

            @pl.when(r == d)
            def _():
                pltpu.make_async_copy(
                    it_ref.at[d, :, pl.ds(0, sq_w)], osq_ref.at[j_sq], recv_sem.at[0]
                ).start()

            @pl.when(r != d)
            def _():
                sq_copy(r).start()

            return carry

        lax.fori_loop(0, n_dp, start, 0)

    @pl.when(is_sw)
    def _():
        def start(k, carry):
            r = lax.rem(d + k, n_dp)

            @pl.when(r == d)
            def _():
                pltpu.make_async_copy(
                    it_ref.at[d, :, pl.ds(0, sw_w)], osw_ref.at[j_sw], recv_sem.at[1]
                ).start()

            @pl.when(r != d)
            def _():
                sw_copy(r).start()

            return carry

        lax.fori_loop(0, n_dp, start, 0)

    pltpu.make_async_copy(osq_ref, osq_ref, recv_sem.at[0]).wait()
    pltpu.make_async_copy(osw_ref, osw_ref, recv_sem.at[1]).wait()

    @pl.when(is_sq)
    def _():
        def wait(r, carry):
            @pl.when(r != d)
            def _():
                sq_copy(r).wait_send()

            return carry

        lax.fori_loop(0, n_dp, wait, 0)

    @pl.when(is_sw)
    def _():
        def wait(r, carry):
            @pl.when(r != d)
            def _():
                sw_copy(r).wait_send()

            return carry

        lax.fori_loop(0, n_dp, wait, 0)


def swap_halves(x):
    return lax.ppermute(x, "tensor", perm=[(0, 1), (1, 0)])


def orthogonalize(arrived, factor):
    t = lax.axis_index("tensor")
    rows = arrived.shape[0] // 2
    mine = pl.multiple_of(t * rows, rows)
    theirs = pl.multiple_of((1 - t) * rows, rows)
    iterate = arrived
    first_scale = jnp.float32(1.0)
    for round_index in range(NS_STEPS):
        current = iterate
        their_rows = lax.dynamic_slice_in_dim(current, theirs, rows, 0)
        my_rows = lax.dynamic_slice_in_dim(current, mine, rows, 0)
        sent = swap_halves(
            jnp.einsum("rc,sc->rs", their_rows, current, preferred_element_type=jnp.float32)
        )
        kept = lax.optimization_barrier(
            jnp.einsum("rc,sc->rs", my_rows, current, preferred_element_type=jnp.float32)
        )
        gram_part = kept + sent
        if round_index == 0:
            squares_total = lax.psum(jnp.sum(gram_part * gram_part), "tensor")
            gram_scale = jnp.sqrt(squares_total) + 1e-06
            first_scale = gram_scale
        else:
            gram_scale = jnp.float32(1.0)
        normed_part = (gram_part / gram_scale).astype(jnp.bfloat16)
        normed_other = swap_halves(normed_part)
        squared = lax.optimization_barrier(
            jnp.dot(
                lax.dynamic_slice_in_dim(normed_part, mine, rows, 1),
                normed_part,
                preferred_element_type=jnp.float32,
            )
        ) + jnp.dot(
            lax.dynamic_slice_in_dim(normed_part, theirs, rows, 1),
            normed_other,
            preferred_element_type=jnp.float32,
        )
        polynomial = (
            QUINTIC_CUBIC * normed_part.astype(jnp.float32) + QUINTIC_FIFTH * squared
        ).astype(jnp.bfloat16)
        poly_other = swap_halves(polynomial)
        product_mine = lax.optimization_barrier(
            jnp.dot(polynomial, current, preferred_element_type=jnp.float32)
        )
        product_other = jnp.dot(poly_other, current, preferred_element_type=jnp.float32)
        scale_root = jnp.sqrt(gram_scale)
        halves = []
        for rows_here, product_here in ((my_rows, product_mine), (their_rows, product_other)):
            mixed = (QUINTIC_LINEAR * rows_here.astype(jnp.float32) + product_here) / scale_root
            if round_index == NS_STEPS - 1:
                mixed = factor * mixed
            halves.append(mixed.astype(jnp.bfloat16))
        iterate = lax.dynamic_update_slice_in_dim(
            lax.dynamic_update_slice_in_dim(jnp.zeros_like(current), halves[0], mine, 0),
            halves[1],
            theirs,
            0,
        )
    return (iterate, first_scale)


def with_scale_row(blocks, scale):
    high = scale.astype(jnp.bfloat16)
    low = (scale - high.astype(jnp.float32)).astype(jnp.bfloat16)
    lanes = lax.broadcasted_iota(jnp.int32, (blocks.shape[0], 1, blocks.shape[2]), 2)
    row = jnp.where(lanes == 0, high, jnp.where(lanes == 1, low, jnp.zeros((), jnp.bfloat16)))
    return jnp.concatenate([blocks, row], axis=1)


def scale_of_row(returned):
    row = returned[:, -1, :2].astype(jnp.float32)
    return row[:, 0] + row[:, 1]


def local(
    square_grad,
    square_state,
    swiglu_grad,
    swiglu_state,
    square_order,
    swiglu_order,
    owners,
    vector_values,
    vector_grad,
    vector_first,
    vector_second,
    embed_values,
    embed_grad,
    embed_first,
    embed_second,
    embed_ranges,
):
    wide_count = lax.axis_size("dp")
    n_dev = wide_count * 2
    d = lax.axis_index("dp")
    t = lax.axis_index("tensor")
    n_sq = square_grad.shape[0]
    n_sw = swiglu_grad.shape[0]
    flat_rows = D // n_dev
    out_rows = D // wide_count
    square_next, square_send = momentum_terms(square_grad, square_state)
    swiglu_next, swiglu_send = momentum_terms(swiglu_grad, swiglu_state)
    sq_pieces = square_send.reshape(n_sq, flat_rows, D)
    sw_pieces = swiglu_send.reshape(n_sw, flat_rows, FF)

    half = FF // 2
    sq_halves = jnp.pad(
        sq_pieces.reshape(n_sq, flat_rows, 2, D // 2).transpose(0, 2, 1, 3),
        ((0, 0), (0, 0), (0, 0), (0, half - D // 2)),
    )
    sw_halves = sw_pieces.reshape(n_sw, flat_rows, 2, half).transpose(0, 2, 1, 3)
    outgoing = jnp.pad(
        jnp.concatenate([sq_halves, sw_halves], axis=0),
        ((0, wide_count - n_sq - n_sw), (0, 0), (0, 0), (0, 0)),
    )
    arrived = lax.all_to_all(
        outgoing.reshape(D, half), ("dp", "tensor"), split_axis=0, concat_axis=0, tiled=True
    )

    is_sq = d < n_sq
    is_sw = (d >= n_sq) & (d < n_sq + n_sw)
    factor = jnp.where(is_sq, jnp.float32(math.sqrt(D)), jnp.float32(math.sqrt(FF)))
    iterate, first_scale = orthogonalize(arrived, factor)

    returned = lax.all_to_all(
        iterate.reshape(wide_count, out_rows, half),
        "dp",
        split_axis=0,
        concat_axis=0,
        tiled=True,
    )
    returned_sq = returned[:n_sq, :, : D // 2]
    returned_sw = returned[n_sq : n_sq + n_sw]

    inv_sq = inverse_of(square_order)
    inv_sw = inverse_of(swiglu_order)
    square_update = returned_sq[inv_sq][:, :out_rows]
    swiglu_update = returned_sw[inv_sw][:, :out_rows]

    scale_blocks = lax.all_to_all(
        jnp.broadcast_to(first_scale, (wide_count, 8, 128)),
        "dp",
        split_axis=0,
        concat_axis=0,
        tiled=True,
    )
    slot_scales = scale_blocks[: n_sq + n_sw, 0, 0]
    slot_norms = 0.5 * jnp.log(slot_scales)
    matrix_slot = jnp.concatenate([inv_sq, n_sq + inv_sw])
    matrix_norms = slot_norms[matrix_slot]
    owner_norms = jnp.sum(jnp.where(owners == d, matrix_norms, 0.0)).reshape(1)

    vector_step, first_vector, second_vector = adamw_terms(
        vector_values, vector_grad, vector_first, vector_second
    )
    embed_rows = embed_values.shape[0]
    row_numbers = d * embed_rows + jnp.arange(embed_rows, dtype=jnp.int32)
    inside = (row_numbers[:, None] >= embed_ranges[None, :, 0]) & (
        row_numbers[:, None] < embed_ranges[None, :, 1]
    )
    row_live = jnp.sum(inside.astype(jnp.int32), axis=1) > 0
    direction, first_next, second_next = adamw_terms(
        embed_values, embed_grad, embed_first, embed_second
    )
    embed_step = jnp.where(row_live[:, None], direction, 0.0)
    first_embed = jnp.where(row_live[:, None], first_next, embed_first)
    second_embed = jnp.where(row_live[:, None], second_next, embed_second)
    return (
        square_next,
        swiglu_next,
        square_update,
        swiglu_update,
        owner_norms,
        vector_step,
        first_vector,
        second_vector,
        embed_step,
        first_embed,
        second_embed,
    )


def solution(mesh):
    placed = (
        P(None, ("dp", "tensor")),
        P(None, ("dp", "tensor")),
        P(None, ("dp", "tensor")),
        P(None, ("dp", "tensor")),
        P(),
        P(),
        P(),
        P(("dp", "tensor")),
        P(("dp", "tensor")),
        P(("dp", "tensor")),
        P(("dp", "tensor")),
        P("dp", "tensor"),
        P("dp", "tensor"),
        P("dp", "tensor"),
        P("dp", "tensor"),
        P(),
    )
    return jax.shard_map(
        local,
        mesh=mesh,
        in_specs=placed,
        out_specs=(
            P(None, ("dp", "tensor")),
            P(None, ("dp", "tensor")),
            P(None, "dp", "tensor"),
            P(None, "dp", "tensor"),
            P("dp"),
            P(("dp", "tensor")),
            P(("dp", "tensor")),
            P(("dp", "tensor")),
            P("dp", "tensor"),
            P("dp", "tensor"),
            P("dp", "tensor"),
        ),
        check_vma=False,
    )
```

```python
import math

import jax
import jax.numpy as jnp
from jax import lax
from jax.experimental import pallas as pl
from jax.experimental.pallas import tpu as pltpu
from jax.sharding import PartitionSpec as P

D = 1536
FF = 4096
NS_STEPS = 2
MESH = pl.DeviceIdType.MESH

QUINTIC_LINEAR = 3.4445
QUINTIC_CUBIC = -4.775
QUINTIC_FIFTH = 2.0315
MOMENTUM = 0.95
BIAS_FIRST = 1.0 - 0.9**10
BIAS_SECOND = 1.0 - 0.95**10


def momentum_terms(gradient, state):
    state_next = MOMENTUM * state + gradient
    return (state_next, (gradient + MOMENTUM * state_next).astype(jnp.bfloat16))


def adamw_terms(values, gradient, first, second):
    first_next = 0.9 * first + 0.1 * gradient
    second_next = 0.95 * second + 0.05 * gradient * gradient
    direction = (
        first_next / BIAS_FIRST / (jnp.sqrt(second_next / BIAS_SECOND) + 1e-08) + 0.1 * values
    )
    return (direction, first_next, second_next)


def inverse_of(order):
    count = order.shape[0]
    return jnp.zeros((count,), jnp.int32).at[order].set(jnp.arange(count, dtype=jnp.int32))


def device_barrier(n_dev, me, pairs):
    barrier = pltpu.get_barrier_semaphore()
    t = lax.axis_index("tensor")

    def signal(k, carry):
        target = lax.rem(me + k, n_dev)
        if pairs:
            device = (target // 2, lax.rem(target, 2))
        else:
            device = (target, t)
        pl.semaphore_signal(barrier, inc=1, device_id=device, device_id_type=MESH)
        return carry

    lax.fori_loop(1, n_dev, signal, 0)
    pl.semaphore_wait(barrier, n_dev - 1)


def scatter_kernel(n_sq, n_sw, sq_ref, sw_ref, zero_ref, out_ref, comb_sq, comb_sw, send_sem, recv_sem, pair_sem):
    del zero_ref
    d = lax.axis_index("dp")
    t = lax.axis_index("tensor")
    n_dev = lax.axis_size("dp") * 2
    n_slots = n_sq + n_sw
    me = d * 2 + t
    sq_w = comb_sq.shape[3]
    sw_w = comb_sw.shape[3]
    device_barrier(n_dev, me, True)

    other = 1 - t
    swap_sq = pltpu.make_async_remote_copy(
        src_ref=sq_ref.at[:, :, pl.ds(pl.multiple_of(other * sq_w, 128), sq_w)],
        dst_ref=comb_sq.at[:, t],
        send_sem=pair_sem.at[0],
        recv_sem=pair_sem.at[1],
        device_id=(d, other),
        device_id_type=MESH,
    )
    swap_sw = pltpu.make_async_remote_copy(
        src_ref=sw_ref.at[:, :, pl.ds(pl.multiple_of(other * sw_w, 128), sw_w)],
        dst_ref=comb_sw.at[:, t],
        send_sem=pair_sem.at[2],
        recv_sem=pair_sem.at[3],
        device_id=(d, other),
        device_id_type=MESH,
    )
    keep_sq = pltpu.make_async_copy(
        sq_ref.at[:, :, pl.ds(pl.multiple_of(t * sq_w, 128), sq_w)], comb_sq.at[:, t], pair_sem.at[4]
    )
    keep_sw = pltpu.make_async_copy(
        sw_ref.at[:, :, pl.ds(pl.multiple_of(t * sw_w, 128), sw_w)], comb_sw.at[:, t], pair_sem.at[5]
    )
    swap_sq.start()
    swap_sw.start()
    keep_sq.start()
    keep_sw.start()
    keep_sq.wait()
    keep_sw.wait()
    pltpu.make_async_copy(comb_sq.at[:, other], comb_sq.at[:, other], pair_sem.at[1]).wait()
    pltpu.make_async_copy(comb_sw.at[:, other], comb_sw.at[:, other], pair_sem.at[3]).wait()
    swap_sq.wait_send()
    swap_sw.wait_send()

    def sq_copy(g):
        return pltpu.make_async_remote_copy(
            src_ref=comb_sq.at[g],
            dst_ref=out_ref.at[d, :, :, pl.ds(0, sq_w)],
            send_sem=send_sem.at[g],
            recv_sem=recv_sem.at[0],
            device_id=(g, t),
            device_id_type=MESH,
        )

    def sw_copy(g):
        return pltpu.make_async_remote_copy(
            src_ref=comb_sw.at[g - n_sq],
            dst_ref=out_ref.at[d, :, :, pl.ds(0, sw_w)],
            send_sem=send_sem.at[g],
            recv_sem=recv_sem.at[0],
            device_id=(g, t),
            device_id_type=MESH,
        )

    def start(k, carry):
        g = lax.rem(k + d, n_slots)
        local = g == d

        @pl.when(local & (g < n_sq))
        def _():
            pltpu.make_async_copy(
                comb_sq.at[g], out_ref.at[d, :, :, pl.ds(0, sq_w)], recv_sem.at[0]
            ).start()

        @pl.when(local & (g >= n_sq))
        def _():
            pltpu.make_async_copy(
                comb_sw.at[g - n_sq], out_ref.at[d, :, :, pl.ds(0, sw_w)], recv_sem.at[0]
            ).start()

        @pl.when(jnp.logical_not(local) & (g < n_sq))
        def _():
            sq_copy(g).start()

        @pl.when(jnp.logical_not(local) & (g >= n_sq))
        def _():
            sw_copy(g).start()

        return carry

    lax.fori_loop(0, n_slots, start, 0)

    @pl.when(d < n_sq)
    def _():
        region = out_ref.at[:, :, :, pl.ds(0, sq_w)]
        pltpu.make_async_copy(region, region, recv_sem.at[0]).wait()

    @pl.when((d >= n_sq) & (d < n_slots))
    def _():
        region = out_ref.at[:, :, :, pl.ds(0, sw_w)]
        pltpu.make_async_copy(region, region, recv_sem.at[0]).wait()

    def wait(g, carry):
        @pl.when((g != d) & (g < n_sq))
        def _():
            sq_copy(g).wait_send()

        @pl.when((g != d) & (g >= n_sq))
        def _():
            sw_copy(g).wait_send()

        return carry

    lax.fori_loop(0, n_slots, wait, 0)


def gather_kernel(n_sq, n_sw, it_ref, osq_ref, osw_ref, send_sem, recv_sem):
    d = lax.axis_index("dp")
    t = lax.axis_index("tensor")
    n_dp = lax.axis_size("dp")
    device_barrier(n_dp, d, False)
    is_sq = d < n_sq
    is_sw = (d >= n_sq) & (d < n_sq + n_sw)
    sq_w = osq_ref.shape[2]
    sw_w = osw_ref.shape[2]
    j_sq = jnp.minimum(d, n_sq - 1)
    j_sw = jnp.clip(d - n_sq, 0, n_sw - 1)

    def sq_copy(r):
        return pltpu.make_async_remote_copy(
            src_ref=it_ref.at[r, :, pl.ds(0, sq_w)],
            dst_ref=osq_ref.at[j_sq],
            send_sem=send_sem.at[r],
            recv_sem=recv_sem.at[0],
            device_id=(r, t),
            device_id_type=MESH,
        )

    def sw_copy(r):
        return pltpu.make_async_remote_copy(
            src_ref=it_ref.at[r, :, pl.ds(0, sw_w)],
            dst_ref=osw_ref.at[j_sw],
            send_sem=send_sem.at[r],
            recv_sem=recv_sem.at[1],
            device_id=(r, t),
            device_id_type=MESH,
        )

    @pl.when(is_sq)
    def _():
        def start(k, carry):
            r = lax.rem(d + k, n_dp)

            @pl.when(r == d)
            def _():
                pltpu.make_async_copy(
                    it_ref.at[d, :, pl.ds(0, sq_w)], osq_ref.at[j_sq], recv_sem.at[0]
                ).start()

            @pl.when(r != d)
            def _():
                sq_copy(r).start()

            return carry

        lax.fori_loop(0, n_dp, start, 0)

    @pl.when(is_sw)
    def _():
        def start(k, carry):
            r = lax.rem(d + k, n_dp)

            @pl.when(r == d)
            def _():
                pltpu.make_async_copy(
                    it_ref.at[d, :, pl.ds(0, sw_w)], osw_ref.at[j_sw], recv_sem.at[1]
                ).start()

            @pl.when(r != d)
            def _():
                sw_copy(r).start()

            return carry

        lax.fori_loop(0, n_dp, start, 0)

    pltpu.make_async_copy(osq_ref, osq_ref, recv_sem.at[0]).wait()
    pltpu.make_async_copy(osw_ref, osw_ref, recv_sem.at[1]).wait()

    @pl.when(is_sq)
    def _():
        def wait(r, carry):
            @pl.when(r != d)
            def _():
                sq_copy(r).wait_send()

            return carry

        lax.fori_loop(0, n_dp, wait, 0)

    @pl.when(is_sw)
    def _():
        def wait(r, carry):
            @pl.when(r != d)
            def _():
                sw_copy(r).wait_send()

            return carry

        lax.fori_loop(0, n_dp, wait, 0)


def swap_halves(x):
    return lax.ppermute(x, "tensor", perm=[(0, 1), (1, 0)])


def orthogonalize(arrived, factor):
    t = lax.axis_index("tensor")
    rows = arrived.shape[0] // 2
    mine = pl.multiple_of(t * rows, rows)
    theirs = pl.multiple_of((1 - t) * rows, rows)
    iterate = arrived
    first_scale = jnp.float32(1.0)
    for round_index in range(NS_STEPS):
        current = iterate
        their_rows = lax.dynamic_slice_in_dim(current, theirs, rows, 0)
        my_rows = lax.dynamic_slice_in_dim(current, mine, rows, 0)
        sent = swap_halves(
            jnp.einsum("rc,sc->rs", their_rows, current, preferred_element_type=jnp.float32)
        )
        kept = lax.optimization_barrier(
            jnp.einsum("rc,sc->rs", my_rows, current, preferred_element_type=jnp.float32)
        )
        gram_part = kept + sent
        if round_index == 0:
            squares_total = lax.psum(jnp.sum(gram_part * gram_part), "tensor")
            gram_scale = jnp.sqrt(squares_total) + 1e-06
            first_scale = gram_scale
        else:
            gram_scale = jnp.float32(1.0)
        normed_part = (gram_part / gram_scale).astype(jnp.bfloat16)
        normed_other = swap_halves(normed_part)
        squared = lax.optimization_barrier(
            jnp.dot(
                lax.dynamic_slice_in_dim(normed_part, mine, rows, 1),
                normed_part,
                preferred_element_type=jnp.float32,
            )
        ) + jnp.dot(
            lax.dynamic_slice_in_dim(normed_part, theirs, rows, 1),
            normed_other,
            preferred_element_type=jnp.float32,
        )
        polynomial = (
            QUINTIC_CUBIC * normed_part.astype(jnp.float32) + QUINTIC_FIFTH * squared
        ).astype(jnp.bfloat16)
        poly_other = swap_halves(polynomial)
        product_mine = lax.optimization_barrier(
            jnp.dot(polynomial, current, preferred_element_type=jnp.float32)
        )
        product_other = jnp.dot(poly_other, current, preferred_element_type=jnp.float32)
        scale_root = jnp.sqrt(gram_scale)
        halves = []
        for rows_here, product_here in ((my_rows, product_mine), (their_rows, product_other)):
            mixed = (QUINTIC_LINEAR * rows_here.astype(jnp.float32) + product_here) / scale_root
            if round_index == NS_STEPS - 1:
                mixed = factor * mixed
            halves.append(mixed.astype(jnp.bfloat16))
        iterate = lax.dynamic_update_slice_in_dim(
            lax.dynamic_update_slice_in_dim(jnp.zeros_like(current), halves[0], mine, 0),
            halves[1],
            theirs,
            0,
        )
    return (iterate, first_scale)


def with_scale_row(blocks, scale):
    high = scale.astype(jnp.bfloat16)
    low = (scale - high.astype(jnp.float32)).astype(jnp.bfloat16)
    lanes = lax.broadcasted_iota(jnp.int32, (blocks.shape[0], 1, blocks.shape[2]), 2)
    row = jnp.where(lanes == 0, high, jnp.where(lanes == 1, low, jnp.zeros((), jnp.bfloat16)))
    return jnp.concatenate([blocks, row], axis=1)


def scale_of_row(returned):
    row = returned[:, -1, :2].astype(jnp.float32)
    return row[:, 0] + row[:, 1]


def local(
    square_grad,
    square_state,
    swiglu_grad,
    swiglu_state,
    square_order,
    swiglu_order,
    owners,
    vector_values,
    vector_grad,
    vector_first,
    vector_second,
    embed_values,
    embed_grad,
    embed_first,
    embed_second,
    embed_ranges,
):
    wide_count = lax.axis_size("dp")
    n_dev = wide_count * 2
    d = lax.axis_index("dp")
    t = lax.axis_index("tensor")
    n_sq = square_grad.shape[0]
    n_sw = swiglu_grad.shape[0]
    flat_rows = D // n_dev
    out_rows = D // wide_count
    _, square_send = momentum_terms(*lax.optimization_barrier((square_grad, square_state)))
    _, swiglu_send = momentum_terms(*lax.optimization_barrier((swiglu_grad, swiglu_state)))
    square_next = MOMENTUM * square_state + square_grad
    swiglu_next = MOMENTUM * swiglu_state + swiglu_grad
    sq_pieces = square_send.reshape(n_sq, flat_rows, D)
    sw_pieces = swiglu_send.reshape(n_sw, flat_rows, FF)

    half = FF // 2
    sq_halves = jnp.pad(
        sq_pieces.reshape(n_sq, flat_rows, 2, D // 2).transpose(0, 2, 1, 3),
        ((0, 0), (0, 0), (0, 0), (0, half - D // 2)),
    )
    sw_halves = sw_pieces.reshape(n_sw, flat_rows, 2, half).transpose(0, 2, 1, 3)
    outgoing = jnp.pad(
        jnp.concatenate([sq_halves, sw_halves], axis=0),
        ((0, wide_count - n_sq - n_sw), (0, 0), (0, 0), (0, 0)),
    )
    arrived = lax.all_to_all(
        outgoing.reshape(D, half), ("dp", "tensor"), split_axis=0, concat_axis=0, tiled=True
    )

    is_sq = d < n_sq
    is_sw = (d >= n_sq) & (d < n_sq + n_sw)
    factor = jnp.where(is_sq, jnp.float32(math.sqrt(D)), jnp.float32(math.sqrt(FF)))
    iterate, first_scale = orthogonalize(arrived, factor)

    returned = lax.all_to_all(
        iterate.reshape(wide_count, out_rows, half),
        "dp",
        split_axis=0,
        concat_axis=0,
        tiled=True,
    )
    returned_sq = returned[:n_sq, :, : D // 2]
    returned_sw = returned[n_sq : n_sq + n_sw]

    inv_sq = inverse_of(square_order)
    inv_sw = inverse_of(swiglu_order)
    square_update = returned_sq[inv_sq][:, :out_rows]
    swiglu_update = returned_sw[inv_sw][:, :out_rows]

    scale_blocks = lax.all_to_all(
        jnp.broadcast_to(first_scale, (wide_count, 8, 128)),
        "dp",
        split_axis=0,
        concat_axis=0,
        tiled=True,
    )
    slot_scales = scale_blocks[: n_sq + n_sw, 0, 0]
    slot_norms = 0.5 * jnp.log(slot_scales)
    matrix_slot = jnp.concatenate([inv_sq, n_sq + inv_sw])
    matrix_norms = slot_norms[matrix_slot]
    owner_norms = jnp.sum(jnp.where(owners == d, matrix_norms, 0.0)).reshape(1)

    vector_step, first_vector, second_vector = adamw_terms(
        vector_values, vector_grad, vector_first, vector_second
    )
    embed_rows = embed_values.shape[0]
    row_numbers = d * embed_rows + jnp.arange(embed_rows, dtype=jnp.int32)
    inside = (row_numbers[:, None] >= embed_ranges[None, :, 0]) & (
        row_numbers[:, None] < embed_ranges[None, :, 1]
    )
    row_live = jnp.sum(inside.astype(jnp.int32), axis=1) > 0
    direction, first_next, second_next = adamw_terms(
        embed_values, embed_grad, embed_first, embed_second
    )
    embed_step = jnp.where(row_live[:, None], direction, 0.0)
    first_embed = jnp.where(row_live[:, None], first_next, embed_first)
    second_embed = jnp.where(row_live[:, None], second_next, embed_second)
    return (
        square_next,
        swiglu_next,
        square_update,
        swiglu_update,
        owner_norms,
        vector_step,
        first_vector,
        second_vector,
        embed_step,
        first_embed,
        second_embed,
    )


def solution(mesh):
    placed = (
        P(None, ("dp", "tensor")),
        P(None, ("dp", "tensor")),
        P(None, ("dp", "tensor")),
        P(None, ("dp", "tensor")),
        P(),
        P(),
        P(),
        P(("dp", "tensor")),
        P(("dp", "tensor")),
        P(("dp", "tensor")),
        P(("dp", "tensor")),
        P("dp", "tensor"),
        P("dp", "tensor"),
        P("dp", "tensor"),
        P("dp", "tensor"),
        P(),
    )
    return jax.shard_map(
        local,
        mesh=mesh,
        in_specs=placed,
        out_specs=(
            P(None, ("dp", "tensor")),
            P(None, ("dp", "tensor")),
            P(None, "dp", "tensor"),
            P(None, "dp", "tensor"),
            P("dp"),
            P(("dp", "tensor")),
            P(("dp", "tensor")),
            P(("dp", "tensor")),
            P("dp", "tensor"),
            P("dp", "tensor"),
            P("dp", "tensor"),
        ),
        check_vma=False,
    )
```

```python
import math

import jax
import jax.numpy as jnp
from jax import lax
from jax.experimental import pallas as pl
from jax.experimental.pallas import tpu as pltpu
from jax.sharding import PartitionSpec as P

D = 1536
FF = 4096
NS_STEPS = 2
MESH = pl.DeviceIdType.MESH

QUINTIC_LINEAR = 3.4445
QUINTIC_CUBIC = -4.775
QUINTIC_FIFTH = 2.0315
MOMENTUM = 0.95
BIAS_FIRST = 1.0 - 0.9**10
BIAS_SECOND = 1.0 - 0.95**10


def momentum_terms(gradient, state):
    state_next = MOMENTUM * state + gradient
    return (state_next, (gradient + MOMENTUM * state_next).astype(jnp.bfloat16))


def adamw_terms(values, gradient, first, second):
    first_next = 0.9 * first + 0.1 * gradient
    second_next = 0.95 * second + 0.05 * gradient * gradient
    direction = (
        first_next / BIAS_FIRST / (jnp.sqrt(second_next / BIAS_SECOND) + 1e-08) + 0.1 * values
    )
    return (direction, first_next, second_next)


def inverse_of(order):
    count = order.shape[0]
    return jnp.zeros((count,), jnp.int32).at[order].set(jnp.arange(count, dtype=jnp.int32))


def device_barrier(n_dev, me, pairs):
    barrier = pltpu.get_barrier_semaphore()
    t = lax.axis_index("tensor")

    def signal(k, carry):
        target = lax.rem(me + k, n_dev)
        if pairs:
            device = (target // 2, lax.rem(target, 2))
        else:
            device = (target, t)
        pl.semaphore_signal(barrier, inc=1, device_id=device, device_id_type=MESH)
        return carry

    lax.fori_loop(1, n_dev, signal, 0)
    pl.semaphore_wait(barrier, n_dev - 1)


def scatter_kernel(n_sq, n_sw, sq_ref, sw_ref, zero_ref, out_ref, comb_sq, comb_sw, send_sem, recv_sem, pair_sem):
    del zero_ref
    d = lax.axis_index("dp")
    t = lax.axis_index("tensor")
    n_dev = lax.axis_size("dp") * 2
    n_slots = n_sq + n_sw
    me = d * 2 + t
    sq_w = comb_sq.shape[3]
    sw_w = comb_sw.shape[3]
    device_barrier(n_dev, me, True)

    other = 1 - t
    swap_sq = pltpu.make_async_remote_copy(
        src_ref=sq_ref.at[:, :, pl.ds(pl.multiple_of(other * sq_w, 128), sq_w)],
        dst_ref=comb_sq.at[:, t],
        send_sem=pair_sem.at[0],
        recv_sem=pair_sem.at[1],
        device_id=(d, other),
        device_id_type=MESH,
    )
    swap_sw = pltpu.make_async_remote_copy(
        src_ref=sw_ref.at[:, :, pl.ds(pl.multiple_of(other * sw_w, 128), sw_w)],
        dst_ref=comb_sw.at[:, t],
        send_sem=pair_sem.at[2],
        recv_sem=pair_sem.at[3],
        device_id=(d, other),
        device_id_type=MESH,
    )
    keep_sq = pltpu.make_async_copy(
        sq_ref.at[:, :, pl.ds(pl.multiple_of(t * sq_w, 128), sq_w)], comb_sq.at[:, t], pair_sem.at[4]
    )
    keep_sw = pltpu.make_async_copy(
        sw_ref.at[:, :, pl.ds(pl.multiple_of(t * sw_w, 128), sw_w)], comb_sw.at[:, t], pair_sem.at[5]
    )
    swap_sq.start()
    swap_sw.start()
    keep_sq.start()
    keep_sw.start()
    keep_sq.wait()
    keep_sw.wait()
    pltpu.make_async_copy(comb_sq.at[:, other], comb_sq.at[:, other], pair_sem.at[1]).wait()
    pltpu.make_async_copy(comb_sw.at[:, other], comb_sw.at[:, other], pair_sem.at[3]).wait()
    swap_sq.wait_send()
    swap_sw.wait_send()

    def sq_copy(g):
        return pltpu.make_async_remote_copy(
            src_ref=comb_sq.at[g],
            dst_ref=out_ref.at[d, :, :, pl.ds(0, sq_w)],
            send_sem=send_sem.at[g],
            recv_sem=recv_sem.at[0],
            device_id=(g, t),
            device_id_type=MESH,
        )

    def sw_copy(g):
        return pltpu.make_async_remote_copy(
            src_ref=comb_sw.at[g - n_sq],
            dst_ref=out_ref.at[d, :, :, pl.ds(0, sw_w)],
            send_sem=send_sem.at[g],
            recv_sem=recv_sem.at[0],
            device_id=(g, t),
            device_id_type=MESH,
        )

    def start(k, carry):
        g = lax.rem(k + d, n_slots)
        local = g == d

        @pl.when(local & (g < n_sq))
        def _():
            pltpu.make_async_copy(
                comb_sq.at[g], out_ref.at[d, :, :, pl.ds(0, sq_w)], recv_sem.at[0]
            ).start()

        @pl.when(local & (g >= n_sq))
        def _():
            pltpu.make_async_copy(
                comb_sw.at[g - n_sq], out_ref.at[d, :, :, pl.ds(0, sw_w)], recv_sem.at[0]
            ).start()

        @pl.when(jnp.logical_not(local) & (g < n_sq))
        def _():
            sq_copy(g).start()

        @pl.when(jnp.logical_not(local) & (g >= n_sq))
        def _():
            sw_copy(g).start()

        return carry

    lax.fori_loop(0, n_slots, start, 0)

    @pl.when(d < n_sq)
    def _():
        region = out_ref.at[:, :, :, pl.ds(0, sq_w)]
        pltpu.make_async_copy(region, region, recv_sem.at[0]).wait()

    @pl.when((d >= n_sq) & (d < n_slots))
    def _():
        region = out_ref.at[:, :, :, pl.ds(0, sw_w)]
        pltpu.make_async_copy(region, region, recv_sem.at[0]).wait()

    def wait(g, carry):
        @pl.when((g != d) & (g < n_sq))
        def _():
            sq_copy(g).wait_send()

        @pl.when((g != d) & (g >= n_sq))
        def _():
            sw_copy(g).wait_send()

        return carry

    lax.fori_loop(0, n_slots, wait, 0)


def gather_kernel(n_sq, n_sw, it_ref, osq_ref, osw_ref, send_sem, recv_sem):
    d = lax.axis_index("dp")
    t = lax.axis_index("tensor")
    n_dp = lax.axis_size("dp")
    device_barrier(n_dp, d, False)
    is_sq = d < n_sq
    is_sw = (d >= n_sq) & (d < n_sq + n_sw)
    sq_w = osq_ref.shape[2]
    sw_w = osw_ref.shape[2]
    j_sq = jnp.minimum(d, n_sq - 1)
    j_sw = jnp.clip(d - n_sq, 0, n_sw - 1)

    def sq_copy(r):
        return pltpu.make_async_remote_copy(
            src_ref=it_ref.at[r, :, pl.ds(0, sq_w)],
            dst_ref=osq_ref.at[j_sq],
            send_sem=send_sem.at[r],
            recv_sem=recv_sem.at[0],
            device_id=(r, t),
            device_id_type=MESH,
        )

    def sw_copy(r):
        return pltpu.make_async_remote_copy(
            src_ref=it_ref.at[r, :, pl.ds(0, sw_w)],
            dst_ref=osw_ref.at[j_sw],
            send_sem=send_sem.at[r],
            recv_sem=recv_sem.at[1],
            device_id=(r, t),
            device_id_type=MESH,
        )

    @pl.when(is_sq)
    def _():
        def start(k, carry):
            r = lax.rem(d + k, n_dp)

            @pl.when(r == d)
            def _():
                pltpu.make_async_copy(
                    it_ref.at[d, :, pl.ds(0, sq_w)], osq_ref.at[j_sq], recv_sem.at[0]
                ).start()

            @pl.when(r != d)
            def _():
                sq_copy(r).start()

            return carry

        lax.fori_loop(0, n_dp, start, 0)

    @pl.when(is_sw)
    def _():
        def start(k, carry):
            r = lax.rem(d + k, n_dp)

            @pl.when(r == d)
            def _():
                pltpu.make_async_copy(
                    it_ref.at[d, :, pl.ds(0, sw_w)], osw_ref.at[j_sw], recv_sem.at[1]
                ).start()

            @pl.when(r != d)
            def _():
                sw_copy(r).start()

            return carry

        lax.fori_loop(0, n_dp, start, 0)

    pltpu.make_async_copy(osq_ref, osq_ref, recv_sem.at[0]).wait()
    pltpu.make_async_copy(osw_ref, osw_ref, recv_sem.at[1]).wait()

    @pl.when(is_sq)
    def _():
        def wait(r, carry):
            @pl.when(r != d)
            def _():
                sq_copy(r).wait_send()

            return carry

        lax.fori_loop(0, n_dp, wait, 0)

    @pl.when(is_sw)
    def _():
        def wait(r, carry):
            @pl.when(r != d)
            def _():
                sw_copy(r).wait_send()

            return carry

        lax.fori_loop(0, n_dp, wait, 0)


def swap_halves(x):
    return lax.ppermute(x, "tensor", perm=[(0, 1), (1, 0)])


def orthogonalize(arrived, factor):
    t = lax.axis_index("tensor")
    rows = arrived.shape[0] // 2
    mine = pl.multiple_of(t * rows, rows)
    theirs = pl.multiple_of((1 - t) * rows, rows)
    iterate = arrived
    first_scale = jnp.float32(1.0)
    for round_index in range(NS_STEPS):
        current = iterate
        their_rows = lax.dynamic_slice_in_dim(current, theirs, rows, 0)
        my_rows = lax.dynamic_slice_in_dim(current, mine, rows, 0)
        sent = swap_halves(
            jnp.einsum("rc,sc->rs", their_rows, current, preferred_element_type=jnp.float32)
        )
        kept = lax.optimization_barrier(
            jnp.einsum("rc,sc->rs", my_rows, current, preferred_element_type=jnp.float32)
        )
        gram_part = kept + sent
        if round_index == 0:
            squares_total = lax.psum(jnp.sum(gram_part * gram_part), "tensor")
            gram_scale = jnp.sqrt(squares_total) + 1e-06
            first_scale = gram_scale
        else:
            gram_scale = jnp.float32(1.0)
        normed_part = (gram_part / gram_scale).astype(jnp.bfloat16)
        normed_other = swap_halves(normed_part)
        squared = lax.optimization_barrier(
            jnp.dot(
                lax.dynamic_slice_in_dim(normed_part, mine, rows, 1),
                normed_part,
                preferred_element_type=jnp.float32,
            )
        ) + jnp.dot(
            lax.dynamic_slice_in_dim(normed_part, theirs, rows, 1),
            normed_other,
            preferred_element_type=jnp.float32,
        )
        polynomial = (
            QUINTIC_CUBIC * normed_part.astype(jnp.float32) + QUINTIC_FIFTH * squared
        ).astype(jnp.bfloat16)
        poly_other = swap_halves(polynomial)
        product_mine = lax.optimization_barrier(
            jnp.dot(polynomial, current, preferred_element_type=jnp.float32)
        )
        product_other = jnp.dot(poly_other, current, preferred_element_type=jnp.float32)
        scale_root = jnp.sqrt(gram_scale)
        halves = []
        for rows_here, product_here in ((my_rows, product_mine), (their_rows, product_other)):
            mixed = (QUINTIC_LINEAR * rows_here.astype(jnp.float32) + product_here) / scale_root
            if round_index == NS_STEPS - 1:
                mixed = factor * mixed
            halves.append(mixed.astype(jnp.bfloat16))
        iterate = lax.dynamic_update_slice_in_dim(
            lax.dynamic_update_slice_in_dim(jnp.zeros_like(current), halves[0], mine, 0),
            halves[1],
            theirs,
            0,
        )
    return (iterate, first_scale)


def with_scale_columns(blocks, scale):
    high = scale.astype(jnp.bfloat16)
    low = (scale - high.astype(jnp.float32)).astype(jnp.bfloat16)
    shape = (blocks.shape[0], blocks.shape[1], 128)
    rows = lax.broadcasted_iota(jnp.int32, shape, 1)
    lanes = lax.broadcasted_iota(jnp.int32, shape, 2)
    extra = jnp.where(
        rows == 0,
        jnp.where(lanes == 0, high, jnp.where(lanes == 1, low, jnp.zeros((), jnp.bfloat16))),
        jnp.zeros((), jnp.bfloat16),
    )
    return jnp.concatenate([blocks, extra], axis=2)


def with_scale_row(blocks, scale):
    high = scale.astype(jnp.bfloat16)
    low = (scale - high.astype(jnp.float32)).astype(jnp.bfloat16)
    lanes = lax.broadcasted_iota(jnp.int32, (blocks.shape[0], 1, blocks.shape[2]), 2)
    row = jnp.where(lanes == 0, high, jnp.where(lanes == 1, low, jnp.zeros((), jnp.bfloat16)))
    return jnp.concatenate([blocks, row], axis=1)


def scale_of_row(returned):
    row = returned[:, -1, :2].astype(jnp.float32)
    return row[:, 0] + row[:, 1]


def local(
    square_grad,
    square_state,
    swiglu_grad,
    swiglu_state,
    square_order,
    swiglu_order,
    owners,
    vector_values,
    vector_grad,
    vector_first,
    vector_second,
    embed_values,
    embed_grad,
    embed_first,
    embed_second,
    embed_ranges,
):
    wide_count = lax.axis_size("dp")
    n_dev = wide_count * 2
    d = lax.axis_index("dp")
    t = lax.axis_index("tensor")
    n_sq = square_grad.shape[0]
    n_sw = swiglu_grad.shape[0]
    flat_rows = D // n_dev
    out_rows = D // wide_count
    square_next, square_send = momentum_terms(square_grad, square_state)
    swiglu_next, swiglu_send = momentum_terms(swiglu_grad, swiglu_state)
    sq_pieces = square_send.reshape(n_sq, flat_rows, D)
    sw_pieces = swiglu_send.reshape(n_sw, flat_rows, FF)

    half = FF // 2
    sq_halves = jnp.pad(
        sq_pieces.reshape(n_sq, flat_rows, 2, D // 2).transpose(0, 2, 1, 3),
        ((0, 0), (0, 0), (0, 0), (0, half - D // 2)),
    )
    sw_halves = sw_pieces.reshape(n_sw, flat_rows, 2, half).transpose(0, 2, 1, 3)
    outgoing = jnp.pad(
        jnp.concatenate([sq_halves, sw_halves], axis=0),
        ((0, wide_count - n_sq - n_sw), (0, 0), (0, 0), (0, 0)),
    )
    arrived = lax.all_to_all(
        outgoing.reshape(D, half), ("dp", "tensor"), split_axis=0, concat_axis=0, tiled=True
    )

    is_sq = d < n_sq
    is_sw = (d >= n_sq) & (d < n_sq + n_sw)
    factor = jnp.where(is_sq, jnp.float32(math.sqrt(D)), jnp.float32(math.sqrt(FF)))
    iterate, first_scale = orthogonalize(arrived, factor)

    returned = lax.all_to_all(
        with_scale_columns(iterate.reshape(wide_count, out_rows, half), first_scale),
        "dp",
        split_axis=0,
        concat_axis=0,
        tiled=True,
    )
    returned_sq = returned[:n_sq, :, : D // 2]
    returned_sw = returned[n_sq : n_sq + n_sw, :, :half]

    inv_sq = inverse_of(square_order)
    inv_sw = inverse_of(swiglu_order)
    square_update = returned_sq[inv_sq][:, :out_rows]
    swiglu_update = returned_sw[inv_sw][:, :out_rows]

    scale_pair = returned[: n_sq + n_sw, 0, half : half + 2].astype(jnp.float32)
    slot_scales = scale_pair[:, 0] + scale_pair[:, 1]
    slot_norms = 0.5 * jnp.log(slot_scales)
    matrix_slot = jnp.concatenate([inv_sq, n_sq + inv_sw])
    matrix_norms = slot_norms[matrix_slot]
    owner_norms = jnp.sum(jnp.where(owners == d, matrix_norms, 0.0)).reshape(1)

    vector_step, first_vector, second_vector = adamw_terms(
        vector_values, vector_grad, vector_first, vector_second
    )
    embed_rows = embed_values.shape[0]
    row_numbers = d * embed_rows + jnp.arange(embed_rows, dtype=jnp.int32)
    inside = (row_numbers[:, None] >= embed_ranges[None, :, 0]) & (
        row_numbers[:, None] < embed_ranges[None, :, 1]
    )
    row_live = jnp.sum(inside.astype(jnp.int32), axis=1) > 0
    direction, first_next, second_next = adamw_terms(
        embed_values, embed_grad, embed_first, embed_second
    )
    embed_step = jnp.where(row_live[:, None], direction, 0.0)
    first_embed = jnp.where(row_live[:, None], first_next, embed_first)
    second_embed = jnp.where(row_live[:, None], second_next, embed_second)
    return (
        square_next,
        swiglu_next,
        square_update,
        swiglu_update,
        owner_norms,
        vector_step,
        first_vector,
        second_vector,
        embed_step,
        first_embed,
        second_embed,
    )


def solution(mesh):
    placed = (
        P(None, ("dp", "tensor")),
        P(None, ("dp", "tensor")),
        P(None, ("dp", "tensor")),
        P(None, ("dp", "tensor")),
        P(),
        P(),
        P(),
        P(("dp", "tensor")),
        P(("dp", "tensor")),
        P(("dp", "tensor")),
        P(("dp", "tensor")),
        P("dp", "tensor"),
        P("dp", "tensor"),
        P("dp", "tensor"),
        P("dp", "tensor"),
        P(),
    )
    return jax.shard_map(
        local,
        mesh=mesh,
        in_specs=placed,
        out_specs=(
            P(None, ("dp", "tensor")),
            P(None, ("dp", "tensor")),
            P(None, "dp", "tensor"),
            P(None, "dp", "tensor"),
            P("dp"),
            P(("dp", "tensor")),
            P(("dp", "tensor")),
            P(("dp", "tensor")),
            P("dp", "tensor"),
            P("dp", "tensor"),
            P("dp", "tensor"),
        ),
        check_vma=False,
    )
```

```python
import math

import jax
import jax.numpy as jnp
from jax import lax
from jax.experimental import pallas as pl
from jax.experimental.pallas import tpu as pltpu
from jax.sharding import PartitionSpec as P

D = 1536
FF = 4096
NS_STEPS = 2
MESH = pl.DeviceIdType.MESH

QUINTIC_LINEAR = 3.4445
QUINTIC_CUBIC = -4.775
QUINTIC_FIFTH = 2.0315
MOMENTUM = 0.95
BIAS_FIRST = 1.0 - 0.9**10
BIAS_SECOND = 1.0 - 0.95**10


def momentum_terms(gradient, state):
    state_next = MOMENTUM * state + gradient
    return (state_next, (gradient + MOMENTUM * state_next).astype(jnp.bfloat16))


def adamw_terms(values, gradient, first, second):
    first_next = 0.9 * first + 0.1 * gradient
    second_next = 0.95 * second + 0.05 * gradient * gradient
    direction = (
        first_next / BIAS_FIRST / (jnp.sqrt(second_next / BIAS_SECOND) + 1e-08) + 0.1 * values
    )
    return (direction, first_next, second_next)


def inverse_of(order):
    count = order.shape[0]
    return jnp.zeros((count,), jnp.int32).at[order].set(jnp.arange(count, dtype=jnp.int32))


def device_barrier(n_dev, me, pairs):
    barrier = pltpu.get_barrier_semaphore()
    t = lax.axis_index("tensor")

    def signal(k, carry):
        target = lax.rem(me + k, n_dev)
        if pairs:
            device = (target // 2, lax.rem(target, 2))
        else:
            device = (target, t)
        pl.semaphore_signal(barrier, inc=1, device_id=device, device_id_type=MESH)
        return carry

    lax.fori_loop(1, n_dev, signal, 0)
    pl.semaphore_wait(barrier, n_dev - 1)


def scatter_kernel(n_sq, n_sw, sq_ref, sw_ref, zero_ref, out_ref, comb_sq, comb_sw, send_sem, recv_sem, pair_sem):
    del zero_ref
    d = lax.axis_index("dp")
    t = lax.axis_index("tensor")
    n_dev = lax.axis_size("dp") * 2
    n_slots = n_sq + n_sw
    me = d * 2 + t
    sq_w = comb_sq.shape[3]
    sw_w = comb_sw.shape[3]
    device_barrier(n_dev, me, True)

    other = 1 - t
    swap_sq = pltpu.make_async_remote_copy(
        src_ref=sq_ref.at[:, :, pl.ds(pl.multiple_of(other * sq_w, 128), sq_w)],
        dst_ref=comb_sq.at[:, t],
        send_sem=pair_sem.at[0],
        recv_sem=pair_sem.at[1],
        device_id=(d, other),
        device_id_type=MESH,
    )
    swap_sw = pltpu.make_async_remote_copy(
        src_ref=sw_ref.at[:, :, pl.ds(pl.multiple_of(other * sw_w, 128), sw_w)],
        dst_ref=comb_sw.at[:, t],
        send_sem=pair_sem.at[2],
        recv_sem=pair_sem.at[3],
        device_id=(d, other),
        device_id_type=MESH,
    )
    keep_sq = pltpu.make_async_copy(
        sq_ref.at[:, :, pl.ds(pl.multiple_of(t * sq_w, 128), sq_w)], comb_sq.at[:, t], pair_sem.at[4]
    )
    keep_sw = pltpu.make_async_copy(
        sw_ref.at[:, :, pl.ds(pl.multiple_of(t * sw_w, 128), sw_w)], comb_sw.at[:, t], pair_sem.at[5]
    )
    swap_sq.start()
    swap_sw.start()
    keep_sq.start()
    keep_sw.start()
    keep_sq.wait()
    keep_sw.wait()
    pltpu.make_async_copy(comb_sq.at[:, other], comb_sq.at[:, other], pair_sem.at[1]).wait()
    pltpu.make_async_copy(comb_sw.at[:, other], comb_sw.at[:, other], pair_sem.at[3]).wait()
    swap_sq.wait_send()
    swap_sw.wait_send()

    def sq_copy(g):
        return pltpu.make_async_remote_copy(
            src_ref=comb_sq.at[g],
            dst_ref=out_ref.at[d, :, :, pl.ds(0, sq_w)],
            send_sem=send_sem.at[g],
            recv_sem=recv_sem.at[0],
            device_id=(g, t),
            device_id_type=MESH,
        )

    def sw_copy(g):
        return pltpu.make_async_remote_copy(
            src_ref=comb_sw.at[g - n_sq],
            dst_ref=out_ref.at[d, :, :, pl.ds(0, sw_w)],
            send_sem=send_sem.at[g],
            recv_sem=recv_sem.at[0],
            device_id=(g, t),
            device_id_type=MESH,
        )

    def start(k, carry):
        g = lax.rem(k + d, n_slots)
        local = g == d

        @pl.when(local & (g < n_sq))
        def _():
            pltpu.make_async_copy(
                comb_sq.at[g], out_ref.at[d, :, :, pl.ds(0, sq_w)], recv_sem.at[0]
            ).start()

        @pl.when(local & (g >= n_sq))
        def _():
            pltpu.make_async_copy(
                comb_sw.at[g - n_sq], out_ref.at[d, :, :, pl.ds(0, sw_w)], recv_sem.at[0]
            ).start()

        @pl.when(jnp.logical_not(local) & (g < n_sq))
        def _():
            sq_copy(g).start()

        @pl.when(jnp.logical_not(local) & (g >= n_sq))
        def _():
            sw_copy(g).start()

        return carry

    lax.fori_loop(0, n_slots, start, 0)

    @pl.when(d < n_sq)
    def _():
        region = out_ref.at[:, :, :, pl.ds(0, sq_w)]
        pltpu.make_async_copy(region, region, recv_sem.at[0]).wait()

    @pl.when((d >= n_sq) & (d < n_slots))
    def _():
        region = out_ref.at[:, :, :, pl.ds(0, sw_w)]
        pltpu.make_async_copy(region, region, recv_sem.at[0]).wait()

    def wait(g, carry):
        @pl.when((g != d) & (g < n_sq))
        def _():
            sq_copy(g).wait_send()

        @pl.when((g != d) & (g >= n_sq))
        def _():
            sw_copy(g).wait_send()

        return carry

    lax.fori_loop(0, n_slots, wait, 0)


def gather_kernel(n_sq, n_sw, it_ref, osq_ref, osw_ref, send_sem, recv_sem):
    d = lax.axis_index("dp")
    t = lax.axis_index("tensor")
    n_dp = lax.axis_size("dp")
    device_barrier(n_dp, d, False)
    is_sq = d < n_sq
    is_sw = (d >= n_sq) & (d < n_sq + n_sw)
    sq_w = osq_ref.shape[2]
    sw_w = osw_ref.shape[2]
    j_sq = jnp.minimum(d, n_sq - 1)
    j_sw = jnp.clip(d - n_sq, 0, n_sw - 1)

    def sq_copy(r):
        return pltpu.make_async_remote_copy(
            src_ref=it_ref.at[r, :, pl.ds(0, sq_w)],
            dst_ref=osq_ref.at[j_sq],
            send_sem=send_sem.at[r],
            recv_sem=recv_sem.at[0],
            device_id=(r, t),
            device_id_type=MESH,
        )

    def sw_copy(r):
        return pltpu.make_async_remote_copy(
            src_ref=it_ref.at[r, :, pl.ds(0, sw_w)],
            dst_ref=osw_ref.at[j_sw],
            send_sem=send_sem.at[r],
            recv_sem=recv_sem.at[1],
            device_id=(r, t),
            device_id_type=MESH,
        )

    @pl.when(is_sq)
    def _():
        def start(k, carry):
            r = lax.rem(d + k, n_dp)

            @pl.when(r == d)
            def _():
                pltpu.make_async_copy(
                    it_ref.at[d, :, pl.ds(0, sq_w)], osq_ref.at[j_sq], recv_sem.at[0]
                ).start()

            @pl.when(r != d)
            def _():
                sq_copy(r).start()

            return carry

        lax.fori_loop(0, n_dp, start, 0)

    @pl.when(is_sw)
    def _():
        def start(k, carry):
            r = lax.rem(d + k, n_dp)

            @pl.when(r == d)
            def _():
                pltpu.make_async_copy(
                    it_ref.at[d, :, pl.ds(0, sw_w)], osw_ref.at[j_sw], recv_sem.at[1]
                ).start()

            @pl.when(r != d)
            def _():
                sw_copy(r).start()

            return carry

        lax.fori_loop(0, n_dp, start, 0)

    pltpu.make_async_copy(osq_ref, osq_ref, recv_sem.at[0]).wait()
    pltpu.make_async_copy(osw_ref, osw_ref, recv_sem.at[1]).wait()

    @pl.when(is_sq)
    def _():
        def wait(r, carry):
            @pl.when(r != d)
            def _():
                sq_copy(r).wait_send()

            return carry

        lax.fori_loop(0, n_dp, wait, 0)

    @pl.when(is_sw)
    def _():
        def wait(r, carry):
            @pl.when(r != d)
            def _():
                sw_copy(r).wait_send()

            return carry

        lax.fori_loop(0, n_dp, wait, 0)


def swap_halves(x):
    return lax.ppermute(x, "tensor", perm=[(0, 1), (1, 0)])


def orthogonalize(arrived, factor):
    t = lax.axis_index("tensor")
    rows = arrived.shape[0] // 2
    mine = pl.multiple_of(t * rows, rows)
    theirs = pl.multiple_of((1 - t) * rows, rows)
    iterate = arrived
    first_scale = jnp.float32(1.0)
    for round_index in range(NS_STEPS):
        current = iterate
        their_rows = lax.dynamic_slice_in_dim(current, theirs, rows, 0)
        my_rows = lax.dynamic_slice_in_dim(current, mine, rows, 0)
        sent = swap_halves(
            jnp.einsum("rc,sc->rs", their_rows, current, preferred_element_type=jnp.float32)
        )
        kept = lax.optimization_barrier(
            jnp.einsum("rc,sc->rs", my_rows, current, preferred_element_type=jnp.float32)
        )
        gram_part = kept + sent
        if round_index == 0:
            squares_total = lax.psum(jnp.sum(gram_part * gram_part), "tensor")
            gram_scale = jnp.sqrt(squares_total) + 1e-06
            first_scale = gram_scale
        else:
            gram_scale = jnp.float32(1.0)
        normed_part = (gram_part / gram_scale).astype(jnp.bfloat16)
        normed_other = swap_halves(normed_part)
        squared = lax.optimization_barrier(
            jnp.dot(
                lax.dynamic_slice_in_dim(normed_part, mine, rows, 1),
                normed_part,
                preferred_element_type=jnp.float32,
            )
        ) + jnp.dot(
            lax.dynamic_slice_in_dim(normed_part, theirs, rows, 1),
            normed_other,
            preferred_element_type=jnp.float32,
        )
        polynomial = (
            QUINTIC_CUBIC * normed_part.astype(jnp.float32) + QUINTIC_FIFTH * squared
        ).astype(jnp.bfloat16)
        poly_other = swap_halves(polynomial)
        product_mine = lax.optimization_barrier(
            jnp.dot(polynomial, current, preferred_element_type=jnp.float32)
        )
        product_other = jnp.dot(poly_other, current, preferred_element_type=jnp.float32)
        scale_root = jnp.sqrt(gram_scale)
        halves = []
        for rows_here, product_here in ((my_rows, product_mine), (their_rows, product_other)):
            mixed = (QUINTIC_LINEAR * rows_here.astype(jnp.float32) + product_here) / scale_root
            if round_index == NS_STEPS - 1:
                mixed = factor * mixed
            halves.append(mixed.astype(jnp.bfloat16))
        iterate = lax.dynamic_update_slice_in_dim(
            lax.dynamic_update_slice_in_dim(jnp.zeros_like(current), halves[0], mine, 0),
            halves[1],
            theirs,
            0,
        )
    return (iterate, first_scale)


def with_scale_columns(blocks, scale):
    high = scale.astype(jnp.bfloat16)
    low = (scale - high.astype(jnp.float32)).astype(jnp.bfloat16)
    shape = (blocks.shape[0], blocks.shape[1], 128)
    rows = lax.broadcasted_iota(jnp.int32, shape, 1)
    lanes = lax.broadcasted_iota(jnp.int32, shape, 2)
    extra = jnp.where(
        rows == 0,
        jnp.where(lanes == 0, high, jnp.where(lanes == 1, low, jnp.zeros((), jnp.bfloat16))),
        jnp.zeros((), jnp.bfloat16),
    )
    return jnp.concatenate([blocks, extra], axis=2)


def with_scale_row(blocks, scale):
    high = scale.astype(jnp.bfloat16)
    low = (scale - high.astype(jnp.float32)).astype(jnp.bfloat16)
    lanes = lax.broadcasted_iota(jnp.int32, (blocks.shape[0], 1, blocks.shape[2]), 2)
    row = jnp.where(lanes == 0, high, jnp.where(lanes == 1, low, jnp.zeros((), jnp.bfloat16)))
    return jnp.concatenate([blocks, row], axis=1)


def scale_of_row(returned):
    row = returned[:, -1, :2].astype(jnp.float32)
    return row[:, 0] + row[:, 1]


def local(
    square_grad,
    square_state,
    swiglu_grad,
    swiglu_state,
    square_order,
    swiglu_order,
    owners,
    vector_values,
    vector_grad,
    vector_first,
    vector_second,
    embed_values,
    embed_grad,
    embed_first,
    embed_second,
    embed_ranges,
):
    wide_count = lax.axis_size("dp")
    n_dev = wide_count * 2
    d = lax.axis_index("dp")
    t = lax.axis_index("tensor")
    n_sq = square_grad.shape[0]
    n_sw = swiglu_grad.shape[0]
    flat_rows = D // n_dev
    out_rows = D // wide_count
    square_next, square_send = momentum_terms(square_grad, square_state)
    swiglu_next, swiglu_send = momentum_terms(swiglu_grad, swiglu_state)
    sq_pieces = square_send.reshape(n_sq, flat_rows, D)
    sw_pieces = swiglu_send.reshape(n_sw, flat_rows, FF)

    half = FF // 2
    sq_halves = jnp.pad(
        sq_pieces.reshape(n_sq, flat_rows, 2, D // 2).transpose(0, 2, 1, 3),
        ((0, 0), (0, 0), (0, 0), (0, half - D // 2)),
    )
    sw_halves = sw_pieces.reshape(n_sw, flat_rows, 2, half).transpose(0, 2, 1, 3)
    idle = jnp.zeros((wide_count - n_sq - n_sw,) + sw_halves.shape[1:], jnp.bfloat16)
    outgoing = jnp.concatenate([sq_halves, sw_halves, idle], axis=0)
    arrived = lax.all_to_all(
        outgoing.reshape(D, half), ("dp", "tensor"), split_axis=0, concat_axis=0, tiled=True
    )

    is_sq = d < n_sq
    is_sw = (d >= n_sq) & (d < n_sq + n_sw)
    factor = jnp.where(is_sq, jnp.float32(math.sqrt(D)), jnp.float32(math.sqrt(FF)))
    iterate, first_scale = orthogonalize(arrived, factor)

    returned = lax.all_to_all(
        with_scale_columns(iterate.reshape(wide_count, out_rows, half), first_scale),
        "dp",
        split_axis=0,
        concat_axis=0,
        tiled=True,
    )
    returned_sq = returned[:n_sq, :, : D // 2]
    returned_sw = returned[n_sq : n_sq + n_sw, :, :half]

    inv_sq = inverse_of(square_order)
    inv_sw = inverse_of(swiglu_order)
    square_update = returned_sq[inv_sq][:, :out_rows]
    swiglu_update = returned_sw[inv_sw][:, :out_rows]

    scale_pair = returned[: n_sq + n_sw, 0, half : half + 2].astype(jnp.float32)
    slot_scales = scale_pair[:, 0] + scale_pair[:, 1]
    slot_norms = 0.5 * jnp.log(slot_scales)
    matrix_slot = jnp.concatenate([inv_sq, n_sq + inv_sw])
    matrix_norms = slot_norms[matrix_slot]
    owner_norms = jnp.sum(jnp.where(owners == d, matrix_norms, 0.0)).reshape(1)

    vector_step, first_vector, second_vector = adamw_terms(
        vector_values, vector_grad, vector_first, vector_second
    )
    embed_rows = embed_values.shape[0]
    row_numbers = d * embed_rows + jnp.arange(embed_rows, dtype=jnp.int32)
    inside = (row_numbers[:, None] >= embed_ranges[None, :, 0]) & (
        row_numbers[:, None] < embed_ranges[None, :, 1]
    )
    row_live = jnp.sum(inside.astype(jnp.int32), axis=1) > 0
    direction, first_next, second_next = adamw_terms(
        embed_values, embed_grad, embed_first, embed_second
    )
    embed_step = jnp.where(row_live[:, None], direction, 0.0)
    first_embed = jnp.where(row_live[:, None], first_next, embed_first)
    second_embed = jnp.where(row_live[:, None], second_next, embed_second)
    return (
        square_next,
        swiglu_next,
        square_update,
        swiglu_update,
        owner_norms,
        vector_step,
        first_vector,
        second_vector,
        embed_step,
        first_embed,
        second_embed,
    )


def solution(mesh):
    placed = (
        P(None, ("dp", "tensor")),
        P(None, ("dp", "tensor")),
        P(None, ("dp", "tensor")),
        P(None, ("dp", "tensor")),
        P(),
        P(),
        P(),
        P(("dp", "tensor")),
        P(("dp", "tensor")),
        P(("dp", "tensor")),
        P(("dp", "tensor")),
        P("dp", "tensor"),
        P("dp", "tensor"),
        P("dp", "tensor"),
        P("dp", "tensor"),
        P(),
    )
    return jax.shard_map(
        local,
        mesh=mesh,
        in_specs=placed,
        out_specs=(
            P(None, ("dp", "tensor")),
            P(None, ("dp", "tensor")),
            P(None, "dp", "tensor"),
            P(None, "dp", "tensor"),
            P("dp"),
            P(("dp", "tensor")),
            P(("dp", "tensor")),
            P(("dp", "tensor")),
            P("dp", "tensor"),
            P("dp", "tensor"),
            P("dp", "tensor"),
        ),
        check_vma=False,
    )
```
